256 devices in a mesh: facet: 8 (over y, core), sub: 32 (over x, z).
Axes of the slice: x: 4, y: 4, z: 8, core: 2. Of those that a mesh axis runs over, the one named last changes fastest.
Arguments:
- facet_strips: bfloat16 [2, 32768, 4096], P(None, 'facet', 'sub'), may hold values from -6 to 6
- row_window: float32 [4096], replicated, may hold values from 0.25 to 1.75
- col_window: float32 [4096], P('sub'), may hold values from 0.25 to 1.75
- row_offsets: int32 [8], replicated, may hold values from 0 to 3584
- col_offsets: int32 [8], replicated, may hold values from 0 to 3584
- tile_owner: int32 [32, 8, 32, 1], P('sub', 'facet'), may hold values from 0 to 31; in each aligned block of 32 rows (0 to 31, 32 to 63, ..., all dimensions but the last counted through in order) at most 4 rows name the same one
- measured: float32 [8, 32, 128, 2, 128], P('facet', 'sub'), may hold values from -12 to 12
- vis_weight: float32 [8, 32, 128, 128], P('facet', 'sub'), may hold values from 0.1 to 1
- uvw_pixels: int32 [8, 32, 128, 3, 128], P('facet', 'sub'), may hold values from 0 to 15
- vis_count: int32 [8, 32, 128], P('facet', 'sub'), may hold values from 1 to 128
Outputs:
- facet_update: bfloat16 [2, 32768, 4096], P(None, 'facet', 'sub')
The draws below stay inside these ranges and needn't reach their ends.
Inputs may be any that keep to these rules, and one draw needn't show every extreme that they name: Among the tiles of one row block of the subgrids of one facet index (the entries of tile_owner at one s and the 1 subgrids of one index of facet), no owner is named more than 4 times, and one owner is named exactly 4 times by some row block.
All inputs are finite; a program needn't handle non-finite values.
Results may differ from the reference program's by a relative error of at most 0.024.
Values may be sent and summed in bfloat16 or wider, within the bound.
A program may use at most 128 MiB of HBM per device.

```python
import math
from functools import partial
import jax
import jax.numpy as jnp
import numpy as np
from jax import lax

FL = 4096
FW = 4096
SG = 512
RADIX = 64
TS = 16
SGF = 1
VPT = 128
FBLK = 8
OWNERS = 32
RBLK = 32
NSG = 8
TR = 1
TC = 32
TPS = 32
TILES_DEV = 32
CAP = 4
SLOTS = 128


def draw_vis_count(key, part):
    keys = jax.random.split(jax.random.fold_in(key, 17), 2)
    total_slots = FBLK * OWNERS * SLOTS
    counts = jax.random.randint(keys[0], (total_slots,), 1, VPT + 1)
    chosen = jax.random.randint(keys[1], (), 0, total_slots)
    positions = jnp.arange(total_slots, dtype=jnp.int32)
    counts = jnp.where(positions == chosen, VPT, counts)
    counts = jnp.where(positions == (chosen + 1) % total_slots, 1, counts)
    return counts.reshape(FBLK, OWNERS, SLOTS).astype(jnp.int32)


def place_ends(entries, stream_key, least, largest):
    index_at = [jax.random.randint(jax.random.fold_in(stream_key, axis), (), 0, length) for axis, length in enumerate(entries.shape)]
    widest = entries.shape.index(max(entries.shape))
    beside = index_at[:widest] + [(index_at[widest] + 1) % entries.shape[widest]] + index_at[widest + 1:]
    return entries.at[tuple(index_at)].set(least).at[tuple(beside)].set(largest)


def block_levels(key, shape, cuts, least, largest):
    def one(dim, parts):
        draws = jax.random.uniform(jax.random.fold_in(jax.random.fold_in(key, 6), dim), (parts,), jnp.float32, least / len(cuts), largest / len(cuts))
        return jnp.repeat(jnp.exp(draws), shape[dim] // parts).reshape((-1,) + (1,) * (len(shape) - dim - 1))

    loudness = one(*cuts[0])
    for cut in cuts[1:]:
        loudness = loudness * one(*cut)
    return loudness


def routed_block(stream_key, own, number, rows, count, top, limit, slope):
    order = jax.random.permutation(stream_key, count)
    crowded, ordinary = load_shares(count, rows * top, limit, slope, True), load_shares(count, rows * top, limit, slope, False)
    places = jnp.arange(count)

    def named(lengths, turn):
        used = int((lengths > 0).sum())
        fixed = max(1, used // 4)
        passed = fixed + (places - fixed + turn * (used - fixed)) % max(1, count - fixed)
        return jnp.zeros((count,), jnp.int32).at[order[jnp.where(places < fixed, places, passed)]].set(jnp.asarray(lengths, jnp.int32))

    lengths = jnp.where(number % 4 == 0, named(crowded, number // 4), named(ordinary, number - number // 4 - 1))
    mixed = jax.random.permutation(jax.random.fold_in(own, 3), count)
    giver, taker = mixed[0:count // 2 * 2:2], mixed[1:count // 2 * 2:2]
    margin = jnp.minimum(lengths[giver] - 1, limit - lengths[taker]) // 2
    margin = jnp.where((giver == order[0]) | (taker == order[0]) | (lengths[taker] == 0), 0, jnp.maximum(margin, 0))
    passed = jax.random.randint(jax.random.fold_in(own, 4), (count // 2,), 0, 1 << 20) % (margin + 1)
    lengths = lengths.at[giver].add(-passed).at[taker].add(passed)
    items = jnp.searchsorted(jnp.cumsum(lengths), jnp.arange(rows * top), side="right").astype(jnp.int32)
    listing = items.reshape(top, rows).T
    listing = listing[jax.random.permutation(jax.random.fold_in(own, 1), rows)]
    turn = jax.random.randint(jax.random.fold_in(own, 2), (rows, 1), 0, top)
    return jnp.take_along_axis(listing, (jnp.arange(top)[None, :] + turn) % top, axis=1)


def load_shares(amount, total, reach, slope, full):
    portions = [(1 << 20) // math.isqrt(rank ** slope) + 1 for rank in range(1, amount + 1)]
    largest = reach if full else min(reach, max(-(-total // amount), total * portions[0] // sum(portions)))
    least = 1 if total - largest >= amount - 1 else 0
    given, surplus = [largest] + [least] * (amount - 1), total - largest - least * (amount - 1)
    while surplus > 0:
        free = [i for i in range(1, amount) if given[i] < largest] or [i for i in range(1, amount) if given[i] < reach]
        mass, remaining = sum([portions[i] for i in free]), surplus
        for i in free:
            more = min(reach - given[i], max(1, remaining * portions[i] // mass), surplus)
            given[i] = given[i] + more
            surplus = surplus - more
    return np.array(given)


def scatter_about(rng, shape, deviation, reach, cuts=(), held_as=jnp.bfloat16):
    loudness = block_levels(rng, shape, cuts, -0.22, 0.18) if cuts else 1.0
    values = jax.random.normal(rng, shape, jnp.float32) * deviation * loudness
    return jnp.minimum(jnp.maximum(values, -reach), reach).astype(held_as)


def setup_inputs(seed: int = 0) -> dict:
    streams_of = jax.random.split(jax.random.key(seed), 11)
    facet_strips = scatter_about(streams_of[0], (2, FBLK * FL, FW), 1.0, 6.0, ((1, 8), (2, 32)))
    row_window = jnp.clip(1.0 + 0.15 * jax.random.normal(streams_of[1], (FL,), jnp.float32), 0.25, 1.75)
    col_window = jnp.clip(1.0 + 0.15 * jax.random.normal(streams_of[2], (FW,), jnp.float32), 0.25, 1.75)
    row_offsets = place_ends(jax.random.randint(streams_of[3], (NSG,), 0, FL - SG + 1), jax.random.fold_in(streams_of[3], 1), 0, FL - SG).astype(jnp.int32)
    col_offsets = place_ends(jax.random.randint(streams_of[4], (NSG,), 0, FW - SG + 1), jax.random.fold_in(streams_of[4], 1), 0, FW - SG).astype(jnp.int32)
    tile_owner_keys = jax.random.split(jax.random.fold_in(streams_of[5], 1), RBLK * NSG * TPS // TILES_DEV)
    tile_owner_turns = jax.random.permutation(jax.random.fold_in(streams_of[5], 3), RBLK * NSG * TPS // TILES_DEV)
    tile_owner = jax.vmap(lambda own, number: routed_block(jax.random.fold_in(streams_of[5], 2), own, number, TILES_DEV, OWNERS, 1, CAP, 2))(tile_owner_keys, tile_owner_turns).reshape((RBLK, NSG, TPS, 1))
    measured = scatter_about(streams_of[6], (FBLK, OWNERS, SLOTS, 2, VPT), 2.0, 12.0, ((0, 8), (1, 32)), jnp.float32)
    vis_weight = jnp.clip(jnp.exp(math.log(1.0) - 2.3025851 * jax.random.uniform(streams_of[7], (FBLK, OWNERS, SLOTS, VPT), jnp.float32) ** block_levels(streams_of[7], (FBLK, OWNERS, SLOTS, VPT), ((0, 8), (1, 32)), -0.2, 0.2)), 0.1, 1.0)
    uvw_pixels = place_ends(jax.random.randint(streams_of[8], (FBLK, OWNERS, SLOTS, 3, VPT), 0, TS), jax.random.fold_in(streams_of[8], 1), 0, TS - 1).astype(jnp.int32)
    vis_count = draw_vis_count(jax.random.fold_in(streams_of[10], 71), 0)
    return {"facet_strips": facet_strips, "row_window": row_window, "col_window": col_window, "row_offsets": row_offsets, "col_offsets": col_offsets, "tile_owner": tile_owner, "measured": measured, "vis_weight": vis_weight, "uvw_pixels": uvw_pixels, "vis_count": vis_count}


kernel_width = 2.5
kernel_norm = 0.565

def contract(pattern, first, other):
    return jnp.einsum(pattern, first.astype(jnp.float32), other.astype(jnp.float32), precision=lax.Precision.HIGHEST)

def angle_table(row_count, col_count, length):
    lefts = jnp.arange(row_count, dtype=jnp.int32)[:, None]
    rights = jnp.arange(col_count, dtype=jnp.int32)[None, :]
    turn_count = (lefts * rights % length).astype(jnp.float32)
    angles = turn_count * (2.0 * math.pi / length)
    return (jnp.cos(angles), jnp.sin(angles))

def complex_matrix(extent, direction):
    cosine, sine_table = angle_table(extent, extent, extent)
    sine_table = direction * sine_table
    upper = jnp.stack([cosine, -sine_table], axis=1)
    lower = jnp.stack([sine_table, cosine], axis=1)
    return jnp.stack([upper, lower], axis=0).astype(jnp.bfloat16)

def apply_twist(values, cosine, sine_table, direction):
    real_part = values[:, 0]
    imag_part = values[:, 1]
    sine_table = direction * sine_table
    return jnp.stack([cosine * real_part - sine_table * imag_part, sine_table * real_part + cosine * imag_part], axis=1).astype(jnp.bfloat16)

def rows_forward(values, radix_size):
    batches = values.shape[0]
    length = values.shape[2]
    columns = values.shape[3]
    second = length // radix_size
    shaped = values.reshape(batches, 2, radix_size, second, columns)
    inner_sum = contract('akzn,bznqc->bakqc', complex_matrix(radix_size, -1.0), shaped)
    cosine, sine_table = angle_table(radix_size, second, length)
    turned = apply_twist(inner_sum, cosine[:, :, None], sine_table[:, :, None], -1.0)
    outer_sum = contract('ajzq,bzkqc->bajkc', complex_matrix(second, -1.0), turned)
    return outer_sum.reshape(batches, 2, length, columns)

def rows_backward(values, radix_size):
    batches = values.shape[0]
    length = values.shape[2]
    columns = values.shape[3]
    second = length // radix_size
    shaped = values.reshape(batches, 2, second, radix_size, columns)
    inner_sum = contract('ajzq,bzqkc->bajkc', complex_matrix(second, 1.0), shaped)
    cosine, sine_table = angle_table(second, radix_size, length)
    turned = apply_twist(inner_sum, cosine[:, :, None], sine_table[:, :, None], 1.0)
    outer_sum = contract('anzk,bzjkc->banjc', complex_matrix(radix_size, 1.0), turned)
    return outer_sum.reshape(batches, 2, length, columns)

def cols_forward(values, radix_size):
    batches = values.shape[0]
    middle = values.shape[2]
    length = values.shape[3]
    second = length // radix_size
    shaped = values.reshape(batches, 2, middle, radix_size, second)
    inner_sum = contract('akzn,bzmnq->bamkq', complex_matrix(radix_size, -1.0), shaped)
    cosine, sine_table = angle_table(radix_size, second, length)
    turned = apply_twist(inner_sum, cosine, sine_table, -1.0)
    outer_sum = contract('ajzq,bzmkq->bamjk', complex_matrix(second, -1.0), turned)
    return outer_sum.reshape(batches, 2, middle, length)

def cols_backward(values, radix_size):
    batches = values.shape[0]
    middle = values.shape[2]
    length = values.shape[3]
    second = length // radix_size
    shaped = values.reshape(batches, 2, middle, second, radix_size)
    inner_sum = contract('ajzq,bzmqk->bamjk', complex_matrix(second, 1.0), shaped)
    cosine, sine_table = angle_table(second, radix_size, length)
    turned = apply_twist(inner_sum, cosine, sine_table, 1.0)
    outer_sum = contract('anzk,bzmjk->bamnj', complex_matrix(radix_size, 1.0), turned)
    return outer_sum.reshape(batches, 2, middle, length)

def rotate(values, facet_index, offsets, facet_count, direction):
    turn_count = (facet_index * offsets % facet_count).astype(jnp.float32)
    angles = turn_count * (2.0 * math.pi / facet_count)
    extra = (1,) * (values.ndim - 2)
    cosine = jnp.cos(angles).reshape(angles.shape + extra)
    sine_table = direction * jnp.sin(angles).reshape(angles.shape + extra)
    real_part = values[:, 0]
    imag_part = values[:, 1]
    return jnp.stack([cosine * real_part - sine_table * imag_part, sine_table * real_part + cosine * imag_part], axis=1)

def kernel_rows(centre, w_plane, tile_size):
    pixels = jnp.arange(tile_size, dtype=jnp.int32)
    offset = pixels[None, :, None] - centre[:, None, :]
    falloff = kernel_norm * jnp.exp(-jnp.square(offset.astype(jnp.float32) / kernel_width))
    square = jnp.square(pixels - tile_size // 2)
    turn_count = w_plane[:, None, :] * square[None, :, None] % (tile_size * tile_size)
    angles = turn_count.astype(jnp.float32) * (2.0 * math.pi / (tile_size * tile_size))
    return jnp.stack([falloff * jnp.cos(angles), -falloff * jnp.sin(angles)], axis=2).astype(jnp.bfloat16)

def visit_slots(slot_tiles, measured, weight, uvw_pixels, counts, tile_size):
    slots = slot_tiles.shape[0]
    visits = measured.shape[2]
    stacked_grid = slot_tiles.reshape(slots, 2 * tile_size, tile_size)
    row_kernel = kernel_rows(uvw_pixels[:, 0], uvw_pixels[:, 2], tile_size)
    col_kernel = kernel_rows(uvw_pixels[:, 1], uvw_pixels[:, 2], tile_size)
    products = contract('sab,sbv->sav', stacked_grid, col_kernel.reshape(slots, tile_size, 2 * visits))
    products = products.reshape(slots, 2, tile_size, 2, visits)
    part_real = products[:, 0, :, 0] - products[:, 1, :, 1]
    part_imag = products[:, 0, :, 1] + products[:, 1, :, 0]
    row_real = row_kernel[:, :, 0].astype(jnp.float32)
    row_imag = row_kernel[:, :, 1].astype(jnp.float32)
    pred_real = lax.optimization_barrier(jnp.sum(row_real * part_real - row_imag * part_imag, axis=1))
    pred_imag = lax.optimization_barrier(jnp.sum(row_real * part_imag + row_imag * part_real, axis=1))
    live_mask = jnp.arange(visits, dtype=jnp.int32)[None, :] < counts[:, None]
    res_real = jnp.where(live_mask, weight * (measured[:, 0] - pred_real), 0.0)
    res_imag = jnp.where(live_mask, weight * (measured[:, 1] - pred_imag), 0.0)
    spread_real = row_real * res_real[:, None, :] + row_imag * res_imag[:, None, :]
    spread_imag = row_real * res_imag[:, None, :] - row_imag * res_real[:, None, :]
    spread = jnp.stack([spread_real, spread_imag], axis=1).astype(jnp.bfloat16).reshape(slots, 2 * tile_size, visits)
    regrid = contract('sav,sbv->sab', spread, col_kernel.reshape(slots, 2 * tile_size, visits))
    regrid = regrid.reshape(slots, 2, tile_size, tile_size, 2)
    tile_real = regrid[:, 0, :, :, 0] + regrid[:, 1, :, :, 1]
    tile_imag = regrid[:, 1, :, :, 0] - regrid[:, 0, :, :, 1]
    return jnp.stack([tile_real, tile_imag], axis=1).astype(jnp.bfloat16).reshape(slots, 2 * tile_size * tile_size)

def routing(owners, sub_count):
    matches = (owners[:, None] == jnp.arange(sub_count, dtype=jnp.int32)[None, :]).astype(jnp.int32)
    return lax.optimization_barrier(jnp.sum(jnp.cumsum(matches, axis=0) * matches, axis=1)) - 1

def reference(facet_strips, row_window, col_window, row_offsets, col_offsets, tile_owner, measured, vis_weight, uvw_pixels, vis_count):
    facets = jnp.transpose(facet_strips.reshape(2, FBLK, FL, FW), (1, 0, 2, 3))

    def forward_facet(subgrids, packed):
        facet_index, one_facet = packed
        prepared = (one_facet.astype(jnp.float32) * row_window[None, :, None] * col_window[None, None, :]).astype(jnp.bfloat16)
        spectrum = rows_forward(prepared[None], RADIX)[0] * (1.0 / math.sqrt(FL))

        def per_subgrid(offset_pair):
            row_start, col_start = offset_pair
            piece = lax.dynamic_slice_in_dim(spectrum, row_start, SG, 1).astype(jnp.bfloat16)
            columns = cols_forward(piece[None], RADIX)[0] * (1.0 / math.sqrt(FW))
            return lax.dynamic_slice_in_dim(columns, col_start, SG, 2)
        extracted = lax.map(per_subgrid, (row_offsets, col_offsets))
        return (subgrids + rotate(extracted, facet_index, row_offsets, FBLK, -1.0), None)
    subgrids, _ = lax.scan(forward_facet, jnp.zeros((NSG, 2, SG, SG), jnp.float32), (jnp.arange(FBLK, dtype=jnp.int32), facets))
    tile_data = subgrids.astype(jnp.bfloat16).reshape(FBLK, SGF, 2, RBLK, TR, TS, TC, TS)
    tile_data = jnp.transpose(tile_data, (0, 3, 1, 4, 6, 2, 5, 7)).reshape(FBLK, RBLK, TILES_DEV, 2 * TS * TS)
    owners = jnp.transpose(tile_owner.reshape(RBLK, FBLK, TILES_DEV), (1, 0, 2))

    def visit_group(packed):
        group_tiles, group_owners, group_measured, group_weight, group_pixels, group_counts = packed
        ranks = jax.vmap(partial(routing, sub_count=OWNERS))(group_owners)
        source = jnp.arange(RBLK, dtype=jnp.int32)[:, None] * CAP + ranks
        buffers = jnp.zeros((OWNERS, SLOTS, 2 * TS * TS), jnp.bfloat16).at[group_owners, source].set(group_tiles)
        answered = jax.vmap(partial(visit_slots, tile_size=TS))(buffers, group_measured, group_weight, group_pixels, group_counts)
        return answered[group_owners, source]
    returned = lax.map(visit_group, (tile_data, owners, measured, vis_weight, uvw_pixels, vis_count))
    returned = returned.reshape(FBLK, RBLK, SGF, TR, TC, 2, TS, TS)
    residual_subgrids = jnp.transpose(returned, (0, 2, 5, 1, 3, 6, 4, 7)).reshape(NSG, 2, SG, SG)

    def column_image(packed):
        one_block, col_start = packed
        placed = lax.dynamic_update_slice_in_dim(jnp.zeros((2, SG, FW), jnp.bfloat16), one_block, col_start, 2)
        image = cols_backward(placed[None], RADIX)[0] * (1.0 / math.sqrt(FW))
        return image.astype(jnp.bfloat16)
    images = lax.map(column_image, (residual_subgrids, col_offsets))

    def backward_facet(facet_index):

        def add_one(which, running):
            one_image = lax.optimization_barrier(images[which]).astype(jnp.float32)
            turned = rotate(one_image[None], facet_index, row_offsets[which][None], FBLK, 1.0)
            turned = lax.optimization_barrier(turned.astype(jnp.bfloat16))
            current = lax.dynamic_slice_in_dim(running, row_offsets[which], SG, 1)
            return lax.dynamic_update_slice_in_dim(running, current + turned[0].astype(jnp.float32), row_offsets[which], 1)
        running = lax.fori_loop(0, NSG, add_one, jnp.zeros((2, FL, FW), jnp.float32))
        sums_bf = running.astype(jnp.bfloat16)
        update = rows_backward(sums_bf[None], RADIX)[0] * (1.0 / math.sqrt(FL))
        return (update * row_window[None, :, None] * col_window[None, None, :]).astype(jnp.bfloat16)
    updates = lax.map(backward_facet, jnp.arange(FBLK, dtype=jnp.int32))
    return jnp.transpose(updates, (1, 0, 2, 3)).reshape(2, FBLK * FL, FW)
```

```python
import math

import jax
import jax.numpy as jnp
from jax import lax
from jax.sharding import PartitionSpec as P

SG = 512
RADIX = 64
TS = 16


kernel_width = 2.5
kernel_norm = 0.565


def contract(pattern, first, other):
    return jnp.einsum(pattern, first, other, preferred_element_type=jnp.float32)


def angle_table(row_count, col_count, length):
    lefts = jnp.arange(row_count, dtype=jnp.int32)[:, None]
    rights = jnp.arange(col_count, dtype=jnp.int32)[None, :]
    turn_count = (lefts * rights % length).astype(jnp.float32)
    angles = turn_count * (2.0 * math.pi / length)
    return (jnp.cos(angles), jnp.sin(angles))


def complex_matrix(extent, direction):
    cosine, sine_table = angle_table(extent, extent, extent)
    sine_table = direction * sine_table
    upper = jnp.stack([cosine, -sine_table], axis=1)
    lower = jnp.stack([sine_table, cosine], axis=1)
    return jnp.stack([upper, lower], axis=0).astype(jnp.bfloat16)


def apply_twist(values, cosine, sine_table, direction):
    real_part = values[:, 0]
    imag_part = values[:, 1]
    sine_table = direction * sine_table
    return jnp.stack(
        [cosine * real_part - sine_table * imag_part, sine_table * real_part + cosine * imag_part],
        axis=1,
    ).astype(jnp.bfloat16)


def rows_forward(values, radix_size):
    batches = values.shape[0]
    length = values.shape[2]
    columns = values.shape[3]
    second = length // radix_size
    shaped = values.reshape(batches, 2, radix_size, second, columns)
    inner_sum = contract("akzn,bznqc->bakqc", complex_matrix(radix_size, -1.0), shaped)
    cosine, sine_table = angle_table(radix_size, second, length)
    turned = apply_twist(inner_sum, cosine[:, :, None], sine_table[:, :, None], -1.0)
    outer_sum = contract("ajzq,bzkqc->bajkc", complex_matrix(second, -1.0), turned)
    return outer_sum.reshape(batches, 2, length, columns)


def rows_backward(values, radix_size):
    batches = values.shape[0]
    length = values.shape[2]
    columns = values.shape[3]
    second = length // radix_size
    shaped = values.reshape(batches, 2, second, radix_size, columns)
    inner_sum = contract("ajzq,bzqkc->bajkc", complex_matrix(second, 1.0), shaped)
    cosine, sine_table = angle_table(second, radix_size, length)
    turned = apply_twist(inner_sum, cosine[:, :, None], sine_table[:, :, None], 1.0)
    outer_sum = contract("anzk,bzjkc->banjc", complex_matrix(radix_size, 1.0), turned)
    return outer_sum.reshape(batches, 2, length, columns)


def cols_forward(values, radix_size):
    batches = values.shape[0]
    middle = values.shape[2]
    length = values.shape[3]
    second = length // radix_size
    shaped = values.reshape(batches, 2, middle, radix_size, second)
    inner_sum = contract("akzn,bzmnq->bamkq", complex_matrix(radix_size, -1.0), shaped)
    cosine, sine_table = angle_table(radix_size, second, length)
    turned = apply_twist(inner_sum, cosine, sine_table, -1.0)
    outer_sum = contract("ajzq,bzmkq->bamjk", complex_matrix(second, -1.0), turned)
    return outer_sum.reshape(batches, 2, middle, length)


def cols_backward(values, radix_size):
    batches = values.shape[0]
    middle = values.shape[2]
    length = values.shape[3]
    second = length // radix_size
    shaped = values.reshape(batches, 2, middle, second, radix_size)
    inner_sum = contract("ajzq,bzmqk->bamjk", complex_matrix(second, 1.0), shaped)
    cosine, sine_table = angle_table(second, radix_size, length)
    turned = apply_twist(inner_sum, cosine, sine_table, 1.0)
    outer_sum = contract("anzk,bzmjk->bamnj", complex_matrix(radix_size, 1.0), turned)
    return outer_sum.reshape(batches, 2, middle, length)


def rotate(values, facet_index, offsets, facet_count, direction):
    turn_count = (facet_index * offsets % facet_count).astype(jnp.float32)
    angles = turn_count * (2.0 * math.pi / facet_count)
    extra = (1,) * (values.ndim - 2)
    cosine = jnp.cos(angles).reshape(angles.shape + extra)
    sine_table = direction * jnp.sin(angles).reshape(angles.shape + extra)
    real_part = values[:, 0]
    imag_part = values[:, 1]
    return jnp.stack(
        [cosine * real_part - sine_table * imag_part, sine_table * real_part + cosine * imag_part],
        axis=1,
    )


def kernel_rows(centre, w_plane, tile_size):
    pixels = jnp.arange(tile_size, dtype=jnp.int32)
    offset = pixels[None, :, None] - centre[:, None, :]
    falloff = kernel_norm * jnp.exp(-jnp.square(offset.astype(jnp.float32) / kernel_width))
    square = jnp.square(pixels - tile_size // 2)
    turn_count = w_plane[:, None, :] * square[None, :, None] % (tile_size * tile_size)
    angles = turn_count.astype(jnp.float32) * (2.0 * math.pi / (tile_size * tile_size))
    return jnp.stack([falloff * jnp.cos(angles), -falloff * jnp.sin(angles)], axis=2).astype(
        jnp.bfloat16
    )


def visit_slots(slot_tiles, measured, weight, uvw_pixels, counts, tile_size):
    slots = slot_tiles.shape[0]
    visits = measured.shape[2]
    stacked_grid = slot_tiles.reshape(slots, 2 * tile_size, tile_size)
    row_kernel = kernel_rows(uvw_pixels[:, 0], uvw_pixels[:, 2], tile_size)
    col_kernel = kernel_rows(uvw_pixels[:, 1], uvw_pixels[:, 2], tile_size)
    products = contract(
        "sab,sbv->sav", stacked_grid, col_kernel.reshape(slots, tile_size, 2 * visits)
    )
    products = products.reshape(slots, 2, tile_size, 2, visits)
    part_real = products[:, 0, :, 0] - products[:, 1, :, 1]
    part_imag = products[:, 0, :, 1] + products[:, 1, :, 0]
    row_real = row_kernel[:, :, 0].astype(jnp.float32)
    row_imag = row_kernel[:, :, 1].astype(jnp.float32)
    pred_real = jnp.sum(row_real * part_real - row_imag * part_imag, axis=1)
    pred_imag = jnp.sum(row_real * part_imag + row_imag * part_real, axis=1)
    live_mask = jnp.arange(visits, dtype=jnp.int32)[None, :] < counts[:, None]
    res_real = jnp.where(live_mask, weight * (measured[:, 0] - pred_real), 0.0)
    res_imag = jnp.where(live_mask, weight * (measured[:, 1] - pred_imag), 0.0)
    spread_real = row_real * res_real[:, None, :] + row_imag * res_imag[:, None, :]
    spread_imag = row_real * res_imag[:, None, :] - row_imag * res_real[:, None, :]
    spread = (
        jnp.stack([spread_real, spread_imag], axis=1)
        .astype(jnp.bfloat16)
        .reshape(slots, 2 * tile_size, visits)
    )
    regrid = contract("sav,sbv->sab", spread, col_kernel.reshape(slots, 2 * tile_size, visits))
    regrid = regrid.reshape(slots, 2, tile_size, tile_size, 2)
    tile_real = regrid[:, 0, :, :, 0] + regrid[:, 1, :, :, 1]
    tile_imag = regrid[:, 1, :, :, 0] - regrid[:, 0, :, :, 1]
    return (
        jnp.stack([tile_real, tile_imag], axis=1)
        .astype(jnp.bfloat16)
        .reshape(slots, 2 * tile_size * tile_size)
    )


def routing(owners, sub_count):
    matches = (owners[:, None] == jnp.arange(sub_count, dtype=jnp.int32)[None, :]).astype(jnp.int32)
    return jnp.sum(jnp.cumsum(matches, axis=0) * matches, axis=1) - 1


def per_device(
    facet_strips,
    row_window,
    col_window,
    row_offsets,
    col_offsets,
    tile_owner,
    measured,
    vis_weight,
    uvw_pixels,
    vis_count,
):
    sub_count = lax.axis_size("sub")
    facet_count = lax.axis_size("facet")
    my_facet = lax.axis_index("facet")
    length = facet_strips.shape[1]
    strip_width = facet_strips.shape[2]
    total_subgrids = row_offsets.shape[0]
    my_subgrids = total_subgrids // facet_count
    full_width = strip_width * sub_count
    row_block = SG // sub_count
    prepared = (
        facet_strips.astype(jnp.float32) * row_window[None, :, None] * col_window[None, None, :]
    ).astype(jnp.bfloat16)
    spectrum = (rows_forward(prepared[None], RADIX)[0] * (1.0 / math.sqrt(length))).astype(
        jnp.bfloat16
    )

    contributions = jnp.stack(
        [lax.dynamic_slice_in_dim(spectrum, row_offsets[j], SG, 1) for j in range(total_subgrids)]
    )
    phased = rotate(
        contributions.astype(jnp.float32), my_facet, row_offsets, facet_count, -1.0
    ).astype(jnp.bfloat16)
    mine = lax.psum_scatter(phased, "facet", scatter_dimension=0, tiled=True)
    row_blocks = lax.all_to_all(mine, "sub", split_axis=2, concat_axis=3, tiled=True)
    spectra = cols_forward(row_blocks, RADIX) * (1.0 / math.sqrt(full_width))
    my_start = lax.dynamic_index_in_dim(col_offsets, my_facet, keepdims=False)
    summed = lax.dynamic_slice_in_dim(spectra, my_start, SG, 3).astype(jnp.bfloat16)
    tile_rows = row_block // TS
    tile_cols = SG // TS
    tile_data = summed.reshape(my_subgrids, 2, tile_rows, TS, tile_cols, TS)
    tile_data = jnp.transpose(tile_data, (0, 2, 4, 1, 3, 5)).reshape(
        my_subgrids * tile_rows * tile_cols, 2 * TS * TS
    )
    owners = tile_owner.reshape(-1)
    capacity = measured.shape[2] // sub_count
    slot_index = owners * capacity + routing(owners, sub_count)
    chooser = (
        slot_index[None, :] == jnp.arange(sub_count * capacity, dtype=jnp.int32)[:, None]
    ).astype(jnp.bfloat16)
    outgoing = jnp.dot(chooser, tile_data, preferred_element_type=jnp.float32).astype(jnp.bfloat16)
    values_here = measured[0, 0]
    weights_here = vis_weight[0, 0]
    pixels_here = uvw_pixels[0, 0]
    counts_here = vis_count[0, 0]
    arrived = lax.all_to_all(outgoing, "sub", split_axis=0, concat_axis=0, tiled=True)
    answered = visit_slots(arrived, values_here, weights_here, pixels_here, counts_here, TS)
    returned = lax.all_to_all(answered, "sub", split_axis=0, concat_axis=0, tiled=True)
    my_tiles = jnp.einsum(
        "st,sf->tf", chooser, returned, preferred_element_type=jnp.float32
    ).astype(jnp.bfloat16)
    my_tiles = my_tiles.reshape(my_subgrids, tile_rows, tile_cols, 2, TS, TS)
    residual_block = jnp.transpose(my_tiles, (0, 3, 1, 4, 2, 5)).reshape(
        my_subgrids, 2, row_block, SG
    )
    placed = lax.dynamic_update_slice_in_dim(
        jnp.zeros(residual_block.shape[:-1] + (full_width,), jnp.bfloat16),
        residual_block,
        my_start,
        3,
    )
    images = (cols_backward(placed, RADIX) * (1.0 / math.sqrt(full_width))).astype(jnp.bfloat16)
    strip = lax.all_to_all(images, "sub", split_axis=3, concat_axis=2, tiled=True)
    strips = lax.all_gather(strip, "facet", axis=0, tiled=True)
    turned_all = rotate(
        strips.astype(jnp.float32), my_facet, row_offsets, facet_count, 1.0
    ).astype(jnp.bfloat16).astype(jnp.float32)
    running = jnp.zeros((2, length, strip_width), jnp.float32)
    for j in range(total_subgrids):
        current = lax.dynamic_slice_in_dim(running, row_offsets[j], SG, 1)
        running = lax.dynamic_update_slice_in_dim(
            running, current + turned_all[j], row_offsets[j], 1
        )
    sums_bf = running.astype(jnp.bfloat16)
    update = rows_backward(sums_bf[None], RADIX)[0] * (1.0 / math.sqrt(length))
    return (update * row_window[None, :, None] * col_window[None, None, :]).astype(jnp.bfloat16)


def solution(mesh):
    in_specs = (
        P(None, "facet", "sub"),
        P(),
        P("sub"),
        P(),
        P(),
        P("sub", "facet", None, None),
        P("facet", "sub", None, None, None),
        P("facet", "sub", None, None),
        P("facet", "sub", None, None, None),
        P("facet", "sub", None),
    )
    out_specs = P(None, "facet", "sub")
    return jax.shard_map(
        per_device, mesh=mesh, in_specs=in_specs, out_specs=out_specs, check_vma=False
    )
```

```python
import math

import jax
import jax.numpy as jnp
import numpy as np
from jax import lax
from jax.experimental import pallas as pl
from jax.experimental.pallas import tpu as pltpu
from jax.sharding import PartitionSpec as P

SG = 512
RADIX = 64
TS = 16
LONG = 4096
SUBS = 32
FACETS = 8
CAP = 4
LANES = 128
MESH = pl.DeviceIdType.MESH
F32 = jnp.float32
BF16 = jnp.bfloat16

kernel_width = 2.5
kernel_norm = 0.565


def as_real(theta):
    cosine, sine = np.cos(theta), np.sin(theta)
    return np.block([[cosine, sine], [-sine, cosine]])


def row_tables():
    idx = np.arange(RADIX)
    first = as_real(2 * np.pi * (np.outer(idx, idx) % RADIX) / RADIX)
    second = [
        as_real(2 * np.pi * (np.outer(k1 + RADIX * idx, idx) % LONG) / LONG) / RADIX
        for k1 in range(RADIX)
    ]
    return jnp.asarray(first, BF16), jnp.asarray(np.stack(second), BF16)


def col_tables():
    high = np.outer(np.arange(16), np.arange(LANES)) % LANES
    dense = as_real(2 * np.pi * high / LANES)
    low = 2 * np.pi * np.outer(np.arange(SUBS), np.arange(LANES)) / LONG
    twist = np.stack([np.cos(low), np.sin(low)]) / 64.0
    rep = np.zeros((512, 32))
    rep[np.arange(512), np.arange(512) // 16] = 1
    sel = np.zeros((2, 16, 16, 4, 2, 16))
    for z in range(2):
        for r in range(16):
            sel[z, :, r, :, z, r] = 1
    sel = sel.reshape(512, 128)
    keep = (np.arange(512)[:, None] % 16) == (np.arange(512)[None, :] // 16 % 16)
    return (
        jnp.asarray(dense, BF16),
        jnp.asarray(twist, F32),
        jnp.asarray(rep, BF16),
        jnp.asarray(rep.T, BF16),
        jnp.asarray(sel, BF16),
        jnp.asarray(keep, BF16),
    )


def mm(first, other):
    return jnp.dot(first, other, preferred_element_type=F32)


def mm_nt(first, other):
    return lax.dot_general(first, other, (((1,), (1,)), ((), ())), preferred_element_type=F32)


def mm_tn(first, other):
    return lax.dot_general(first, other, (((0,), (0,)), ((), ())), preferred_element_type=F32)


def transform_rows(re, im, mid_re, mid_im, first, second):
    def stage_a(step, carry):
        parts = []
        for u in range(2):
            rows = pl.ds(2 * step + u, RADIX, stride=RADIX)
            parts.append(jnp.concatenate([re[rows, :], im[rows, :]], axis=0).astype(BF16))
        res = mm(first[...], jnp.concatenate(parts, axis=1))
        for u in range(2):
            rows = pl.ds(2 * step + u, RADIX, stride=RADIX)
            mid_re[rows, :] = res[:RADIX, u * LANES : (u + 1) * LANES]
            mid_im[rows, :] = res[RADIX:, u * LANES : (u + 1) * LANES]
        return carry

    lax.fori_loop(0, RADIX // 2, stage_a, 0, unroll=2)

    def stage_b(step, carry):
        rows = pl.ds(pl.multiple_of(step * RADIX, RADIX), RADIX)
        block = jnp.concatenate([mid_re[rows, :], mid_im[rows, :]], axis=0).astype(BF16)
        res = mm(second[step], block)
        out_rows = pl.ds(step, RADIX, stride=RADIX)
        re[out_rows, :] = res[:RADIX]
        im[out_rows, :] = res[RADIX:]
        return carry

    lax.fori_loop(0, RADIX, stage_b, 0, unroll=4)


def forward_kernel(offs, turn, strip, win, first, second, out, re, im, mid_re, mid_im):
    def load(step, carry):
        rows = pl.ds(pl.multiple_of(step * 128, 128), 128)
        re[rows, :] = strip[0, rows, :].astype(F32) * win[rows, :]
        im[rows, :] = strip[1, rows, :].astype(F32) * win[rows, :]
        return carry

    lax.fori_loop(0, LONG // 128, load, 0, unroll=2)
    transform_rows(re, im, mid_re, mid_im, first, second)

    def emit(step, carry):
        which, part = step // 4, step % 4
        rows = pl.ds(offs[which] + part * 128, 128)
        real, imag = re[rows, :], im[rows, :]
        cosine, sine = turn[0, which], turn[1, which]
        blocks = pl.ds(part * 8, 8)
        out[which, blocks, 0] = (cosine * real + sine * imag).astype(BF16).reshape(8, 16, LANES)
        out[which, blocks, 1] = (cosine * imag - sine * real).astype(BF16).reshape(8, 16, LANES)
        return carry

    lax.fori_loop(0, 4 * FACETS, emit, 0, unroll=2)


def backward_kernel(offs, turn, strips, win, first, second, out, re, im, mid_re, mid_im):
    def clear(step, carry):
        rows = pl.ds(pl.multiple_of(step * 128, 128), 128)
        re[rows, :] = jnp.zeros((128, LANES), F32)
        im[rows, :] = jnp.zeros((128, LANES), F32)
        return carry

    lax.fori_loop(0, LONG // 128, clear, 0, unroll=2)

    def place(step, carry):
        which, part = step // 4, step % 4
        rows = pl.ds(offs[which] + part * 128, 128)
        blocks = pl.ds(part * 8, 8)
        real = strips[which, blocks, 0].reshape(128, LANES).astype(F32)
        imag = strips[which, blocks, 1].reshape(128, LANES).astype(F32)
        cosine, sine = turn[0, which], turn[1, which]
        re[rows, :] = re[rows, :] + (cosine * real - sine * imag)
        im[rows, :] = im[rows, :] - (sine * real + cosine * imag)
        return carry

    lax.fori_loop(0, 4 * FACETS, place, 0)
    transform_rows(re, im, mid_re, mid_im, first, second)

    def emit(step, carry):
        rows = pl.ds(pl.multiple_of(step * 128, 128), 128)
        out[0, rows, :] = (re[rows, :] * win[rows, :]).astype(BF16)
        out[1, rows, :] = (-im[rows, :] * win[rows, :]).astype(BF16)
        return carry

    lax.fori_loop(0, LONG // 128, emit, 0, unroll=2)


def times(pair, cosine, sine):
    return (pair[0] * cosine - pair[1] * sine, pair[0] * sine + pair[1] * cosine)


def times_unit(pair, num, den, sign):
    num = num % den
    if num == 0:
        return pair
    if 4 * num == den:
        return (-sign * pair[1], sign * pair[0])
    if 2 * num == den:
        return (-pair[0], -pair[1])
    angle = 2 * math.pi * num / den
    return times(pair, math.cos(angle), sign * math.sin(angle))


def small_dft(items, sign):
    count = len(items)
    if count == 1:
        return items
    even = small_dft(items[0::2], sign)
    odd = small_dft(items[1::2], sign)
    odd = [times_unit(odd[i], i, count, sign) for i in range(count // 2)]
    low = [(a[0] + b[0], a[1] + b[1]) for a, b in zip(even, odd)]
    high = [(a[0] - b[0], a[1] - b[1]) for a, b in zip(even, odd)]
    return low + high


def dft_over_blocks(get, put, work, sign):
    for lo in range(8):
        items = small_dft([get(lo + 8 * hi) for hi in range(4)], sign)
        for p_lo in range(4):
            value = times_unit(items[p_lo], lo * p_lo, SUBS, sign)
            work[p_lo * 8 + lo, 0] = value[0]
            work[p_lo * 8 + lo, 1] = value[1]
    for p_lo in range(4):
        items = small_dft([(work[p_lo * 8 + lo, 0], work[p_lo * 8 + lo, 1]) for lo in range(8)], sign)
        for p_hi in range(8):
            put(p_lo + 4 * p_hi, items[p_hi])


def columns_to_tiles(blocks, phase, dense, twist, rep, sel, keep, work, folded, tiles):
    def get(s):
        pair = (blocks[s, 0].astype(F32), blocks[s, 1].astype(F32))
        return times(pair, phase[0, s : s + 1, :], -phase[1, s : s + 1, :])

    def put(p, pair):
        pair = times(pair, twist[0, p : p + 1, :], -twist[1, p : p + 1, :])
        rows = slice(p * 16, p * 16 + 16)
        folded[rows, 0:LANES] = pair[0].astype(BF16)
        folded[rows, LANES : 2 * LANES] = pair[1].astype(BF16)

    dft_over_blocks(get, put, work, -1.0)
    flat = mm_nt(dense[...], folded[...]).astype(BF16)
    stacked = jnp.concatenate(
        [
            jnp.concatenate([flat[0:16, 0:256], flat[16:32, 0:256]], axis=1),
            jnp.concatenate([flat[0:16, 256:512], flat[16:32, 256:512]], axis=1),
        ],
        axis=0,
    )
    spread = mm(rep[...], stacked).astype(BF16) * keep[...]
    tiles[...] = mm(spread, sel[...]).astype(BF16)


def tiles_to_columns(tiles, phase, dense, twist, rep_t, sel, keep, work, folded_f32, images):
    spread = mm_nt(tiles[...], sel[...]).astype(BF16) * keep[...]
    stacked = mm(rep_t[...], spread).astype(BF16)
    flat = jnp.concatenate(
        [
            jnp.concatenate([stacked[0:16, 0:256], stacked[16:32, 0:256]], axis=1),
            jnp.concatenate([stacked[0:16, 256:512], stacked[16:32, 256:512]], axis=1),
        ],
        axis=0,
    )
    folded_f32[...] = mm_tn(flat, dense[...])

    def get(p):
        rows = slice(p * 16, p * 16 + 16)
        pair = (folded_f32[rows, 0:LANES], folded_f32[rows, LANES : 2 * LANES])
        return times(pair, twist[0, p : p + 1, :], twist[1, p : p + 1, :])

    def put(s, pair):
        pair = times(pair, phase[0, s : s + 1, :], phase[1, s : s + 1, :])
        images[s, 0] = pair[0].astype(BF16)
        images[s, 1] = pair[1].astype(BF16)

    dft_over_blocks(get, put, work, 1.0)


def lane_group(shape):
    return lax.broadcasted_iota(jnp.int32, shape, 1) // 32


def unit_circle(turns):
    half = jnp.where(turns >= 128.0, turns - 256.0, turns) * (math.pi / 256.0)
    sq = half * half
    sine = 1.0 / 6227020800.0
    for term in (-1.0 / 39916800.0, 1.0 / 362880.0, -1.0 / 5040.0, 1.0 / 120.0, -1.0 / 6.0, 1.0):
        sine = sine * sq + term
    sine = sine * half
    cosine = 1.0 / 479001600.0
    for term in (-1.0 / 3628800.0, 1.0 / 40320.0, -1.0 / 720.0, 1.0 / 24.0, -0.5, 1.0):
        cosine = cosine * sq + term
    return 1.0 - 2.0 * sine * sine, 2.0 * sine * cosine


def over_pixels(values):
    return jnp.broadcast_to(values[:, None, :], (8, TS, LANES)).reshape(8 * TS, LANES)


def kernel_values(aux, weights, cols):
    pixel = (lax.broadcasted_iota(jnp.int32, (8 * TS, LANES), 0) % TS).astype(F32)
    square = (pixel - 8.0) * (pixel - 8.0)

    def one(step, carry):
        rows = pl.ds(pl.multiple_of(step * 8, 8), 8)
        turns = over_pixels(aux[5, rows, :]) * square
        turns = turns - 256.0 * jnp.floor(turns * (1.0 / 256.0))
        cosine, sine = unit_circle(turns)
        row_off = (pixel - over_pixels(aux[3, rows, :])) / kernel_width
        col_off = (pixel - over_pixels(aux[4, rows, :])) / kernel_width
        row_fall = kernel_norm * jnp.exp(-(row_off * row_off))
        col_fall = kernel_norm * jnp.exp(-(col_off * col_off))
        row_re, row_im = (row_fall * cosine).astype(BF16), (-row_fall * sine).astype(BF16)
        col_re, col_im = (col_fall * cosine).astype(BF16), (-col_fall * sine).astype(BF16)
        for half in range(2):
            which = 2 * step + half
            for slot in range(4):
                src = slice(half * 64 + slot * 16, half * 64 + slot * 16 + 16)
                lo = slice(slot * 32, slot * 32 + 16)
                hi = slice(slot * 32 + 16, slot * 32 + 32)
                weights[which, lo, 0:LANES] = row_re[src]
                weights[which, lo, LANES : 2 * LANES] = row_im[src]
                weights[which, hi, 0:LANES] = -row_im[src]
                weights[which, hi, LANES : 2 * LANES] = row_re[src]
        cols[step, :, 0:LANES] = col_re
        cols[step, :, LANES : 2 * LANES] = col_im
        return carry

    lax.fori_loop(0, SUBS // 2, one, 0)


def visit(tiles, aux, weights, cols, answers):
    group = lane_group((64, LANES))
    own = group == lax.broadcasted_iota(jnp.int32, (64, LANES), 0) // TS
    own_bf = own.astype(F32).astype(BF16)
    own_f32 = own.astype(F32)

    def one(step, carry):
        rows = pl.ds(pl.multiple_of(step * 8, 8), 8)
        parts = []
        for half in range(2):
            tile = tiles[2 * step + half]
            lhs = jnp.concatenate([tile, tile, tile, tile], axis=0) * own_bf
            parts.append(mm(lhs, weights[2 * step + half]))
        part = jnp.concatenate(parts, axis=0)
        part_re, part_im = part[:, 0:LANES], part[:, LANES : 2 * LANES]
        col_re = cols[step, :, 0:LANES].astype(F32)
        col_im = cols[step, :, LANES : 2 * LANES].astype(F32)
        pred_re = jnp.sum((col_re * part_re - col_im * part_im).reshape(8, TS, LANES), axis=1)
        pred_im = jnp.sum((col_re * part_im + col_im * part_re).reshape(8, TS, LANES), axis=1)
        weight = aux[2, rows, :]
        res_re = over_pixels(weight * (aux[0, rows, :] - pred_re))
        res_im = over_pixels(weight * (aux[1, rows, :] - pred_im))
        back_re = (col_re * res_re + col_im * res_im).astype(BF16)
        back_im = (col_re * res_im - col_im * res_re).astype(BF16)
        back = jnp.concatenate([back_re, back_im], axis=1)
        for half in range(2):
            grid = mm_nt(back[half * 64 : half * 64 + 64], weights[2 * step + half]) * own_f32
            tile = (grid[0:16] + grid[16:32]) + (grid[32:48] + grid[48:64])
            answers[2 * step + half] = tile.astype(BF16)
        return carry

    lax.fori_loop(0, SUBS // 2, one, 0)


def routing(own_lane, own_col, out_rows, back_rows):
    def one(step, carry):
        start = pl.multiple_of(step * 64, 64)
        rows = pl.ds(start, 64)
        row = lax.broadcasted_iota(jnp.int32, (64, 512), 0)
        lane = lax.broadcasted_iota(jnp.int32, (64, 512), 1)
        same = row % TS == lane % TS
        to_owner = same & (own_lane[0:1, :] == row // TS + step * 4)
        owner = own_col[rows, :]
        to_tile = same & (jnp.concatenate([owner] * 4, axis=1) == lane // TS)
        out_rows[rows, :] = to_owner.astype(F32).astype(BF16)
        back_rows[rows, :] = to_tile.astype(F32).astype(BF16)
        return carry

    lax.fori_loop(0, 8, one, 0)


def add_blocks(dst, sources, lo, count):
    def one(step, carry):
        total = sources[0][lo + step].astype(F32)
        for src in sources[1:]:
            total = total + src[lo + step].astype(F32)
        dst[lo + step] = total.astype(BF16)
        return carry

    lax.fori_loop(0, count, one, 0, unroll=4)


def middle_kernel(
    mine, phase, aux, own_lane, own_col, rank, dense, twist, rep, rep_t, sel, keep,
    out,
    pair_buf, sums, carry_a, carry_b, from_dn, from_up, total, gathered,
    work, folded, folded_f32, tiles, outgoing, arrived, answers, returned, my_tiles, images,
    weights, cols, out_rows, back_rows,
    pair_s, pair_r, ring_s, ring_r, send_s, first_r, tile_r, back_r, image_r, gath_s, gath_r,
):
    me = lax.axis_index("sub")
    facet = lax.axis_index("facet")
    core, chip = lax.rem(facet, 2), facet // 2
    sib = facet + 1 - 2 * core
    up, dn = lax.rem(facet + 2, FACETS), lax.rem(facet + 6, FACETS)
    opp = lax.rem(facet + 4, FACETS)
    low, high = pl.ds(0, 16), pl.ds(16, 16)

    barrier = pltpu.get_barrier_semaphore()

    def greet(step, carry):
        pl.semaphore_signal(barrier, inc=1, device_id={"sub": lax.rem(me + step, SUBS)}, device_id_type=MESH)
        return carry

    for peer in (sib, up, dn):
        pl.semaphore_signal(barrier, inc=1, device_id={"facet": peer}, device_id_type=MESH)
    lax.fori_loop(1, SUBS, greet, 0)
    pl.semaphore_wait(barrier, SUBS + 2)

    def to_facet(src, dst, ssem, rsem, peer):
        return pltpu.make_async_remote_copy(
            src_ref=src, dst_ref=dst, send_sem=ssem, recv_sem=rsem,
            device_id={"facet": peer}, device_id_type=MESH,
        )

    pairs = {}
    for hop in (2, 1, 3, 0):
        target = 2 * lax.rem(chip + hop, 4) + 1 - core
        pairs[hop] = to_facet(mine.at[target], pair_buf.at[hop], pair_s.at[hop], pair_r.at[hop], sib)
        pairs[hop].start()

    def merge_pair(hop):
        pairs[hop].wait_recv()
        target = 2 * lax.rem(chip + hop, 4) + core
        add_blocks(sums.at[hop], [mine.at[target], pair_buf.at[hop]], 0, SUBS)

    merge_pair(2)
    ring = [
        to_facet(sums.at[2, low], carry_a, ring_s.at[0], ring_r.at[0], up),
        to_facet(sums.at[2, high], carry_b, ring_s.at[1], ring_r.at[1], dn),
        to_facet(sums.at[1, high], from_dn.at[high], ring_s.at[2], ring_r.at[2], up),
        to_facet(sums.at[3, low], from_up.at[low], ring_s.at[3], ring_r.at[3], dn),
        to_facet(sums.at[1, low], from_dn.at[low], ring_s.at[4], ring_r.at[4], up),
        to_facet(sums.at[3, high], from_up.at[high], ring_s.at[5], ring_r.at[5], dn),
    ]
    ring[0].start()
    ring[1].start()
    merge_pair(1)
    ring[2].start()
    merge_pair(3)
    ring[3].start()
    kernel_values(aux, weights, cols)
    routing(own_lane, own_col, out_rows, back_rows)
    ring[0].wait_recv()
    add_blocks(sums.at[1, low], [sums.at[1, low], carry_a], 0, 16)
    ring[4].start()
    ring[1].wait_recv()
    add_blocks(sums.at[3, high], [sums.at[3, high], carry_b], 0, 16)
    ring[5].start()
    pairs[0].wait_recv()
    for step in (2, 3, 4, 5):
        ring[step].wait_recv()
    own_target = 2 * chip + core
    add_blocks(total, [mine.at[own_target], pair_buf.at[0], from_dn, from_up], 0, SUBS)

    def swap(src_of, dst, kind, rsem):
        def copy_to(peer, slot):
            return pltpu.make_async_remote_copy(
                src_ref=src_of.at[peer], dst_ref=dst.at[slot],
                send_sem=send_s.at[kind, peer], recv_sem=rsem.at[slot],
                device_id={"sub": peer}, device_id_type=MESH,
            )

        def send(step, carry):
            copy_to(lax.rem(me + step, SUBS), me).start()
            return carry

        def receive(step, carry):
            peer = lax.rem(me + SUBS - step, SUBS)
            copy_to(peer, peer).wait_recv()
            return carry

        def drain(step, carry):
            copy_to(lax.rem(me + step, SUBS), me).wait_send()
            return carry

        lax.fori_loop(1, SUBS, send, 0)
        dst[me] = src_of[me]
        lax.fori_loop(1, SUBS, receive, 0)
        return lambda: lax.fori_loop(1, SUBS, drain, 0)

    drains = [swap(total, gathered, 0, first_r)]
    columns_to_tiles(gathered, phase, dense, twist, rep, sel, keep, work, folded, tiles)
    outgoing[...] = mm(out_rows[...], tiles[...] * rank[...]).astype(BF16).reshape(SUBS, TS, LANES)
    drains.append(swap(outgoing, arrived, 1, tile_r))
    visit(arrived, aux, weights, cols, answers)
    drains.append(swap(answers, returned, 2, back_r))
    answer = returned[...].reshape(SUBS * TS, LANES)
    my_tiles[...] = mm(back_rows[...], answer).astype(BF16) * rank[...]
    tiles_to_columns(my_tiles, phase, dense, twist, rep_t, sel, keep, work, folded_f32, images)
    drains.append(swap(images, out.at[facet], 3, image_r))

    def share(index, src, peer):
        return to_facet(src, src, gath_s.at[index], gath_r.at[index], peer)

    own = out.at[facet]
    sends = [share(0, own, up), share(1, own, dn), share(2, own, sib)]
    for copy in sends:
        copy.start()

    def arrives(index, ref):
        share(index, ref, sib).wait_recv()

    arrives(0, out.at[dn])
    onward = [share(3, out.at[dn, low], up), share(5, out.at[dn], sib)]
    for copy in onward:
        copy.start()
    arrives(1, out.at[up])
    more = [share(4, out.at[up, high], dn), share(6, out.at[up], sib)]
    for copy in more:
        copy.start()
    arrives(3, out.at[opp, low])
    last = [share(7, out.at[opp, low], sib)]
    last[0].start()
    arrives(4, out.at[opp, high])
    last.append(share(8, out.at[opp, high], sib))
    last[1].start()
    other = 1 - 2 * core
    arrives(2, out.at[sib])
    arrives(5, out.at[dn + other])
    arrives(6, out.at[up + other])
    arrives(7, out.at[opp + other, low])
    arrives(8, out.at[opp + other, high])
    for copy in sends + onward + more + last + ring:
        copy.wait_send()
    for hop in range(4):
        pairs[hop].wait_send()
    for drain in drains:
        drain()


def vmem_specs(count):
    return [pl.BlockSpec(memory_space=pltpu.VMEM)] * count


def smem_specs(count):
    return [pl.BlockSpec(memory_space=pltpu.SMEM)] * count


BIG = 60 * 1024 * 1024
STRIPS = (FACETS, SUBS, 2, 16, LANES)


def rows_call(body, out_shape):
    return pl.pallas_call(
        body,
        out_shape=out_shape,
        in_specs=smem_specs(2) + vmem_specs(4),
        out_specs=pl.BlockSpec(memory_space=pltpu.VMEM),
        scratch_shapes=[pltpu.VMEM((LONG, LANES), F32)] * 4,
        compiler_params=pltpu.CompilerParams(vmem_limit_bytes=BIG),
    )


def middle_call():
    block = (SUBS, 2, 16, LANES)
    half = (16, 2, 16, LANES)
    tile = (SUBS, 16, LANES)
    vm = pltpu.VMEM
    dma = pltpu.SemaphoreType.DMA
    return pl.pallas_call(
        middle_kernel,
        out_shape=jax.ShapeDtypeStruct(STRIPS, BF16),
        in_specs=vmem_specs(12),
        out_specs=pl.BlockSpec(memory_space=pltpu.VMEM),
        scratch_shapes=[
            vm((4,) + block, BF16), vm((4,) + block, BF16), vm(half, BF16), vm(half, BF16),
            vm(block, BF16), vm(block, BF16), vm(block, BF16), vm(block, BF16),
            vm(block, F32), vm((512, 256), BF16), vm((512, 256), F32), vm((512, LANES), BF16),
            vm(tile, BF16), vm(tile, BF16), vm(tile, BF16), vm(tile, BF16),
            vm((512, LANES), BF16), vm(block, BF16),
            vm((SUBS, LANES, 2 * LANES), BF16), vm((SUBS // 2, LANES, 2 * LANES), BF16),
            vm((512, 512), BF16), vm((512, 512), BF16),
            dma((4,)), dma((4,)), dma((6,)), dma((6,)), dma((4, SUBS)),
            dma((SUBS,)), dma((SUBS,)), dma((SUBS,)), dma((SUBS,)), dma((9,)), dma((9,)),
        ],
        compiler_params=pltpu.CompilerParams(
            vmem_limit_bytes=BIG, collective_id=0, has_side_effects=True
        ),
    )


def route_tables(owners):
    owners = owners.reshape(SUBS)
    same = owners[:, None] == owners[None, :]
    earlier = jnp.arange(SUBS)[None, :] < jnp.arange(SUBS)[:, None]
    rank = jnp.sum((same & earlier).astype(jnp.int32), axis=1)
    owners = jnp.repeat(owners.reshape(16, 2).T.reshape(SUBS), TS)
    rank = jnp.repeat(rank.reshape(16, 2).T.reshape(SUBS), TS)
    group = jnp.arange(LANES, dtype=jnp.int32) // 32
    return (
        jnp.broadcast_to(owners[None, :], (8, 512)),
        jnp.broadcast_to(owners[:, None], (512, LANES)),
        (rank[:, None] == group[None, :]).astype(BF16),
    )


def per_device(
    facet_strips, row_window, col_window, row_offsets, col_offsets,
    tile_owner, measured, vis_weight, uvw_pixels, vis_count,
):
    facet = lax.axis_index("facet")
    first, second = row_tables()
    dense, twist, rep, rep_t, sel, keep = col_tables()
    win = row_window[:, None] * col_window[None, :]
    turns = (facet * row_offsets % FACETS).astype(F32) * (2.0 * math.pi / FACETS)
    turn = jnp.stack([jnp.cos(turns), jnp.sin(turns)])
    start = lax.dynamic_index_in_dim(col_offsets, facet, keepdims=False)
    column = jnp.arange(LONG, dtype=jnp.int32).reshape(SUBS, LANES)
    angle = (column * start % LONG).astype(F32) * (2.0 * math.pi / LONG)
    phase = jnp.stack([jnp.cos(angle), jnp.sin(angle)])
    live = jnp.arange(LANES, dtype=jnp.int32)[None, :] < vis_count[0, 0][:, None]
    weight = jnp.where(live, vis_weight[0, 0], 0.0)
    pixels = uvw_pixels[0, 0].astype(F32)
    aux = jnp.stack(
        [measured[0, 0, :, 0], measured[0, 0, :, 1], weight, pixels[:, 0], pixels[:, 1], pixels[:, 2]]
    )
    own_lane, own_col, rank = route_tables(tile_owner)
    contributions = rows_call(forward_kernel, jax.ShapeDtypeStruct(STRIPS, BF16))(
        row_offsets, turn, facet_strips, win, first, second
    )
    strips = middle_call()(
        contributions, phase, aux, own_lane, own_col, rank, dense, twist, rep, rep_t, sel, keep
    )
    return rows_call(backward_kernel, jax.ShapeDtypeStruct(facet_strips.shape, BF16))(
        row_offsets, turn, strips, win, first, second
    )


def solution(mesh):
    in_specs = (
        P(None, "facet", "sub"),
        P(),
        P("sub"),
        P(),
        P(),
        P("sub", "facet", None, None),
        P("facet", "sub", None, None, None),
        P("facet", "sub", None, None),
        P("facet", "sub", None, None, None),
        P("facet", "sub", None),
    )
    return jax.shard_map(
        per_device, mesh=mesh, in_specs=in_specs, out_specs=P(None, "facet", "sub"), check_vma=False
    )
```

```python
import math

import jax
import jax.numpy as jnp
import numpy as np
from jax import lax
from jax.experimental import pallas as pl
from jax.experimental.pallas import tpu as pltpu
from jax.sharding import PartitionSpec as P

SG = 512
RADIX = 64
TS = 16
LONG = 4096
SUBS = 32
FACETS = 8
CAP = 4
LANES = 128
MESH = pl.DeviceIdType.MESH
F32 = jnp.float32
BF16 = jnp.bfloat16

kernel_width = 2.5
kernel_norm = 0.565


def as_real(theta):
    cosine, sine = np.cos(theta), np.sin(theta)
    return np.block([[cosine, sine], [-sine, cosine]])


def row_tables():
    idx = np.arange(RADIX)
    first = as_real(2 * np.pi * (np.outer(idx, idx) % RADIX) / RADIX)
    second = [
        as_real(2 * np.pi * (np.outer(k1 + RADIX * idx, idx) % LONG) / LONG) / RADIX
        for k1 in range(RADIX)
    ]
    return jnp.asarray(first, BF16), jnp.asarray(np.stack(second), BF16)


def col_tables():
    high = np.outer(np.arange(16), np.arange(LANES)) % LANES
    dense = as_real(2 * np.pi * high / LANES)
    low = 2 * np.pi * np.outer(np.arange(SUBS), np.arange(LANES)) / LONG
    twist = np.stack([np.cos(low), np.sin(low)]) / 64.0
    rep = np.zeros((512, 32))
    rep[np.arange(512), np.arange(512) // 16] = 1
    sel = np.zeros((2, 16, 16, 4, 2, 16))
    for z in range(2):
        for r in range(16):
            sel[z, :, r, :, z, r] = 1
    sel = sel.reshape(512, 128)
    keep = (np.arange(512)[:, None] % 16) == (np.arange(512)[None, :] // 16 % 16)
    return (
        jnp.asarray(dense, BF16),
        jnp.asarray(twist, F32),
        jnp.asarray(rep, BF16),
        jnp.asarray(rep.T, BF16),
        jnp.asarray(sel, BF16),
        jnp.asarray(keep, BF16),
    )


def mm(first, other):
    return jnp.dot(first, other, preferred_element_type=F32)


def mm_nt(first, other):
    return lax.dot_general(first, other, (((1,), (1,)), ((), ())), preferred_element_type=F32)


def mm_tn(first, other):
    return lax.dot_general(first, other, (((0,), (0,)), ((), ())), preferred_element_type=F32)


PITCH = RADIX + 1
WIDE = 2 * RADIX + 1


def strided(index, pitch):
    return pl.ds(index, RADIX, stride=pitch)


def transform_rows(fetch, mid_re, mid_im, first, second, put):
    def stage_a(step, carry):
        parts = []
        for u in range(2):
            real, imag = fetch(2 * step + u)
            parts.append(jnp.concatenate([real, imag], axis=0).astype(BF16))
        res = mm(first[...], jnp.concatenate(parts, axis=1))
        for u in range(2):
            rows = strided(2 * step + u, PITCH)
            mid_re[rows, :] = res[:RADIX, u * LANES : (u + 1) * LANES]
            mid_im[rows, :] = res[RADIX:, u * LANES : (u + 1) * LANES]
        return carry

    lax.fori_loop(0, RADIX // 2, stage_a, 0, unroll=8)

    def stage_b(step, carry):
        rows = pl.ds(step * PITCH, RADIX)
        block = jnp.concatenate([mid_re[rows, :], mid_im[rows, :]], axis=0).astype(BF16)
        res = mm(second[step], block)
        put(step, res[:RADIX], res[RADIX:])
        return carry

    lax.fori_loop(0, RADIX, stage_b, 0, unroll=16)


def forward_kernel(
    offs, turn, strip, row_win, col_win, first, second_hbm, out_hbm,
    re, im, mid_re, mid_im, wide_re, wide_im, second, out, second_sem, out_sem,
):
    table = pltpu.make_async_copy(second_hbm, second, second_sem)
    table.start()
    facet = lax.axis_index("facet")
    row_win = row_win[...].T
    scale = col_win[...]
    for block in range(RADIX):
        window = row_win[:, block : block + 1] * scale
        rows, src = pl.ds(block * PITCH, RADIX), pl.ds(block * RADIX, RADIX)
        re[rows, :] = strip[0, src, :].astype(F32) * window
        im[rows, :] = strip[1, src, :].astype(F32) * window
    table.wait()

    def fetch(index):
        rows = strided(index, PITCH)
        return re[rows, :], im[rows, :]

    def put(index, real, imag):
        here, before = strided(WIDE + index, WIDE), strided(RADIX + index, WIDE)
        wide_re[here, :] = real
        wide_im[here, :] = imag
        wide_re[before, :] = real
        wide_im[before, :] = imag

    transform_rows(fetch, mid_re, mid_im, first, second, put)

    def emit(which, carry):
        base = offs[which]
        index = (facet * base) & (FACETS - 1)
        cosine, sine = turn[0, index], turn[1, index]
        start = WIDE + base // RADIX * WIDE + base % RADIX
        for part in range(8):
            rows = pl.ds(start + part * WIDE, RADIX)
            real, imag = wide_re[rows, :], wide_im[rows, :]
            blocks = pl.ds(part * 4, 4)
            out[which, blocks, 0] = (cosine * real + sine * imag).astype(BF16).reshape(4, 16, LANES)
            out[which, blocks, 1] = (cosine * imag - sine * real).astype(BF16).reshape(4, 16, LANES)
        pltpu.make_async_copy(out.at[which], out_hbm.at[which], out_sem.at[which]).start()
        return carry

    lax.fori_loop(0, FACETS, emit, 0)
    for which in range(FACETS):
        pltpu.make_async_copy(out.at[which], out_hbm.at[which], out_sem.at[which]).wait()


def backward_kernel(
    offs, turn, strips, row_win, col_win, first, second_hbm, out_hbm,
    re, im, mid_re, mid_im, wide_re, wide_im, second, out, second_sem, out_sem,
):
    table = pltpu.make_async_copy(second_hbm, second, second_sem)
    table.start()
    facet = lax.axis_index("facet")
    row_win = row_win[...].T

    def clear(step, carry):
        rows = pl.ds(pl.multiple_of(step * 128, 128), 128)
        wide_re[rows, :] = jnp.zeros((128, LANES), F32)
        wide_im[rows, :] = jnp.zeros((128, LANES), F32)
        return carry

    lax.fori_loop(0, WIDE_ROWS // 128, clear, 0, unroll=2)

    def place(which, carry):
        base = offs[which]
        index = (facet * base) & (FACETS - 1)
        cosine, sine = turn[0, index], turn[1, index]
        start = WIDE + base // RADIX * WIDE + base % RADIX
        for part in range(8):
            rows = pl.ds(start + part * WIDE, RADIX)
            blocks = pl.ds(part * 4, 4)
            real = strips[which, blocks, 0].reshape(RADIX, LANES).astype(F32)
            imag = strips[which, blocks, 1].reshape(RADIX, LANES).astype(F32)
            wide_re[rows, :] = wide_re[rows, :] + (cosine * real - sine * imag)
            wide_im[rows, :] = wide_im[rows, :] - (sine * real + cosine * imag)
        return carry

    lax.fori_loop(0, FACETS, place, 0)
    table.wait()

    def fetch(index):
        here, before = strided(WIDE + index, WIDE), strided(RADIX + index, WIDE)
        return wide_re[here, :] + wide_re[before, :], wide_im[here, :] + wide_im[before, :]

    def put(index, real, imag):
        rows = strided(index, PITCH)
        re[rows, :] = real
        im[rows, :] = imag

    transform_rows(fetch, mid_re, mid_im, first, second, put)
    scale = col_win[...]
    quarter = LONG // 4
    copies = []
    for block in range(RADIX):
        window = row_win[:, block : block + 1] * scale
        rows, dst = pl.ds(block * PITCH, RADIX), pl.ds(block * RADIX, RADIX)
        out[0, dst, :] = (re[rows, :] * window).astype(BF16)
        out[1, dst, :] = (im[rows, :] * -window).astype(BF16)
        if block % 16 == 15:
            done = pl.ds(block // 16 * quarter, quarter)
            copies.append(
                pltpu.make_async_copy(out.at[:, done], out_hbm.at[:, done], out_sem.at[block // 16])
            )
            copies[-1].start()
    for copy in copies:
        copy.wait()


def times(pair, cosine, sine):
    return (pair[0] * cosine - pair[1] * sine, pair[0] * sine + pair[1] * cosine)


def times_unit(pair, num, den, sign):
    num = num % den
    if num == 0:
        return pair
    if 4 * num == den:
        return (-sign * pair[1], sign * pair[0])
    if 2 * num == den:
        return (-pair[0], -pair[1])
    angle = 2 * math.pi * num / den
    return times(pair, math.cos(angle), sign * math.sin(angle))


def small_dft(items, sign):
    count = len(items)
    if count == 1:
        return items
    even = small_dft(items[0::2], sign)
    odd = small_dft(items[1::2], sign)
    odd = [times_unit(odd[i], i, count, sign) for i in range(count // 2)]
    low = [(a[0] + b[0], a[1] + b[1]) for a, b in zip(even, odd)]
    high = [(a[0] - b[0], a[1] - b[1]) for a, b in zip(even, odd)]
    return low + high


def dft_over_blocks(get, put, work, sign):
    for lo in range(8):
        items = small_dft([get(lo + 8 * hi) for hi in range(4)], sign)
        for p_lo in range(4):
            value = times_unit(items[p_lo], lo * p_lo, SUBS, sign)
            work[p_lo * 8 + lo, 0] = value[0]
            work[p_lo * 8 + lo, 1] = value[1]
    for p_lo in range(4):
        items = small_dft([(work[p_lo * 8 + lo, 0], work[p_lo * 8 + lo, 1]) for lo in range(8)], sign)
        for p_hi in range(8):
            put(p_lo + 4 * p_hi, items[p_hi])


def columns_to_tiles(blocks, phase, dense, twist, rep, sel, keep, work, folded, tiles):
    def get(s):
        pair = (blocks[s, 0].astype(F32), blocks[s, 1].astype(F32))
        return times(pair, phase[0, s : s + 1, :], -phase[1, s : s + 1, :])

    def put(p, pair):
        pair = times(pair, twist[0, p : p + 1, :], -twist[1, p : p + 1, :])
        rows = slice(p * 16, p * 16 + 16)
        folded[rows, 0:LANES] = pair[0].astype(BF16)
        folded[rows, LANES : 2 * LANES] = pair[1].astype(BF16)

    dft_over_blocks(get, put, work, -1.0)
    flat = mm_nt(dense[...], folded[...]).astype(BF16)
    stacked = jnp.concatenate(
        [
            jnp.concatenate([flat[0:16, 0:256], flat[16:32, 0:256]], axis=1),
            jnp.concatenate([flat[0:16, 256:512], flat[16:32, 256:512]], axis=1),
        ],
        axis=0,
    )
    spread = mm(rep[...], stacked).astype(BF16) * keep[...]
    own = as_bf(iota((512, LANES), 1) // 32 == iota((512, LANES), 0) // TS % CAP)
    tiles[...] = mm(spread, sel[...]).astype(BF16) * own


def tiles_to_columns(tiles, phase, dense, twist, rep_t, sel, keep, work, folded_f32, images):
    spread = mm_nt(tiles[...], sel[...]).astype(BF16) * keep[...]
    stacked = mm(rep_t[...], spread).astype(BF16)
    flat = jnp.concatenate(
        [
            jnp.concatenate([stacked[0:16, 0:256], stacked[16:32, 0:256]], axis=1),
            jnp.concatenate([stacked[0:16, 256:512], stacked[16:32, 256:512]], axis=1),
        ],
        axis=0,
    )
    folded_f32[...] = mm_tn(flat, dense[...])

    def get(p):
        rows = slice(p * 16, p * 16 + 16)
        pair = (folded_f32[rows, 0:LANES], folded_f32[rows, LANES : 2 * LANES])
        return times(pair, twist[0, p : p + 1, :], twist[1, p : p + 1, :])

    def put(s, pair):
        pair = times(pair, phase[0, s : s + 1, :], phase[1, s : s + 1, :])
        images[s, 0] = pair[0].astype(BF16)
        images[s, 1] = pair[1].astype(BF16)

    dft_over_blocks(get, put, work, 1.0)


VALUES = 8


def unit_circle(turns, total):
    half = jnp.where(turns >= total / 2.0, turns - total, turns) * (math.pi / total)
    sq = half * half
    sine = 1.0 / 6227020800.0
    for term in (-1.0 / 39916800.0, 1.0 / 362880.0, -1.0 / 5040.0, 1.0 / 120.0, -1.0 / 6.0, 1.0):
        sine = sine * sq + term
    sine = sine * half
    cosine = 1.0 / 479001600.0
    for term in (-1.0 / 3628800.0, 1.0 / 40320.0, -1.0 / 720.0, 1.0 / 24.0, -0.5, 1.0):
        cosine = cosine * sq + term
    return 1.0 - 2.0 * sine * sine, 2.0 * sine * cosine


def over_pixels(values):
    return jnp.broadcast_to(values[:, None, :], (8, TS, LANES)).reshape(8 * TS, LANES)


def pack_visibilities(measured, masked, pixels, staged, packed):
    for part in range(4):
        rows = pl.ds(part * 32, 32)
        blocks = pl.ds(part * 8, 8)
        values = []
        for z in range(2):
            value = measured[rows, z, :]
            coarse = value.astype(BF16).astype(F32)
            values += [coarse, value - coarse]
        values.append(masked[rows, :])
        values += [pixels[rows, i, :].astype(F32) for i in range(3)]
        for q in range(VALUES):
            staged[blocks, q * CAP : (q + 1) * CAP, :] = values[q].reshape(8, CAP, LANES)
        packed[blocks] = staged[blocks].astype(BF16)


def visit(tiles, vis, my_tiles):
    pixel = (iota((8 * TS, LANES), 0) % TS).astype(F32)
    square = (pixel - 8.0) * (pixel - 8.0)
    own = (iota((64, LANES), 1) // 32 == iota((64, LANES), 0) // TS).astype(F32)

    for step in range(4):
        def value(q):
            return vis[q * SUBS + step * 8 : q * SUBS + step * 8 + 8, :]

        turns = over_pixels(value(7)) * square
        turns = turns - 256.0 * jnp.floor(turns * (1.0 / 256.0))
        cosine, sine = unit_circle(turns, 256.0)
        row_off = (pixel - over_pixels(value(5))) / kernel_width
        col_off = (pixel - over_pixels(value(6))) / kernel_width
        row_fall = kernel_norm * jnp.exp(-(row_off * row_off))
        col_fall = kernel_norm * jnp.exp(-(col_off * col_off))
        row_re, row_im = (row_fall * cosine).astype(BF16), (-row_fall * sine).astype(BF16)
        upper = jnp.concatenate([row_re, row_im], axis=1)
        lower = jnp.concatenate([-row_im, row_re], axis=1)
        weights = []
        for half in range(2):
            pieces = []
            for slot in range(4):
                src = slice(half * 64 + slot * TS, half * 64 + slot * TS + TS)
                pieces += [upper[src], lower[src]]
            weights.append(jnp.concatenate(pieces, axis=0))
        col_re = (col_fall * cosine).astype(BF16).astype(F32)
        col_im = (-col_fall * sine).astype(BF16).astype(F32)
        first = step * 128
        part = jnp.concatenate(
            [mm(tiles[first + half * 64 : first + half * 64 + 64, :], weights[half]) for half in range(2)],
            axis=0,
        )
        part_re, part_im = part[:, 0:LANES], part[:, LANES : 2 * LANES]
        pred_re = jnp.sum((col_re * part_re - col_im * part_im).reshape(8, TS, LANES), axis=1)
        pred_im = jnp.sum((col_re * part_im + col_im * part_re).reshape(8, TS, LANES), axis=1)
        weight = value(4)
        res_re = over_pixels(weight * (value(0) + value(1) - pred_re))
        res_im = over_pixels(weight * (value(2) + value(3) - pred_im))
        back_re = (col_re * res_re + col_im * res_im).astype(BF16)
        back_im = (col_re * res_im - col_im * res_re).astype(BF16)
        back = jnp.concatenate([back_re, back_im], axis=1)
        for half in range(2):
            grid = mm_nt(back[half * 64 : half * 64 + 64], weights[half]) * own
            my_tiles[first + half * 64 : first + half * 64 + 64, :] = grid.astype(BF16)


def as_bf(condition):
    return condition.astype(F32).astype(BF16)


def iota(shape, dim):
    return lax.broadcasted_iota(jnp.int32, shape, dim)


def masked_weights(weight, counts, masked):
    identity = as_bf(iota((LANES, LANES), 0) == iota((LANES, LANES), 1))
    spread = jnp.broadcast_to(counts[...].astype(F32), (LANES, LANES)).astype(BF16)
    column = mm_nt(identity, spread)
    masked[...] = jnp.where(iota((LANES, LANES), 1).astype(F32) < column, weight[...], 0.0)


def column_phase(facet, offsets, phase):
    mine = jnp.where(iota((1, FACETS), 1) == facet, offsets[...], 0)
    start = jnp.sum(mine.astype(F32), axis=1, keepdims=True).astype(jnp.int32)
    column = iota((SUBS, LANES), 0) * LANES + iota((SUBS, LANES), 1)
    turns = ((column * start) & (LONG - 1)).astype(F32)
    cosine, sine = unit_circle(turns, float(LONG))
    phase[0] = cosine
    phase[1] = sine


def routing(owners, choice):
    square = (SUBS, SUBS)
    up, across = iota(square, 0), iota(square, 1)
    named = as_bf(owners[...] == up)
    moved = as_bf(across == up % 2 * 16 + up // 2)
    identity = as_bf(up == across)
    earlier = mm(named, as_bf(up < across)).astype(BF16)
    named = mm(named, moved).astype(BF16)
    rank = jnp.sum(named.astype(F32) * mm(earlier, moved), axis=0, keepdims=True)
    rank = mm_nt(identity, jnp.broadcast_to(rank, (LANES, SUBS)).astype(BF16))
    by_tile = mm_nt(identity, named).astype(BF16)
    wide = (SUBS, SUBS * SUBS)
    by_tile = mm(by_tile, as_bf(iota(wide, 1) // SUBS == iota(wide, 0)))
    at_rank = (rank == (iota((SUBS, LANES), 1) % CAP).astype(F32)).astype(F32)
    both = by_tile * jnp.concatenate([at_rank] * 8, axis=1)
    which = iota(wide, 1) % SUBS // CAP
    for q in range(VALUES):
        choice[q * SUBS : (q + 1) * SUBS, :] = jnp.where(which == q, both, 0.0).astype(BF16)


def add_blocks(dst, sources, lo, count):
    def one(step, carry):
        total = sources[0][lo + step].astype(F32)
        for src in sources[1:]:
            total = total + src[lo + step].astype(F32)
        dst[lo + step] = total.astype(BF16)
        return carry

    lax.fori_loop(0, count, one, 0, unroll=4)


def middle_kernel(
    mine, offsets, owners, measured, weight, pixels, counts, dense, twist, rep, rep_t, sel, keep,
    out,
    pair_buf, sums, carry_a, carry_b, from_dn, from_up, total, gathered,
    work, folded, folded_f32, tiles, my_tiles, images,
    masked, phase, staged, packed, received, choice, vis,
    pair_s, pair_r, ring_s, ring_r, send_s, first_r, vis_r, image_r, gath_s, gath_r,
):
    me = lax.axis_index("sub")
    facet = lax.axis_index("facet")
    core, chip = lax.rem(facet, 2), facet // 2
    sib = facet + 1 - 2 * core
    up, dn = lax.rem(facet + 2, FACETS), lax.rem(facet + 6, FACETS)
    opp = lax.rem(facet + 4, FACETS)
    low, high = pl.ds(0, 16), pl.ds(16, 16)

    barrier = pltpu.get_barrier_semaphore()

    def greet(step, carry):
        pl.semaphore_signal(barrier, inc=1, device_id={"sub": lax.rem(me + step, SUBS)}, device_id_type=MESH)
        return carry

    for peer in (sib, up, dn):
        pl.semaphore_signal(barrier, inc=1, device_id={"facet": peer}, device_id_type=MESH)
    lax.fori_loop(1, SUBS, greet, 0)
    pl.semaphore_wait(barrier, SUBS + 2)

    def to_facet(src, dst, ssem, rsem, peer):
        return pltpu.make_async_remote_copy(
            src_ref=src, dst_ref=dst, send_sem=ssem, recv_sem=rsem,
            device_id={"facet": peer}, device_id_type=MESH,
        )

    def swap(src_of, dst, kind, rsem):
        def copy_to(peer, slot):
            return pltpu.make_async_remote_copy(
                src_ref=src_of.at[peer], dst_ref=dst.at[slot],
                send_sem=send_s.at[kind, peer], recv_sem=rsem.at[slot],
                device_id={"sub": peer}, device_id_type=MESH,
            )

        def send(step, carry):
            copy_to(lax.rem(me + step, SUBS), me).start()
            return carry

        def receive(step, carry):
            peer = lax.rem(me + SUBS - step, SUBS)
            copy_to(peer, peer).wait_recv()
            return carry

        def drain(step, carry):
            copy_to(lax.rem(me + step, SUBS), me).wait_send()
            return carry

        lax.fori_loop(1, SUBS, send, 0)
        dst[me] = src_of[me]
        return (
            lambda: lax.fori_loop(1, SUBS, receive, 0),
            lambda: lax.fori_loop(1, SUBS, drain, 0),
        )

    pairs = {}
    for hop in (2, 1, 3, 0):
        target = 2 * lax.rem(chip + hop, 4) + 1 - core
        pairs[hop] = to_facet(mine.at[target], pair_buf.at[hop], pair_s.at[hop], pair_r.at[hop], sib)
        pairs[hop].start()

    masked_weights(weight, counts, masked)
    pack_visibilities(measured, masked, pixels, staged, packed)
    receive_vis, drain_vis = swap(packed, received, 1, vis_r)

    def merge_pair(hop):
        pairs[hop].wait_recv()
        target = 2 * lax.rem(chip + hop, 4) + core
        add_blocks(sums.at[hop], [mine.at[target], pair_buf.at[hop]], 0, SUBS)

    merge_pair(2)
    ring = [
        to_facet(sums.at[2, low], carry_a, ring_s.at[0], ring_r.at[0], up),
        to_facet(sums.at[2, high], carry_b, ring_s.at[1], ring_r.at[1], dn),
        to_facet(sums.at[1, high], from_dn.at[high], ring_s.at[2], ring_r.at[2], up),
        to_facet(sums.at[3, low], from_up.at[low], ring_s.at[3], ring_r.at[3], dn),
        to_facet(sums.at[1, low], from_dn.at[low], ring_s.at[4], ring_r.at[4], up),
        to_facet(sums.at[3, high], from_up.at[high], ring_s.at[5], ring_r.at[5], dn),
    ]
    ring[0].start()
    ring[1].start()
    merge_pair(1)
    ring[2].start()
    merge_pair(3)
    ring[3].start()
    column_phase(facet, offsets, phase)
    routing(owners, choice)
    ring[0].wait_recv()
    add_blocks(sums.at[1, low], [sums.at[1, low], carry_a], 0, 16)
    ring[4].start()
    ring[1].wait_recv()
    add_blocks(sums.at[3, high], [sums.at[3, high], carry_b], 0, 16)
    ring[5].start()
    pairs[0].wait_recv()
    for step in (2, 3, 4, 5):
        ring[step].wait_recv()
    own_target = 2 * chip + core
    add_blocks(total, [mine.at[own_target], pair_buf.at[0], from_dn, from_up], 0, SUBS)

    receive_rows, drain_rows = swap(total, gathered, 0, first_r)
    receive_vis()
    vis[...] = mm(choice[...], received[...].reshape(SUBS * SUBS, LANES))
    receive_rows()
    columns_to_tiles(gathered, phase, dense, twist, rep, sel, keep, work, folded, tiles)
    visit(tiles, vis, my_tiles)
    tiles_to_columns(my_tiles, phase, dense, twist, rep_t, sel, keep, work, folded_f32, images)
    receive_images, drain_images = swap(images, out.at[facet], 2, image_r)
    receive_images()

    def share(index, src, peer):
        return to_facet(src, src, gath_s.at[index], gath_r.at[index], peer)

    own = out.at[facet]
    sends = [share(0, own, up), share(1, own, dn), share(2, own, sib)]
    for copy in sends:
        copy.start()

    def arrives(index, ref):
        share(index, ref, sib).wait_recv()

    arrives(0, out.at[dn])
    onward = [share(3, out.at[dn, low], up), share(5, out.at[dn], sib)]
    for copy in onward:
        copy.start()
    arrives(1, out.at[up])
    more = [share(4, out.at[up, high], dn), share(6, out.at[up], sib)]
    for copy in more:
        copy.start()
    arrives(3, out.at[opp, low])
    last = [share(7, out.at[opp, low], sib)]
    last[0].start()
    arrives(4, out.at[opp, high])
    last.append(share(8, out.at[opp, high], sib))
    last[1].start()
    other = 1 - 2 * core
    arrives(2, out.at[sib])
    arrives(5, out.at[dn + other])
    arrives(6, out.at[up + other])
    arrives(7, out.at[opp + other, low])
    arrives(8, out.at[opp + other, high])
    for copy in sends + onward + more + last + ring:
        copy.wait_send()
    for hop in range(4):
        pairs[hop].wait_send()
    for drain in (drain_rows, drain_vis, drain_images):
        drain()


def vmem_specs(count):
    return [pl.BlockSpec(memory_space=pltpu.VMEM)] * count


def smem_specs(count):
    return [pl.BlockSpec(memory_space=pltpu.SMEM)] * count


BIG = 60 * 1024 * 1024
STRIPS = (FACETS, SUBS, 2, 16, LANES)
WIDE_ROWS = 66 * 128


def rows_call(body, shape):
    narrow, wide = pltpu.VMEM((RADIX * PITCH, LANES), F32), pltpu.VMEM((WIDE_ROWS, LANES), F32)
    return pl.pallas_call(
        body,
        out_shape=jax.ShapeDtypeStruct(shape, BF16),
        in_specs=smem_specs(2) + vmem_specs(4) + [pl.BlockSpec(memory_space=pl.ANY)],
        out_specs=pl.BlockSpec(memory_space=pl.ANY),
        scratch_shapes=[narrow] * 4
        + [wide] * 2
        + [
            pltpu.VMEM((RADIX, 2 * RADIX, 2 * RADIX), BF16),
            pltpu.VMEM(shape, BF16),
            pltpu.SemaphoreType.DMA,
            pltpu.SemaphoreType.DMA((FACETS,)),
        ],
        compiler_params=pltpu.CompilerParams(vmem_limit_bytes=BIG),
    )


def middle_call():
    block = (SUBS, 2, 16, LANES)
    half = (16, 2, 16, LANES)
    values = (SUBS, VALUES * CAP, LANES)
    vm = pltpu.VMEM
    dma = pltpu.SemaphoreType.DMA
    return pl.pallas_call(
        middle_kernel,
        out_shape=jax.ShapeDtypeStruct(STRIPS, BF16),
        in_specs=vmem_specs(13),
        out_specs=pl.BlockSpec(memory_space=pltpu.VMEM),
        scratch_shapes=[
            vm((4,) + block, BF16), vm((4,) + block, BF16), vm(half, BF16), vm(half, BF16),
            vm(block, BF16), vm(block, BF16), vm(block, BF16), vm(block, BF16),
            vm(block, F32), vm((512, 256), BF16), vm((512, 256), F32),
            vm((512, LANES), BF16), vm((512, LANES), BF16), vm(block, BF16),
            vm((LANES, LANES), F32), vm((2, SUBS, LANES), F32),
            vm(values, F32), vm(values, BF16), vm(values, BF16),
            vm((VALUES * SUBS, SUBS * SUBS), BF16), vm((VALUES * SUBS, LANES), F32),
            dma((4,)), dma((4,)), dma((6,)), dma((6,)), dma((3, SUBS)),
            dma((SUBS,)), dma((SUBS,)), dma((SUBS,)), dma((9,)), dma((9,)),
        ],
        compiler_params=pltpu.CompilerParams(
            vmem_limit_bytes=BIG, collective_id=0, has_side_effects=True
        ),
    )


def per_device(
    facet_strips, row_window, col_window, row_offsets, col_offsets,
    tile_owner, measured, vis_weight, uvw_pixels, vis_count,
):
    first, second = row_tables()
    dense, twist, rep, rep_t, sel, keep = col_tables()
    eighth = 2 * np.pi * np.arange(FACETS) / FACETS
    turn = jnp.asarray(np.stack([np.cos(eighth), np.sin(eighth)]), F32)
    row_win = row_window.reshape(RADIX, RADIX)
    col_win = col_window.reshape(1, LANES)
    contributions = rows_call(forward_kernel, STRIPS)(
        row_offsets, turn, facet_strips, row_win, col_win, first, second
    )
    strips = middle_call()(
        contributions, col_offsets.reshape(1, FACETS), tile_owner.reshape(1, SUBS), measured[0, 0],
        vis_weight[0, 0], uvw_pixels[0, 0], vis_count.reshape(1, LANES),
        dense, twist, rep, rep_t, sel, keep,
    )
    return rows_call(backward_kernel, facet_strips.shape)(
        row_offsets, turn, strips, row_win, col_win, first, second
    )


def solution(mesh):
    in_specs = (
        P(None, "facet", "sub"),
        P(),
        P("sub"),
        P(),
        P(),
        P("sub", "facet", None, None),
        P("facet", "sub", None, None, None),
        P("facet", "sub", None, None),
        P("facet", "sub", None, None, None),
        P("facet", "sub", None),
    )
    return jax.shard_map(
        per_device, mesh=mesh, in_specs=in_specs, out_specs=P(None, "facet", "sub"), check_vma=False
    )
```

```python
import math

import jax
import jax.numpy as jnp
import numpy as np
from jax import lax
from jax.experimental import pallas as pl
from jax.experimental.pallas import tpu as pltpu
from jax.sharding import PartitionSpec as P

SG = 512
RADIX = 64
TS = 16
LONG = 4096
SUBS = 32
FACETS = 8
CAP = 4
LANES = 128
MESH = pl.DeviceIdType.MESH
F32 = jnp.float32
BF16 = jnp.bfloat16

kernel_width = 2.5
kernel_norm = 0.565


def as_real(theta):
    cosine, sine = np.cos(theta), np.sin(theta)
    return np.block([[cosine, sine], [-sine, cosine]])


def row_tables():
    idx = np.arange(RADIX)
    first = as_real(2 * np.pi * (np.outer(idx, idx) % RADIX) / RADIX)
    second = [
        as_real(2 * np.pi * (np.outer(k1 + RADIX * idx, idx) % LONG) / LONG) / RADIX
        for k1 in range(RADIX)
    ]
    return jnp.asarray(first, BF16), jnp.asarray(np.stack(second), BF16)


def col_tables():
    high = np.outer(np.arange(16), np.arange(LANES)) % LANES
    dense = as_real(2 * np.pi * high / LANES)
    low = 2 * np.pi * np.outer(np.arange(SUBS), np.arange(LANES)) / LONG
    twist = np.stack([np.cos(low), np.sin(low)]) / 64.0
    rep = np.zeros((512, 32))
    rep[np.arange(512), np.arange(512) // 16] = 1
    sel = np.zeros((2, 16, 16, 4, 2, 16))
    for z in range(2):
        for r in range(16):
            sel[z, :, r, :, z, r] = 1
    sel = sel.reshape(512, 128)
    keep = (np.arange(512)[:, None] % 16) == (np.arange(512)[None, :] // 16 % 16)
    return (
        jnp.asarray(dense, BF16),
        jnp.asarray(twist, F32),
        jnp.asarray(rep, BF16),
        jnp.asarray(rep.T, BF16),
        jnp.asarray(sel, BF16),
        jnp.asarray(keep, BF16),
    )


def mm(first, other):
    return jnp.dot(first, other, preferred_element_type=F32)


def mm_nt(first, other):
    return lax.dot_general(first, other, (((1,), (1,)), ((), ())), preferred_element_type=F32)


def mm_tn(first, other):
    return lax.dot_general(first, other, (((0,), (0,)), ((), ())), preferred_element_type=F32)


PITCH = RADIX + 1
WIDE = 2 * RADIX + 1


def strided(index, pitch):
    return pl.ds(index, RADIX, stride=pitch)


def transform_rows(fetch, mid_re, mid_im, first, second, put):
    def stage_a(step, carry):
        parts = []
        for u in range(2):
            real, imag = fetch(2 * step + u)
            parts.append(jnp.concatenate([real, imag], axis=0).astype(BF16))
        res = mm(first[...], jnp.concatenate(parts, axis=1))
        for u in range(2):
            rows = strided(2 * step + u, PITCH)
            mid_re[rows, :] = res[:RADIX, u * LANES : (u + 1) * LANES]
            mid_im[rows, :] = res[RADIX:, u * LANES : (u + 1) * LANES]
        return carry

    lax.fori_loop(0, RADIX // 2, stage_a, 0, unroll=8)

    def stage_b(step, carry):
        rows = pl.ds(step * PITCH, RADIX)
        block = jnp.concatenate([mid_re[rows, :], mid_im[rows, :]], axis=0).astype(BF16)
        res = mm(second[step], block)
        put(step, res[:RADIX], res[RADIX:])
        return carry

    lax.fori_loop(0, RADIX, stage_b, 0, unroll=16)


def load_strip(strip, row_win, col_win, loads, re, im):
    row_win, scale = row_win[...].T, col_win[...]
    for block in range(RADIX):
        if block % (RADIX // len(loads)) == 0:
            loads[block * len(loads) // RADIX].wait()
        half = block % 2 * RADIX
        window = row_win[half : half + RADIX, block // 2 : block // 2 + 1] * scale
        rows, src = pl.ds(block * PITCH, RADIX), pl.ds(block * RADIX, RADIX)
        re[rows, :] = strip[0, src, :].astype(F32) * window
        im[rows, :] = strip[1, src, :].astype(F32) * window


def spectrum(re, im, mid_re, mid_im, wide_re, wide_im, first, second):
    def fetch(index):
        rows = strided(index, PITCH)
        return re[rows, :], im[rows, :]

    def put(index, real, imag):
        here, before = strided(WIDE + index, WIDE), strided(RADIX + index, WIDE)
        wide_re[here, :] = real
        wide_im[here, :] = imag
        wide_re[before, :] = real
        wide_im[before, :] = imag

    transform_rows(fetch, mid_re, mid_im, first, second, put)


def cut_rows(which, facet, offs, turn, wide_re, wide_im, out):
    base = offs[which]
    index = (facet * base) & (FACETS - 1)
    cosine, sine = turn[0, index], turn[1, index]
    start = WIDE + base // RADIX * WIDE + base % RADIX
    for part in range(8):
        rows = pl.ds(start + part * WIDE, RADIX)
        real, imag = wide_re[rows, :], wide_im[rows, :]
        blocks = pl.ds(part * 4, 4)
        out[which, blocks, 0] = (cosine * real + sine * imag).astype(BF16).reshape(4, 16, LANES)
        out[which, blocks, 1] = (cosine * imag - sine * real).astype(BF16).reshape(4, 16, LANES)


def backward_kernel(
    offs, turn, row_win, col_win, first, strips_hbm, second_hbm, out_hbm,
    re, im, mid_re, mid_im, wide_re, wide_im, strips, second, out, second_sem, strip_sem, out_sem,
):
    def load(which):
        return pltpu.make_async_copy(strips_hbm.at[which], strips.at[which], strip_sem.at[which])

    for which in range(FACETS):
        load(which).start()
    table = pltpu.make_async_copy(second_hbm, second, second_sem)
    table.start()
    facet = lax.axis_index("facet")
    row_win = row_win[...].T

    def clear(step, carry):
        rows = pl.ds(pl.multiple_of(step * 128, 128), 128)
        wide_re[rows, :] = jnp.zeros((128, LANES), F32)
        wide_im[rows, :] = jnp.zeros((128, LANES), F32)
        return carry

    lax.fori_loop(0, WIDE_ROWS // 128, clear, 0, unroll=2)

    def place(which, carry):
        load(which).wait()
        base = offs[which]
        index = (facet * base) & (FACETS - 1)
        cosine, sine = turn[0, index], turn[1, index]
        start = WIDE + base // RADIX * WIDE + base % RADIX
        for part in range(8):
            rows = pl.ds(start + part * WIDE, RADIX)
            blocks = pl.ds(part * 4, 4)
            real = strips[which, blocks, 0].reshape(RADIX, LANES).astype(F32)
            imag = strips[which, blocks, 1].reshape(RADIX, LANES).astype(F32)
            wide_re[rows, :] = wide_re[rows, :] + (cosine * real - sine * imag)
            wide_im[rows, :] = wide_im[rows, :] - (sine * real + cosine * imag)
        return carry

    lax.fori_loop(0, FACETS, place, 0)
    table.wait()

    def fetch(index):
        here, before = strided(WIDE + index, WIDE), strided(RADIX + index, WIDE)
        return wide_re[here, :] + wide_re[before, :], wide_im[here, :] + wide_im[before, :]

    def put(index, real, imag):
        rows = strided(index, PITCH)
        re[rows, :] = real
        im[rows, :] = imag

    transform_rows(fetch, mid_re, mid_im, first, second, put)
    scale = col_win[...]
    quarter = LONG // 4
    copies = []
    for block in range(RADIX):
        half = block % 2 * RADIX
        window = row_win[half : half + RADIX, block // 2 : block // 2 + 1] * scale
        rows, dst = pl.ds(block * PITCH, RADIX), pl.ds(block * RADIX, RADIX)
        out[0, dst, :] = (re[rows, :] * window).astype(BF16)
        out[1, dst, :] = (im[rows, :] * -window).astype(BF16)
        if block % 16 == 15:
            done = pl.ds(block // 16 * quarter, quarter)
            copies.append(
                pltpu.make_async_copy(out.at[:, done], out_hbm.at[:, done], out_sem.at[block // 16])
            )
            copies[-1].start()
    for copy in copies:
        copy.wait()


def times(pair, cosine, sine):
    return (pair[0] * cosine - pair[1] * sine, pair[0] * sine + pair[1] * cosine)


def times_unit(pair, num, den, sign):
    num = num % den
    if num == 0:
        return pair
    if 4 * num == den:
        return (-sign * pair[1], sign * pair[0])
    if 2 * num == den:
        return (-pair[0], -pair[1])
    angle = 2 * math.pi * num / den
    return times(pair, math.cos(angle), sign * math.sin(angle))


def small_dft(items, sign):
    count = len(items)
    if count == 1:
        return items
    even = small_dft(items[0::2], sign)
    odd = small_dft(items[1::2], sign)
    odd = [times_unit(odd[i], i, count, sign) for i in range(count // 2)]
    low = [(a[0] + b[0], a[1] + b[1]) for a, b in zip(even, odd)]
    high = [(a[0] - b[0], a[1] - b[1]) for a, b in zip(even, odd)]
    return low + high


def dft_over_blocks(get, put, work, sign):
    for lo in range(8):
        items = small_dft([get(lo + 8 * hi) for hi in range(4)], sign)
        for p_lo in range(4):
            value = times_unit(items[p_lo], lo * p_lo, SUBS, sign)
            work[p_lo * 8 + lo, 0] = value[0]
            work[p_lo * 8 + lo, 1] = value[1]
    for p_lo in range(4):
        items = small_dft([(work[p_lo * 8 + lo, 0], work[p_lo * 8 + lo, 1]) for lo in range(8)], sign)
        for p_hi in range(8):
            put(p_lo + 4 * p_hi, items[p_hi])


def columns_to_tiles(blocks, phase, dense, twist, rep, sel, keep, work, folded, tiles):
    def get(s):
        pair = (blocks[s, 0].astype(F32), blocks[s, 1].astype(F32))
        return times(pair, phase[0, s : s + 1, :], -phase[1, s : s + 1, :])

    def put(p, pair):
        pair = times(pair, twist[0, p : p + 1, :], -twist[1, p : p + 1, :])
        rows = slice(p * 16, p * 16 + 16)
        folded[rows, 0:LANES] = pair[0].astype(BF16)
        folded[rows, LANES : 2 * LANES] = pair[1].astype(BF16)

    dft_over_blocks(get, put, work, -1.0)
    flat = mm_nt(dense[...], folded[...]).astype(BF16)
    stacked = jnp.concatenate(
        [
            jnp.concatenate([flat[0:16, 0:256], flat[16:32, 0:256]], axis=1),
            jnp.concatenate([flat[0:16, 256:512], flat[16:32, 256:512]], axis=1),
        ],
        axis=0,
    )
    spread = mm(rep[...], stacked).astype(BF16) * keep[...]
    own = as_bf(iota((512, LANES), 1) // 32 == iota((512, LANES), 0) // TS % CAP)
    tiles[...] = mm(spread, sel[...]).astype(BF16) * own


def tiles_to_columns(tiles, phase, dense, twist, rep_t, sel, keep, work, folded_f32, images):
    spread = mm_nt(tiles[...], sel[...]).astype(BF16) * keep[...]
    stacked = mm(rep_t[...], spread).astype(BF16)
    flat = jnp.concatenate(
        [
            jnp.concatenate([stacked[0:16, 0:256], stacked[16:32, 0:256]], axis=1),
            jnp.concatenate([stacked[0:16, 256:512], stacked[16:32, 256:512]], axis=1),
        ],
        axis=0,
    )
    folded_f32[...] = mm_tn(flat, dense[...])

    def get(p):
        rows = slice(p * 16, p * 16 + 16)
        pair = (folded_f32[rows, 0:LANES], folded_f32[rows, LANES : 2 * LANES])
        return times(pair, twist[0, p : p + 1, :], twist[1, p : p + 1, :])

    def put(s, pair):
        pair = times(pair, phase[0, s : s + 1, :], phase[1, s : s + 1, :])
        images[s, 0] = pair[0].astype(BF16)
        images[s, 1] = pair[1].astype(BF16)

    dft_over_blocks(get, put, work, 1.0)


VALUES = 8


def unit_circle(turns, total):
    half = jnp.where(turns >= total / 2.0, turns - total, turns) * (math.pi / total)
    sq = half * half
    sine = 1.0 / 6227020800.0
    for term in (-1.0 / 39916800.0, 1.0 / 362880.0, -1.0 / 5040.0, 1.0 / 120.0, -1.0 / 6.0, 1.0):
        sine = sine * sq + term
    sine = sine * half
    cosine = 1.0 / 479001600.0
    for term in (-1.0 / 3628800.0, 1.0 / 40320.0, -1.0 / 720.0, 1.0 / 24.0, -0.5, 1.0):
        cosine = cosine * sq + term
    return 1.0 - 2.0 * sine * sine, 2.0 * sine * cosine


def over_pixels(values):
    return jnp.broadcast_to(values[:, None, :], (8, TS, LANES)).reshape(8 * TS, LANES)


def pack_visibilities(measured, masked, pixels, staged, packed):
    for part in range(4):
        rows = pl.ds(part * 32, 32)
        blocks = pl.ds(part * 8, 8)
        values = []
        for z in range(2):
            value = measured[rows, z, :]
            coarse = value.astype(BF16).astype(F32)
            values += [coarse, value - coarse]
        values.append(masked[rows, :])
        values += [pixels[i, rows, :].astype(F32) for i in range(3)]
        for q in range(VALUES):
            staged[blocks, q * CAP : (q + 1) * CAP, :] = values[q].reshape(8, CAP, LANES)
        packed[blocks] = staged[blocks].astype(BF16)


def visit(tiles, vis, my_tiles):
    pixel = (iota((8 * TS, LANES), 0) % TS).astype(F32)
    square = (pixel - 8.0) * (pixel - 8.0)
    own = (iota((64, LANES), 1) // 32 == iota((64, LANES), 0) // TS).astype(F32)

    for step in range(4):
        def value(q):
            return vis[q * SUBS + step * 8 : q * SUBS + step * 8 + 8, :]

        turns = over_pixels(value(7)) * square
        turns = turns - 256.0 * jnp.floor(turns * (1.0 / 256.0))
        cosine, sine = unit_circle(turns, 256.0)
        row_off = (pixel - over_pixels(value(5))) / kernel_width
        col_off = (pixel - over_pixels(value(6))) / kernel_width
        row_fall = kernel_norm * jnp.exp(-(row_off * row_off))
        col_fall = kernel_norm * jnp.exp(-(col_off * col_off))
        row_re, row_im = (row_fall * cosine).astype(BF16), (-row_fall * sine).astype(BF16)
        upper = jnp.concatenate([row_re, row_im], axis=1)
        lower = jnp.concatenate([-row_im, row_re], axis=1)
        weights = []
        for half in range(2):
            pieces = []
            for slot in range(4):
                src = slice(half * 64 + slot * TS, half * 64 + slot * TS + TS)
                pieces += [upper[src], lower[src]]
            weights.append(jnp.concatenate(pieces, axis=0))
        col_re = (col_fall * cosine).astype(BF16).astype(F32)
        col_im = (-col_fall * sine).astype(BF16).astype(F32)
        first = step * 128
        part = jnp.concatenate(
            [mm(tiles[first + half * 64 : first + half * 64 + 64, :], weights[half]) for half in range(2)],
            axis=0,
        )
        part_re, part_im = part[:, 0:LANES], part[:, LANES : 2 * LANES]
        pred_re = jnp.sum((col_re * part_re - col_im * part_im).reshape(8, TS, LANES), axis=1)
        pred_im = jnp.sum((col_re * part_im + col_im * part_re).reshape(8, TS, LANES), axis=1)
        weight = value(4)
        res_re = over_pixels(weight * (value(0) + value(1) - pred_re))
        res_im = over_pixels(weight * (value(2) + value(3) - pred_im))
        back_re = (col_re * res_re + col_im * res_im).astype(BF16)
        back_im = (col_re * res_im - col_im * res_re).astype(BF16)
        back = jnp.concatenate([back_re, back_im], axis=1)
        for half in range(2):
            grid = mm_nt(back[half * 64 : half * 64 + 64], weights[half]) * own
            my_tiles[first + half * 64 : first + half * 64 + 64, :] = grid.astype(BF16)


def as_bf(condition):
    return condition.astype(F32).astype(BF16)


def iota(shape, dim):
    return lax.broadcasted_iota(jnp.int32, shape, dim)


def masked_weights(weight, counts, masked):
    identity = as_bf(iota((LANES, LANES), 0) == iota((LANES, LANES), 1))
    spread = jnp.broadcast_to(counts[...].astype(F32), (LANES, LANES)).astype(BF16)
    column = mm_nt(identity, spread)
    masked[...] = jnp.where(iota((LANES, LANES), 1).astype(F32) < column, weight[...], 0.0)


def column_phase(facet, offsets, phase):
    mine = jnp.where(iota((1, FACETS), 1) == facet, offsets[...], 0)
    start = jnp.sum(mine.astype(F32), axis=1, keepdims=True).astype(jnp.int32)
    column = iota((SUBS, LANES), 0) * LANES + iota((SUBS, LANES), 1)
    turns = ((column * start) & (LONG - 1)).astype(F32)
    cosine, sine = unit_circle(turns, float(LONG))
    phase[0] = cosine
    phase[1] = sine


def routing(owners, choice):
    square = (SUBS, SUBS)
    up, across = iota(square, 0), iota(square, 1)
    named = as_bf(owners[...] == up)
    moved = as_bf(across == up % 2 * 16 + up // 2)
    identity = as_bf(up == across)
    earlier = mm(named, as_bf(up < across)).astype(BF16)
    named = mm(named, moved).astype(BF16)
    rank = jnp.sum(named.astype(F32) * mm(earlier, moved), axis=0, keepdims=True)
    rank = mm_nt(identity, jnp.broadcast_to(rank, (LANES, SUBS)).astype(BF16))
    by_tile = mm_nt(identity, named).astype(BF16)
    wide = (SUBS, SUBS * SUBS)
    by_tile = mm(by_tile, as_bf(iota(wide, 1) // SUBS == iota(wide, 0)))
    at_rank = (rank == (iota((SUBS, LANES), 1) % CAP).astype(F32)).astype(F32)
    both = by_tile * jnp.concatenate([at_rank] * 8, axis=1)
    which = iota(wide, 1) % SUBS // CAP
    for q in range(VALUES):
        choice[q * SUBS : (q + 1) * SUBS, :] = jnp.where(which == q, both, 0.0).astype(BF16)


def add_blocks(dst, sources, lo, count):
    def one(step, carry):
        total = sources[0][lo + step].astype(F32)
        for src in sources[1:]:
            total = total + src[lo + step].astype(F32)
        dst[lo + step] = total.astype(BF16)
        return carry

    lax.fori_loop(0, count, one, 0, unroll=4)


def facet_to_strips_kernel(
    offs, turn, row_win, col_win, first, offsets, owners, measured, weight, pixels, counts,
    dense, twist, rep, rep_t, sel, strip_hbm, second_hbm, keep_hbm,
    out_hbm,
    strip, re, im, mid_re, mid_im, wide_re, wide_im, second, keep, mine,
    pair_buf, sums, carry_a, carry_b, from_dn, from_up, total, gathered,
    work, folded, folded_f32, tiles, my_tiles, images, out,
    masked, phase, staged, packed, received, choice, vis,
    load_sem, out_sem,
    pair_s, pair_r, ring_s, ring_r, send_s, first_r, vis_r, image_r, gath_s, gath_r,
):
    me = lax.axis_index("sub")
    facet = lax.axis_index("facet")
    core, chip = lax.rem(facet, 2), facet // 2
    sib = facet + 1 - 2 * core
    up, dn = lax.rem(facet + 2, FACETS), lax.rem(facet + 6, FACETS)
    opp = lax.rem(facet + 4, FACETS)
    low, high = pl.ds(0, 16), pl.ds(16, 16)

    barrier = pltpu.get_barrier_semaphore()

    def greet(step, carry):
        pl.semaphore_signal(barrier, inc=1, device_id={"sub": lax.rem(me + step, SUBS)}, device_id_type=MESH)
        return carry

    for peer in (sib, up, dn):
        pl.semaphore_signal(barrier, inc=1, device_id={"facet": peer}, device_id_type=MESH)
    lax.fori_loop(1, SUBS, greet, 0)
    quarter = LONG // 4
    loads = [
        pltpu.make_async_copy(
            strip_hbm.at[:, pl.ds(i * quarter, quarter)], strip.at[:, pl.ds(i * quarter, quarter)], load_sem.at[i]
        )
        for i in range(4)
    ]
    second_load = pltpu.make_async_copy(second_hbm, second, load_sem.at[4])
    keep_load = pltpu.make_async_copy(keep_hbm, keep, load_sem.at[5])
    for copy in loads + [second_load, keep_load]:
        copy.start()
    masked_weights(weight, counts, masked)
    pack_visibilities(measured, masked, pixels, staged, packed)
    load_strip(strip, row_win, col_win, loads, re, im)
    second_load.wait()
    spectrum(re, im, mid_re, mid_im, wide_re, wide_im, first, second)
    pl.semaphore_wait(barrier, SUBS + 2)

    def to_facet(src, dst, ssem, rsem, peer):
        return pltpu.make_async_remote_copy(
            src_ref=src, dst_ref=dst, send_sem=ssem, recv_sem=rsem,
            device_id={"facet": peer}, device_id_type=MESH,
        )

    def swap(src_of, dst, kind, rsem):
        def copy_to(peer, slot):
            return pltpu.make_async_remote_copy(
                src_ref=src_of.at[peer], dst_ref=dst.at[slot],
                send_sem=send_s.at[kind, peer], recv_sem=rsem.at[slot],
                device_id={"sub": peer}, device_id_type=MESH,
            )

        def send(step, carry):
            copy_to(lax.rem(me + step, SUBS), me).start()
            return carry

        def receive(step, carry):
            peer = lax.rem(me + SUBS - step, SUBS)
            copy_to(peer, peer).wait_recv()
            return carry

        def drain(step, carry):
            copy_to(lax.rem(me + step, SUBS), me).wait_send()
            return carry

        lax.fori_loop(1, SUBS, send, 0)
        dst[me] = src_of[me]
        return (
            lambda: lax.fori_loop(1, SUBS, receive, 0),
            lambda: lax.fori_loop(1, SUBS, drain, 0),
        )

    receive_vis, drain_vis = swap(packed, received, 1, vis_r)

    pairs = {}
    for hop in (2, 1, 3, 0):
        target = 2 * lax.rem(chip + hop, 4) + 1 - core
        cut_rows(target, facet, offs, turn, wide_re, wide_im, mine)
        pairs[hop] = to_facet(mine.at[target], pair_buf.at[hop], pair_s.at[hop], pair_r.at[hop], sib)
        pairs[hop].start()
    for hop in (2, 1, 3, 0):
        cut_rows(2 * lax.rem(chip + hop, 4) + core, facet, offs, turn, wide_re, wide_im, mine)

    def merge_pair(hop):
        pairs[hop].wait_recv()
        target = 2 * lax.rem(chip + hop, 4) + core
        add_blocks(sums.at[hop], [mine.at[target], pair_buf.at[hop]], 0, SUBS)

    merge_pair(2)
    ring = [
        to_facet(sums.at[2, low], carry_a, ring_s.at[0], ring_r.at[0], up),
        to_facet(sums.at[2, high], carry_b, ring_s.at[1], ring_r.at[1], dn),
        to_facet(sums.at[1, high], from_dn.at[high], ring_s.at[2], ring_r.at[2], up),
        to_facet(sums.at[3, low], from_up.at[low], ring_s.at[3], ring_r.at[3], dn),
        to_facet(sums.at[1, low], from_dn.at[low], ring_s.at[4], ring_r.at[4], up),
        to_facet(sums.at[3, high], from_up.at[high], ring_s.at[5], ring_r.at[5], dn),
    ]
    ring[0].start()
    ring[1].start()
    merge_pair(1)
    ring[2].start()
    merge_pair(3)
    ring[3].start()
    column_phase(facet, offsets, phase)
    routing(owners, choice)
    ring[0].wait_recv()
    add_blocks(sums.at[1, low], [sums.at[1, low], carry_a], 0, 16)
    ring[4].start()
    ring[1].wait_recv()
    add_blocks(sums.at[3, high], [sums.at[3, high], carry_b], 0, 16)
    ring[5].start()
    pairs[0].wait_recv()
    for step in (2, 3, 4, 5):
        ring[step].wait_recv()
    own_target = 2 * chip + core
    add_blocks(total, [mine.at[own_target], pair_buf.at[0], from_dn, from_up], 0, SUBS)

    receive_rows, drain_rows = swap(total, gathered, 0, first_r)
    keep_load.wait()
    receive_vis()
    vis[...] = mm(choice[...], received[...].reshape(SUBS * SUBS, LANES))
    receive_rows()
    columns_to_tiles(gathered, phase, dense, twist, rep, sel, keep, work, folded, tiles)
    visit(tiles, vis, my_tiles)
    tiles_to_columns(my_tiles, phase, dense, twist, rep_t, sel, keep, work, folded_f32, images)
    receive_images, drain_images = swap(images, out.at[facet], 2, image_r)
    receive_images()

    def share(index, src, peer):
        return to_facet(src, src, gath_s.at[index], gath_r.at[index], peer)

    stores = []

    def store(ref_of):
        copy = pltpu.make_async_copy(ref_of(out), ref_of(out_hbm), out_sem.at[len(stores)])
        copy.start()
        stores.append(copy)

    def whole(which):
        return lambda ref: ref.at[which]

    def part(which, rows):
        return lambda ref: ref.at[which, rows]

    own = out.at[facet]
    sends = [share(0, own, up), share(1, own, dn), share(2, own, sib)]
    for copy in sends:
        copy.start()
    store(whole(facet))

    def arrives(index, ref_of):
        share(index, ref_of(out), sib).wait_recv()
        store(ref_of)

    def forward(index, ref, peer):
        sends.append(share(index, ref, peer))
        sends[-1].start()

    share(0, out.at[dn], sib).wait_recv()
    forward(3, out.at[dn, low], up)
    forward(5, out.at[dn], sib)
    store(whole(dn))
    share(1, out.at[up], sib).wait_recv()
    forward(4, out.at[up, high], dn)
    forward(6, out.at[up], sib)
    store(whole(up))
    other = 1 - 2 * core
    arrives(2, whole(sib))
    arrives(5, whole(dn + other))
    arrives(6, whole(up + other))
    share(3, out.at[opp, low], sib).wait_recv()
    forward(7, out.at[opp, low], sib)
    store(part(opp, low))
    share(4, out.at[opp, high], sib).wait_recv()
    forward(8, out.at[opp, high], sib)
    store(part(opp, high))
    arrives(7, part(opp + other, low))
    arrives(8, part(opp + other, high))
    for copy in sends + ring + list(pairs.values()):
        copy.wait_send()
    for drain in (drain_rows, drain_vis, drain_images):
        drain()
    for copy in stores:
        copy.wait()


def vmem_specs(count):
    return [pl.BlockSpec(memory_space=pltpu.VMEM)] * count


def smem_specs(count):
    return [pl.BlockSpec(memory_space=pltpu.SMEM)] * count


BIG = 60 * 1024 * 1024
STRIPS = (FACETS, SUBS, 2, 16, LANES)
WIDE_ROWS = 66 * 128


def any_specs(count):
    return [pl.BlockSpec(memory_space=pl.ANY)] * count


def row_scratch():
    narrow, wide = pltpu.VMEM((RADIX * PITCH, LANES), F32), pltpu.VMEM((WIDE_ROWS, LANES), F32)
    return [narrow] * 4 + [wide] * 2


TABLE = (RADIX, 2 * RADIX, 2 * RADIX)


def backward_call(shape):
    return pl.pallas_call(
        backward_kernel,
        out_shape=jax.ShapeDtypeStruct(shape, BF16),
        in_specs=smem_specs(2) + vmem_specs(3) + any_specs(2),
        out_specs=pl.BlockSpec(memory_space=pl.ANY),
        scratch_shapes=row_scratch()
        + [
            pltpu.VMEM(STRIPS, BF16),
            pltpu.VMEM(TABLE, BF16),
            pltpu.VMEM(shape, BF16),
            pltpu.SemaphoreType.DMA,
            pltpu.SemaphoreType.DMA((FACETS,)),
            pltpu.SemaphoreType.DMA((4,)),
        ],
        compiler_params=pltpu.CompilerParams(vmem_limit_bytes=BIG),
    )


def strips_call(shape):
    block = (SUBS, 2, 16, LANES)
    half = (16, 2, 16, LANES)
    values = (SUBS, VALUES * CAP, LANES)
    vm = pltpu.VMEM
    dma = pltpu.SemaphoreType.DMA
    return pl.pallas_call(
        facet_to_strips_kernel,
        out_shape=jax.ShapeDtypeStruct(STRIPS, BF16),
        in_specs=smem_specs(2) + vmem_specs(14) + any_specs(3),
        out_specs=pl.BlockSpec(memory_space=pl.ANY),
        scratch_shapes=[vm(shape, BF16)]
        + row_scratch()
        + [
            vm(TABLE, BF16), vm((512, 512), BF16), vm(STRIPS, BF16),
            vm((4,) + block, BF16), vm((4,) + block, BF16), vm(half, BF16), vm(half, BF16),
            vm(block, BF16), vm(block, BF16), vm(block, BF16), vm(block, BF16),
            vm(block, F32), vm((512, 256), BF16), vm((512, 256), F32),
            vm((512, LANES), BF16), vm((512, LANES), BF16), vm(block, BF16), vm(STRIPS, BF16),
            vm((LANES, LANES), F32), vm((2, SUBS, LANES), F32),
            vm(values, F32), vm(values, BF16), vm(values, BF16),
            vm((VALUES * SUBS, SUBS * SUBS), BF16), vm((VALUES * SUBS, LANES), F32),
            dma((6,)), dma((10,)),
            dma((4,)), dma((4,)), dma((6,)), dma((6,)), dma((3, SUBS)),
            dma((SUBS,)), dma((SUBS,)), dma((SUBS,)), dma((9,)), dma((9,)),
        ],
        compiler_params=pltpu.CompilerParams(
            vmem_limit_bytes=BIG, collective_id=0, has_side_effects=True
        ),
    )


def per_device(
    facet_strips, row_window, col_window, row_offsets, col_offsets,
    tile_owner, measured, vis_weight, uvw_pixels, vis_count,
):
    first, second = row_tables()
    dense, twist, rep, rep_t, sel, keep = col_tables()
    eighth = 2 * np.pi * np.arange(FACETS) / FACETS
    turn = jnp.asarray(np.stack([np.cos(eighth), np.sin(eighth)]), F32)
    row_win = row_window.reshape(LONG // LANES, LANES)
    col_win = col_window.reshape(1, LANES)
    strips = strips_call(facet_strips.shape)(
        row_offsets, turn, row_win, col_win, first,
        col_offsets.reshape(1, FACETS), tile_owner.reshape(1, SUBS), measured[0, 0],
        vis_weight[0, 0], jnp.transpose(uvw_pixels[0, 0], (1, 0, 2)), vis_count.reshape(1, LANES),
        dense, twist, rep, rep_t, sel, facet_strips, second, keep,
    )
    return backward_call(facet_strips.shape)(
        row_offsets, turn, row_win, col_win, first, strips, second
    )


def solution(mesh):
    in_specs = (
        P(None, "facet", "sub"),
        P(),
        P("sub"),
        P(),
        P(),
        P("sub", "facet", None, None),
        P("facet", "sub", None, None, None),
        P("facet", "sub", None, None),
        P("facet", "sub", None, None, None),
        P("facet", "sub", None),
    )
    return jax.shard_map(
        per_device, mesh=mesh, in_specs=in_specs, out_specs=P(None, "facet", "sub"), check_vma=False
    )
```

```python
import math

import jax
import jax.numpy as jnp
import numpy as np
from jax import lax
from jax.experimental import pallas as pl
from jax.experimental.pallas import tpu as pltpu
from jax.sharding import PartitionSpec as P

SG = 512
RADIX = 64
TS = 16
LONG = 4096
SUBS = 32
FACETS = 8
CAP = 4
LANES = 128
MESH = pl.DeviceIdType.MESH
F32 = jnp.float32
BF16 = jnp.bfloat16

kernel_width = 2.5
kernel_norm = 0.565


def as_real(theta):
    cosine, sine = np.cos(theta), np.sin(theta)
    return np.block([[cosine, sine], [-sine, cosine]])


def row_tables():
    idx = np.arange(RADIX)
    first = as_real(2 * np.pi * (np.outer(idx, idx) % RADIX) / RADIX)
    second = [
        as_real(2 * np.pi * (np.outer(k1 + RADIX * idx, idx) % LONG) / LONG) / RADIX
        for k1 in range(RADIX)
    ]
    return jnp.asarray(first, BF16), jnp.asarray(np.stack(second), BF16)


def col_tables():
    high = np.outer(np.arange(16), np.arange(LANES)) % LANES
    dense = as_real(2 * np.pi * high / LANES)
    low = 2 * np.pi * np.outer(np.arange(SUBS), np.arange(LANES)) / LONG
    twist = np.stack([np.cos(low), np.sin(low)]) / 64.0
    rep = np.zeros((512, 32))
    rep[np.arange(512), np.arange(512) // 16] = 1
    sel = np.zeros((2, 16, 16, 4, 2, 16))
    for z in range(2):
        for r in range(16):
            sel[z, :, r, :, z, r] = 1
    sel = sel.reshape(512, 128)
    keep = (np.arange(512)[:, None] % 16) == (np.arange(512)[None, :] // 16 % 16)
    return (
        jnp.asarray(dense, BF16),
        jnp.asarray(twist, F32),
        jnp.asarray(rep, BF16),
        jnp.asarray(rep.T, BF16),
        jnp.asarray(sel, BF16),
        jnp.asarray(keep, BF16),
    )


def mm(first, other):
    return jnp.dot(first, other, preferred_element_type=F32)


def mm_nt(first, other):
    return lax.dot_general(first, other, (((1,), (1,)), ((), ())), preferred_element_type=F32)


def mm_tn(first, other):
    return lax.dot_general(first, other, (((0,), (0,)), ((), ())), preferred_element_type=F32)


PITCH = RADIX + 1
WIDE = 2 * RADIX + 1


def strided(index, pitch):
    return pl.ds(index, RADIX, stride=pitch)


def transform_rows(fetch, mid_re, mid_im, first, second, put):
    def stage_a(step, carry):
        parts = []
        for u in range(2):
            real, imag = fetch(2 * step + u)
            parts.append(jnp.concatenate([real, imag], axis=0).astype(BF16))
        res = mm(first[...], jnp.concatenate(parts, axis=1))
        for u in range(2):
            rows = strided(2 * step + u, PITCH)
            mid_re[rows, :] = res[:RADIX, u * LANES : (u + 1) * LANES]
            mid_im[rows, :] = res[RADIX:, u * LANES : (u + 1) * LANES]
        return carry

    lax.fori_loop(0, RADIX // 2, stage_a, 0, unroll=8)

    def stage_b(step, carry):
        rows = pl.ds(step * PITCH, RADIX)
        block = jnp.concatenate([mid_re[rows, :], mid_im[rows, :]], axis=0).astype(BF16)
        res = mm(second[step], block)
        put(step, res[:RADIX], res[RADIX:])
        return carry

    lax.fori_loop(0, RADIX, stage_b, 0, unroll=16)


def load_strip(strip, row_win, col_win, loads, re, im):
    row_win, scale = row_win[...].T, col_win[...]
    for block in range(RADIX):
        if block % (RADIX // len(loads)) == 0:
            loads[block * len(loads) // RADIX].wait()
        half = block % 2 * RADIX
        window = row_win[half : half + RADIX, block // 2 : block // 2 + 1] * scale
        rows, src = pl.ds(block * PITCH, RADIX), pl.ds(block * RADIX, RADIX)
        re[rows, :] = strip[0, src, :].astype(F32) * window
        im[rows, :] = strip[1, src, :].astype(F32) * window


def spectrum(re, im, mid_re, mid_im, wide_re, wide_im, first, second):
    def fetch(index):
        rows = strided(index, PITCH)
        return re[rows, :], im[rows, :]

    def put(index, real, imag):
        here, before = strided(WIDE + index, WIDE), strided(RADIX + index, WIDE)
        wide_re[here, :] = real
        wide_im[here, :] = imag
        wide_re[before, :] = real
        wide_im[before, :] = imag

    transform_rows(fetch, mid_re, mid_im, first, second, put)


def cut_rows(which, facet, offs, turn, wide_re, wide_im, out):
    base = offs[which]
    index = (facet * base) & (FACETS - 1)
    cosine, sine = turn[0, index], turn[1, index]
    start = WIDE + base // RADIX * WIDE + base % RADIX
    for part in range(8):
        rows = pl.ds(start + part * WIDE, RADIX)
        real, imag = wide_re[rows, :], wide_im[rows, :]
        blocks = pl.ds(part * 4, 4)
        out[which, 0, blocks] = (cosine * real + sine * imag).astype(BF16).reshape(4, 16, LANES)
        out[which, 1, blocks] = (cosine * imag - sine * real).astype(BF16).reshape(4, 16, LANES)


def backward_kernel(
    offs, turn, row_win, col_win, first, strips_hbm, second_hbm, out_hbm,
    re, im, mid_re, mid_im, wide_re, wide_im, strips, second, out, second_sem, strip_sem, out_sem,
):
    def load(which):
        return pltpu.make_async_copy(strips_hbm.at[which], strips.at[which], strip_sem.at[which])

    for which in range(FACETS):
        load(which).start()
    table = pltpu.make_async_copy(second_hbm, second, second_sem)
    table.start()
    facet = lax.axis_index("facet")
    row_win = row_win[...].T

    def clear(step, carry):
        rows = pl.ds(pl.multiple_of(step * 128, 128), 128)
        wide_re[rows, :] = jnp.zeros((128, LANES), F32)
        wide_im[rows, :] = jnp.zeros((128, LANES), F32)
        return carry

    lax.fori_loop(0, WIDE_ROWS // 128, clear, 0, unroll=2)

    def place(which, carry):
        load(which).wait()
        base = offs[which]
        index = (facet * base) & (FACETS - 1)
        cosine, sine = turn[0, index], turn[1, index]
        start = WIDE + base // RADIX * WIDE + base % RADIX
        for part in range(8):
            rows = pl.ds(start + part * WIDE, RADIX)
            blocks = pl.ds(part * 4, 4)
            real = strips[which, 0, blocks].reshape(RADIX, LANES).astype(F32)
            imag = strips[which, 1, blocks].reshape(RADIX, LANES).astype(F32)
            wide_re[rows, :] = wide_re[rows, :] + (cosine * real - sine * imag)
            wide_im[rows, :] = wide_im[rows, :] - (sine * real + cosine * imag)
        return carry

    lax.fori_loop(0, FACETS, place, 0)
    table.wait()

    def fetch(index):
        here, before = strided(WIDE + index, WIDE), strided(RADIX + index, WIDE)
        return wide_re[here, :] + wide_re[before, :], wide_im[here, :] + wide_im[before, :]

    def put(index, real, imag):
        rows = strided(index, PITCH)
        re[rows, :] = real
        im[rows, :] = imag

    transform_rows(fetch, mid_re, mid_im, first, second, put)
    scale = col_win[...]
    quarter = LONG // 4
    copies = []
    for block in range(RADIX):
        half = block % 2 * RADIX
        window = row_win[half : half + RADIX, block // 2 : block // 2 + 1] * scale
        rows, dst = pl.ds(block * PITCH, RADIX), pl.ds(block * RADIX, RADIX)
        out[0, dst, :] = (re[rows, :] * window).astype(BF16)
        out[1, dst, :] = (im[rows, :] * -window).astype(BF16)
        if block % 16 == 15:
            done = pl.ds(block // 16 * quarter, quarter)
            copies.append(
                pltpu.make_async_copy(out.at[:, done], out_hbm.at[:, done], out_sem.at[block // 16])
            )
            copies[-1].start()
    for copy in copies:
        copy.wait()


def times(pair, cosine, sine):
    return (pair[0] * cosine - pair[1] * sine, pair[0] * sine + pair[1] * cosine)


def times_unit(pair, num, den, sign):
    num = num % den
    if num == 0:
        return pair
    if 4 * num == den:
        return (-sign * pair[1], sign * pair[0])
    if 2 * num == den:
        return (-pair[0], -pair[1])
    angle = 2 * math.pi * num / den
    return times(pair, math.cos(angle), sign * math.sin(angle))


def small_dft(items, sign):
    count = len(items)
    if count == 1:
        return items
    even = small_dft(items[0::2], sign)
    odd = small_dft(items[1::2], sign)
    odd = [times_unit(odd[i], i, count, sign) for i in range(count // 2)]
    low = [(a[0] + b[0], a[1] + b[1]) for a, b in zip(even, odd)]
    high = [(a[0] - b[0], a[1] - b[1]) for a, b in zip(even, odd)]
    return low + high


def dft_over_blocks(get, put, work, sign):
    for lo in range(8):
        items = small_dft([get(lo + 8 * hi) for hi in range(4)], sign)
        for p_lo in range(4):
            value = times_unit(items[p_lo], lo * p_lo, SUBS, sign)
            work[p_lo * 8 + lo, 0] = value[0]
            work[p_lo * 8 + lo, 1] = value[1]
    for p_lo in range(4):
        items = small_dft([(work[p_lo * 8 + lo, 0], work[p_lo * 8 + lo, 1]) for lo in range(8)], sign)
        for p_hi in range(8):
            put(p_lo + 4 * p_hi, items[p_hi])


def columns_to_tiles(blocks, phase, dense, twist, rep, sel, keep, work, folded, tiles):
    def get(s):
        pair = (blocks[0, s].astype(F32), blocks[1, s].astype(F32))
        return times(pair, phase[0, s : s + 1, :], -phase[1, s : s + 1, :])

    def put(p, pair):
        pair = times(pair, twist[0, p : p + 1, :], -twist[1, p : p + 1, :])
        rows = slice(p * 16, p * 16 + 16)
        folded[rows, 0:LANES] = pair[0].astype(BF16)
        folded[rows, LANES : 2 * LANES] = pair[1].astype(BF16)

    dft_over_blocks(get, put, work, -1.0)
    flat = mm_nt(dense[...], folded[...]).astype(BF16)
    stacked = jnp.concatenate(
        [
            jnp.concatenate([flat[0:16, 0:256], flat[16:32, 0:256]], axis=1),
            jnp.concatenate([flat[0:16, 256:512], flat[16:32, 256:512]], axis=1),
        ],
        axis=0,
    )
    spread = mm(rep[...], stacked).astype(BF16) * keep[...]
    own = as_bf(iota((512, LANES), 1) // 32 == iota((512, LANES), 0) // TS % CAP)
    tiles[...] = mm(spread, sel[...]).astype(BF16) * own


def tiles_to_columns(tiles, phase, dense, twist, rep_t, sel, keep, work, folded_f32, images):
    spread = mm_nt(tiles[...], sel[...]).astype(BF16) * keep[...]
    stacked = mm(rep_t[...], spread).astype(BF16)
    flat = jnp.concatenate(
        [
            jnp.concatenate([stacked[0:16, 0:256], stacked[16:32, 0:256]], axis=1),
            jnp.concatenate([stacked[0:16, 256:512], stacked[16:32, 256:512]], axis=1),
        ],
        axis=0,
    )
    folded_f32[...] = mm_tn(flat, dense[...])

    def get(p):
        rows = slice(p * 16, p * 16 + 16)
        pair = (folded_f32[rows, 0:LANES], folded_f32[rows, LANES : 2 * LANES])
        return times(pair, twist[0, p : p + 1, :], twist[1, p : p + 1, :])

    def put(s, pair):
        pair = times(pair, phase[0, s : s + 1, :], phase[1, s : s + 1, :])
        images[0, s] = pair[0].astype(BF16)
        images[1, s] = pair[1].astype(BF16)

    dft_over_blocks(get, put, work, 1.0)


VALUES = 8


def unit_circle(turns, total):
    half = jnp.where(turns >= total / 2.0, turns - total, turns) * (math.pi / total)
    sq = half * half
    sine = 1.0 / 6227020800.0
    for term in (-1.0 / 39916800.0, 1.0 / 362880.0, -1.0 / 5040.0, 1.0 / 120.0, -1.0 / 6.0, 1.0):
        sine = sine * sq + term
    sine = sine * half
    cosine = 1.0 / 479001600.0
    for term in (-1.0 / 3628800.0, 1.0 / 40320.0, -1.0 / 720.0, 1.0 / 24.0, -0.5, 1.0):
        cosine = cosine * sq + term
    return 1.0 - 2.0 * sine * sine, 2.0 * sine * cosine


def over_pixels(values):
    return jnp.broadcast_to(values[:, None, :], (8, TS, LANES)).reshape(8 * TS, LANES)


def pack_visibilities(measured, masked, pixels, staged, packed):
    for part in range(4):
        rows = pl.ds(part * 32, 32)
        blocks = pl.ds(part * 8, 8)
        values = []
        for z in range(2):
            value = measured[rows, z, :]
            coarse = value.astype(BF16).astype(F32)
            values += [coarse, value - coarse]
        values.append(masked[rows, :])
        values += [pixels[i, rows, :].astype(F32) for i in range(3)]
        for q in range(VALUES):
            staged[blocks, q * CAP : (q + 1) * CAP, :] = values[q].reshape(8, CAP, LANES)
        packed[blocks] = staged[blocks].astype(BF16)


def visit(tiles, vis, my_tiles):
    pixel = (iota((8 * TS, LANES), 0) % TS).astype(F32)
    square = (pixel - 8.0) * (pixel - 8.0)
    own = (iota((64, LANES), 1) // 32 == iota((64, LANES), 0) // TS).astype(F32)

    for step in range(4):
        def value(q):
            return vis[q * SUBS + step * 8 : q * SUBS + step * 8 + 8, :]

        turns = over_pixels(value(7)) * square
        turns = turns - 256.0 * jnp.floor(turns * (1.0 / 256.0))
        cosine, sine = unit_circle(turns, 256.0)
        row_off = (pixel - over_pixels(value(5))) / kernel_width
        col_off = (pixel - over_pixels(value(6))) / kernel_width
        row_fall = kernel_norm * jnp.exp(-(row_off * row_off))
        col_fall = kernel_norm * jnp.exp(-(col_off * col_off))
        row_re, row_im = (row_fall * cosine).astype(BF16), (-row_fall * sine).astype(BF16)
        upper = jnp.concatenate([row_re, row_im], axis=1)
        lower = jnp.concatenate([-row_im, row_re], axis=1)
        weights = []
        for half in range(2):
            pieces = []
            for slot in range(4):
                src = slice(half * 64 + slot * TS, half * 64 + slot * TS + TS)
                pieces += [upper[src], lower[src]]
            weights.append(jnp.concatenate(pieces, axis=0))
        col_re = (col_fall * cosine).astype(BF16).astype(F32)
        col_im = (-col_fall * sine).astype(BF16).astype(F32)
        first = step * 128
        part = jnp.concatenate(
            [mm(tiles[first + half * 64 : first + half * 64 + 64, :], weights[half]) for half in range(2)],
            axis=0,
        )
        part_re, part_im = part[:, 0:LANES], part[:, LANES : 2 * LANES]
        pred_re = jnp.sum((col_re * part_re - col_im * part_im).reshape(8, TS, LANES), axis=1)
        pred_im = jnp.sum((col_re * part_im + col_im * part_re).reshape(8, TS, LANES), axis=1)
        weight = value(4)
        res_re = over_pixels(weight * (value(0) + value(1) - pred_re))
        res_im = over_pixels(weight * (value(2) + value(3) - pred_im))
        back_re = (col_re * res_re + col_im * res_im).astype(BF16)
        back_im = (col_re * res_im - col_im * res_re).astype(BF16)
        back = jnp.concatenate([back_re, back_im], axis=1)
        for half in range(2):
            grid = mm_nt(back[half * 64 : half * 64 + 64], weights[half]) * own
            my_tiles[first + half * 64 : first + half * 64 + 64, :] = grid.astype(BF16)


def as_bf(condition):
    return condition.astype(F32).astype(BF16)


def iota(shape, dim):
    return lax.broadcasted_iota(jnp.int32, shape, dim)


def masked_weights(weight, counts, masked):
    identity = as_bf(iota((LANES, LANES), 0) == iota((LANES, LANES), 1))
    spread = jnp.broadcast_to(counts[...].astype(F32), (LANES, LANES)).astype(BF16)
    column = mm_nt(identity, spread)
    masked[...] = jnp.where(iota((LANES, LANES), 1).astype(F32) < column, weight[...], 0.0)


def column_phase(facet, offsets, phase):
    mine = jnp.where(iota((1, FACETS), 1) == facet, offsets[...], 0)
    start = jnp.sum(mine.astype(F32), axis=1, keepdims=True).astype(jnp.int32)
    column = iota((SUBS, LANES), 0) * LANES + iota((SUBS, LANES), 1)
    turns = ((column * start) & (LONG - 1)).astype(F32)
    cosine, sine = unit_circle(turns, float(LONG))
    phase[0] = cosine
    phase[1] = sine


def routing(owners, choice):
    square = (SUBS, SUBS)
    up, across = iota(square, 0), iota(square, 1)
    named = as_bf(owners[...] == up)
    moved = as_bf(across == up % 2 * 16 + up // 2)
    identity = as_bf(up == across)
    earlier = mm(named, as_bf(up < across)).astype(BF16)
    named = mm(named, moved).astype(BF16)
    rank = jnp.sum(named.astype(F32) * mm(earlier, moved), axis=0, keepdims=True)
    rank = mm_nt(identity, jnp.broadcast_to(rank, (LANES, SUBS)).astype(BF16))
    by_tile = mm_nt(identity, named).astype(BF16)
    wide = (SUBS, SUBS * SUBS)
    by_tile = mm(by_tile, as_bf(iota(wide, 1) // SUBS == iota(wide, 0)))
    at_rank = (rank == (iota((SUBS, LANES), 1) % CAP).astype(F32)).astype(F32)
    both = by_tile * jnp.concatenate([at_rank] * 8, axis=1)
    which = iota(wide, 1) % SUBS // CAP
    for q in range(VALUES):
        choice[q * SUBS : (q + 1) * SUBS, :] = jnp.where(which == q, both, 0.0).astype(BF16)


def add_blocks(dst, sources, lo, count):
    def one(step, carry):
        total = sources[0][lo + step].astype(F32)
        for src in sources[1:]:
            total = total + src[lo + step].astype(F32)
        dst[lo + step] = total.astype(BF16)
        return carry

    lax.fori_loop(0, count, one, 0, unroll=4)


def facet_to_strips_kernel(
    offs, turn, row_win, col_win, first, offsets, owners, measured, weight, pixels, counts,
    dense, twist, rep, rep_t, sel, strip_hbm, second_hbm, keep_hbm,
    out_hbm,
    strip, re, im, mid_re, mid_im, wide_re, wide_im, second, keep, mine,
    pair_buf, sums, carry_a, carry_b, from_dn, from_up, total, gathered,
    work, folded, folded_f32, tiles, my_tiles, images, out,
    masked, phase, staged, packed, received, choice, vis,
    load_sem, out_sem,
    pair_s, pair_r, ring_s, ring_r, send_s, rows_r, vis_r, image_r, gath_s, gath_r,
):
    me = lax.axis_index("sub")
    facet = lax.axis_index("facet")
    core, chip = lax.rem(facet, 2), facet // 2
    sib = facet + 1 - 2 * core
    up, dn = lax.rem(facet + 2, FACETS), lax.rem(facet + 6, FACETS)
    opp = lax.rem(facet + 4, FACETS)
    low, high = pl.ds(0, 16), pl.ds(16, 16)

    barrier = pltpu.get_barrier_semaphore()

    def greet(step, carry):
        pl.semaphore_signal(barrier, inc=1, device_id={"sub": lax.rem(me + step, SUBS)}, device_id_type=MESH)
        return carry

    for peer in (sib, up, dn):
        pl.semaphore_signal(barrier, inc=1, device_id={"facet": peer}, device_id_type=MESH)
    lax.fori_loop(1, SUBS, greet, 0)
    quarter = LONG // 4
    loads = [
        pltpu.make_async_copy(
            strip_hbm.at[:, pl.ds(i * quarter, quarter)], strip.at[:, pl.ds(i * quarter, quarter)], load_sem.at[i]
        )
        for i in range(4)
    ]
    second_load = pltpu.make_async_copy(second_hbm, second, load_sem.at[4])
    keep_load = pltpu.make_async_copy(keep_hbm, keep, load_sem.at[5])
    for copy in loads + [second_load, keep_load]:
        copy.start()
    masked_weights(weight, counts, masked)
    pack_visibilities(measured, masked, pixels, staged, packed)
    load_strip(strip, row_win, col_win, loads, re, im)
    second_load.wait()
    spectrum(re, im, mid_re, mid_im, wide_re, wide_im, first, second)
    pl.semaphore_wait(barrier, SUBS + 2)

    def to_facet(src, dst, ssem, rsem, peer):
        return pltpu.make_async_remote_copy(
            src_ref=src, dst_ref=dst, send_sem=ssem, recv_sem=rsem,
            device_id={"facet": peer}, device_id_type=MESH,
        )

    def swap(src_of, dst, kind, rsem):
        def copy_to(peer, slot):
            return pltpu.make_async_remote_copy(
                src_ref=src_of.at[peer], dst_ref=dst.at[slot],
                send_sem=send_s.at[kind, peer], recv_sem=rsem.at[slot],
                device_id={"sub": peer}, device_id_type=MESH,
            )

        def send(step, carry):
            copy_to(lax.rem(me + step, SUBS), me).start()
            return carry

        def receive(step, carry):
            peer = lax.rem(me + SUBS - step, SUBS)
            copy_to(peer, peer).wait_recv()
            return carry

        def drain(step, carry):
            copy_to(lax.rem(me + step, SUBS), me).wait_send()
            return carry

        lax.fori_loop(1, SUBS, send, 0)
        dst[me] = src_of[me]
        return (
            lambda: lax.fori_loop(1, SUBS, receive, 0),
            lambda: lax.fori_loop(1, SUBS, drain, 0),
        )

    pairs = {}
    for plane in range(2):
        for hop in (2, 1, 3, 0):
            target = 2 * lax.rem(chip + hop, 4) + 1 - core
            if plane == 0:
                cut_rows(target, facet, offs, turn, wide_re, wide_im, mine)
            pairs[plane, hop] = to_facet(
                mine.at[target, plane], pair_buf.at[hop, plane],
                pair_s.at[plane, hop], pair_r.at[plane, hop], sib,
            )
            pairs[plane, hop].start()

    def merge_pair(plane, hop):
        pairs[plane, hop].wait_recv()
        target = 2 * lax.rem(chip + hop, 4) + core
        add_blocks(sums.at[hop, plane], [mine.at[target, plane], pair_buf.at[hop, plane]], 0, SUBS)

    rings = [
        [
            to_facet(src, dst, ring_s.at[plane, i], ring_r.at[plane, i], peer)
            for i, (src, dst, peer) in enumerate((
                (sums.at[2, plane, low], carry_a.at[plane], up),
                (sums.at[2, plane, high], carry_b.at[plane], dn),
                (sums.at[1, plane, high], from_dn.at[plane, high], up),
                (sums.at[3, plane, low], from_up.at[plane, low], dn),
                (sums.at[1, plane, low], from_dn.at[plane, low], up),
                (sums.at[3, plane, high], from_up.at[plane, high], dn),
            ))
        ]
        for plane in range(2)
    ]

    def merge_ring(plane):
        ring = rings[plane]
        ring[0].wait_recv()
        add_blocks(sums.at[1, plane, low], [sums.at[1, plane, low], carry_a.at[plane]], 0, 16)
        ring[4].start()
        ring[1].wait_recv()
        add_blocks(sums.at[3, plane, high], [sums.at[3, plane, high], carry_b.at[plane]], 0, 16)
        ring[5].start()

    def finish(plane):
        pairs[plane, 0].wait_recv()
        for step in (3, 4, 2, 5):
            rings[plane][step].wait_recv()
        own_target = 2 * chip + core
        add_blocks(
            total.at[plane],
            [mine.at[own_target, plane], pair_buf.at[0, plane], from_dn.at[plane], from_up.at[plane]],
            0, SUBS,
        )

    cut_rows(2 * lax.rem(chip + 2, 4) + core, facet, offs, turn, wide_re, wide_im, mine)
    merge_pair(0, 2)
    rings[0][0].start()
    rings[0][1].start()
    cut_rows(2 * lax.rem(chip + 1, 4) + core, facet, offs, turn, wide_re, wide_im, mine)
    merge_pair(0, 1)
    rings[0][2].start()
    cut_rows(2 * lax.rem(chip + 3, 4) + core, facet, offs, turn, wide_re, wide_im, mine)
    merge_pair(0, 3)
    rings[0][3].start()
    receive_vis, drain_vis = swap(packed, received, 2, vis_r)
    merge_pair(1, 2)
    rings[1][0].start()
    rings[1][1].start()
    cut_rows(2 * chip + core, facet, offs, turn, wide_re, wide_im, mine)
    merge_pair(1, 1)
    merge_pair(1, 3)
    column_phase(facet, offsets, phase)
    merge_ring(0)
    rings[1][2].start()
    rings[1][3].start()
    routing(owners, choice)
    merge_ring(1)
    finish(0)
    receive_re, drain_re = swap(total.at[0], gathered.at[0], 0, rows_r.at[0])
    finish(1)
    receive_im, drain_im = swap(total.at[1], gathered.at[1], 1, rows_r.at[1])
    keep_load.wait()
    receive_vis()
    vis[...] = mm(choice[...], received[...].reshape(SUBS * SUBS, LANES))
    receive_re()
    receive_im()
    columns_to_tiles(gathered, phase, dense, twist, rep, sel, keep, work, folded, tiles)
    visit(tiles, vis, my_tiles)
    tiles_to_columns(my_tiles, phase, dense, twist, rep_t, sel, keep, work, folded_f32, images)

    swaps = [swap(images.at[plane], out.at[facet, plane], 3 + plane, image_r.at[plane]) for plane in range(2)]
    stores = []
    sends = []

    def store(where):
        copy = pltpu.make_async_copy(out.at[where], out_hbm.at[where], out_sem.at[len(stores)])
        copy.start()
        stores.append(copy)

    def share(plane, index, where, peer):
        ref = out.at[where]
        return to_facet(ref, ref, gath_s.at[plane, index], gath_r.at[plane, index], peer)

    def send(plane, index, where, peer):
        sends.append(share(plane, index, where, peer))
        sends[-1].start()

    def arrives(plane, index, where):
        share(plane, index, where, sib).wait_recv()

    other = 1 - 2 * core
    for plane in range(2):
        swaps[plane][0]()
        own = (facet, plane)
        send(plane, 0, own, up)
        send(plane, 1, own, dn)
        send(plane, 2, own, sib)
        store(own)
    for plane in range(2):
        arrives(plane, 0, (dn, plane))
        send(plane, 3, (dn, plane, low), up)
        send(plane, 5, (dn, plane), sib)
        store((dn, plane))
        arrives(plane, 1, (up, plane))
        send(plane, 4, (up, plane, high), dn)
        send(plane, 6, (up, plane), sib)
        store((up, plane))
    for plane in range(2):
        arrives(plane, 2, (sib, plane))
        store((sib, plane))
        arrives(plane, 5, (dn + other, plane))
        store((dn + other, plane))
        arrives(plane, 6, (up + other, plane))
        store((up + other, plane))
    for plane in range(2):
        arrives(plane, 3, (opp, plane, low))
        send(plane, 7, (opp, plane, low), sib)
        store((opp, plane, low))
        arrives(plane, 4, (opp, plane, high))
        send(plane, 8, (opp, plane, high), sib)
        store((opp, plane, high))
    for plane in range(2):
        arrives(plane, 7, (opp + other, plane, low))
        store((opp + other, plane, low))
        arrives(plane, 8, (opp + other, plane, high))
        store((opp + other, plane, high))
    for copy in sends + rings[0] + rings[1] + list(pairs.values()):
        copy.wait_send()
    for drain in (drain_re, drain_im, drain_vis, swaps[0][1], swaps[1][1]):
        drain()
    for copy in stores:
        copy.wait()


def vmem_specs(count):
    return [pl.BlockSpec(memory_space=pltpu.VMEM)] * count


def smem_specs(count):
    return [pl.BlockSpec(memory_space=pltpu.SMEM)] * count


BIG = 60 * 1024 * 1024
STRIPS = (FACETS, 2, SUBS, 16, LANES)
WIDE_ROWS = 66 * 128


def any_specs(count):
    return [pl.BlockSpec(memory_space=pl.ANY)] * count


def row_scratch():
    narrow, wide = pltpu.VMEM((RADIX * PITCH, LANES), F32), pltpu.VMEM((WIDE_ROWS, LANES), F32)
    return [narrow] * 4 + [wide] * 2


TABLE = (RADIX, 2 * RADIX, 2 * RADIX)


def backward_call(shape):
    return pl.pallas_call(
        backward_kernel,
        out_shape=jax.ShapeDtypeStruct(shape, BF16),
        in_specs=smem_specs(2) + vmem_specs(3) + any_specs(2),
        out_specs=pl.BlockSpec(memory_space=pl.ANY),
        scratch_shapes=row_scratch()
        + [
            pltpu.VMEM(STRIPS, BF16),
            pltpu.VMEM(TABLE, BF16),
            pltpu.VMEM(shape, BF16),
            pltpu.SemaphoreType.DMA,
            pltpu.SemaphoreType.DMA((FACETS,)),
            pltpu.SemaphoreType.DMA((4,)),
        ],
        compiler_params=pltpu.CompilerParams(vmem_limit_bytes=BIG),
    )


def strips_call(shape):
    block = (2, SUBS, 16, LANES)
    half = (2, 16, 16, LANES)
    values = (SUBS, VALUES * CAP, LANES)
    vm = pltpu.VMEM
    dma = pltpu.SemaphoreType.DMA
    return pl.pallas_call(
        facet_to_strips_kernel,
        out_shape=jax.ShapeDtypeStruct(STRIPS, BF16),
        in_specs=smem_specs(2) + vmem_specs(14) + any_specs(3),
        out_specs=pl.BlockSpec(memory_space=pl.ANY),
        scratch_shapes=[vm(shape, BF16)]
        + row_scratch()
        + [
            vm(TABLE, BF16), vm((512, 512), BF16), vm(STRIPS, BF16),
            vm((4,) + block, BF16), vm((4,) + block, BF16), vm(half, BF16), vm(half, BF16),
            vm(block, BF16), vm(block, BF16), vm(block, BF16), vm(block, BF16),
            vm((SUBS, 2, 16, LANES), F32), vm((512, 256), BF16), vm((512, 256), F32),
            vm((512, LANES), BF16), vm((512, LANES), BF16), vm(block, BF16), vm(STRIPS, BF16),
            vm((LANES, LANES), F32), vm((2, SUBS, LANES), F32),
            vm(values, F32), vm(values, BF16), vm(values, BF16),
            vm((VALUES * SUBS, SUBS * SUBS), BF16), vm((VALUES * SUBS, LANES), F32),
            dma((6,)), dma((20,)),
            dma((2, 4)), dma((2, 4)), dma((2, 6)), dma((2, 6)), dma((5, SUBS)),
            dma((2, SUBS)), dma((SUBS,)), dma((2, SUBS)), dma((2, 9)), dma((2, 9)),
        ],
        compiler_params=pltpu.CompilerParams(
            vmem_limit_bytes=BIG, collective_id=0, has_side_effects=True
        ),
    )


def per_device(
    facet_strips, row_window, col_window, row_offsets, col_offsets,
    tile_owner, measured, vis_weight, uvw_pixels, vis_count,
):
    first, second = row_tables()
    dense, twist, rep, rep_t, sel, keep = col_tables()
    eighth = 2 * np.pi * np.arange(FACETS) / FACETS
    turn = jnp.asarray(np.stack([np.cos(eighth), np.sin(eighth)]), F32)
    row_win = row_window.reshape(LONG // LANES, LANES)
    col_win = col_window.reshape(1, LANES)
    strips = strips_call(facet_strips.shape)(
        row_offsets, turn, row_win, col_win, first,
        col_offsets.reshape(1, FACETS), tile_owner.reshape(1, SUBS), measured[0, 0],
        vis_weight[0, 0], jnp.transpose(uvw_pixels[0, 0], (1, 0, 2)), vis_count.reshape(1, LANES),
        dense, twist, rep, rep_t, sel, facet_strips, second, keep,
    )
    return backward_call(facet_strips.shape)(
        row_offsets, turn, row_win, col_win, first, strips, second
    )


def solution(mesh):
    in_specs = (
        P(None, "facet", "sub"),
        P(),
        P("sub"),
        P(),
        P(),
        P("sub", "facet", None, None),
        P("facet", "sub", None, None, None),
        P("facet", "sub", None, None),
        P("facet", "sub", None, None, None),
        P("facet", "sub", None),
    )
    return jax.shard_map(
        per_device, mesh=mesh, in_specs=in_specs, out_specs=P(None, "facet", "sub"), check_vma=False
    )
```

```python
import math

import jax
import jax.numpy as jnp
import numpy as np
from jax import lax
from jax.experimental import pallas as pl
from jax.experimental.pallas import tpu as pltpu
from jax.sharding import PartitionSpec as P

SG = 512
RADIX = 64
TS = 16
LONG = 4096
SUBS = 32
FACETS = 8
CAP = 4
LANES = 128
MESH = pl.DeviceIdType.MESH
F32 = jnp.float32
BF16 = jnp.bfloat16

kernel_width = 2.5
kernel_norm = 0.565


def as_real(theta):
    cosine, sine = np.cos(theta), np.sin(theta)
    return np.block([[cosine, sine], [-sine, cosine]])


def row_tables():
    idx = np.arange(RADIX)
    first = as_real(2 * np.pi * (np.outer(idx, idx) % RADIX) / RADIX)
    second = [
        as_real(2 * np.pi * (np.outer(k1 + RADIX * idx, idx) % LONG) / LONG) / RADIX
        for k1 in range(RADIX)
    ]
    return jnp.asarray(first, BF16), jnp.asarray(np.stack(second), BF16)


def col_tables():
    high = np.outer(np.arange(16), np.arange(LANES)) % LANES
    dense = as_real(2 * np.pi * high / LANES)
    low = 2 * np.pi * np.outer(np.arange(SUBS), np.arange(LANES)) / LONG
    twist = np.stack([np.cos(low), np.sin(low)]) / 64.0
    rep = np.zeros((512, 32))
    rep[np.arange(512), np.arange(512) // 16] = 1
    sel = np.zeros((2, 16, 16, 4, 2, 16))
    for z in range(2):
        for r in range(16):
            sel[z, :, r, :, z, r] = 1
    sel = sel.reshape(512, 128)
    return (
        jnp.asarray(dense, BF16),
        jnp.asarray(twist, F32),
        jnp.asarray(rep, BF16),
        jnp.asarray(rep.T, BF16),
        jnp.asarray(sel, BF16),
    )


def mm(first, other):
    return jnp.dot(first, other, preferred_element_type=F32)


def mm_nt(first, other):
    return lax.dot_general(first, other, (((1,), (1,)), ((), ())), preferred_element_type=F32)


def mm_tn(first, other):
    return lax.dot_general(first, other, (((0,), (0,)), ((), ())), preferred_element_type=F32)


PITCH = RADIX + 1
WIDE = 2 * RADIX + 1


def strided(index, pitch):
    return pl.ds(index, RADIX, stride=pitch)


def transform_rows(fetch, mid_re, mid_im, first, second, put):
    def stage_a(step, carry):
        parts = []
        for u in range(2):
            real, imag = fetch(2 * step + u)
            parts.append(jnp.concatenate([real, imag], axis=0).astype(BF16))
        res = mm(first[...], jnp.concatenate(parts, axis=1))
        for u in range(2):
            rows = strided(2 * step + u, PITCH)
            mid_re[rows, :] = res[:RADIX, u * LANES : (u + 1) * LANES]
            mid_im[rows, :] = res[RADIX:, u * LANES : (u + 1) * LANES]
        return carry

    lax.fori_loop(0, RADIX // 2, stage_a, 0, unroll=16)

    def stage_b(step, carry):
        rows = pl.ds(step * PITCH, RADIX)
        block = jnp.concatenate([mid_re[rows, :], mid_im[rows, :]], axis=0).astype(BF16)
        res = mm(second[step], block)
        put(step, res[:RADIX], res[RADIX:])
        return carry

    lax.fori_loop(0, RADIX, stage_b, 0, unroll=32)


SMALL = (
    ((FACETS,), jnp.int32), ((2, FACETS), F32), ((SUBS, LANES), F32), ((1, LANES), F32),
    ((LANES, LANES), BF16), ((1, FACETS), jnp.int32), ((1, SUBS), jnp.int32),
    ((LANES, 2, LANES), F32), ((LANES, LANES), F32), ((3, LANES, LANES), jnp.int32), ((1, LANES), jnp.int32),
    ((SUBS, 2 * LANES), BF16), ((2, SUBS, LANES), F32), ((512, SUBS), BF16), ((SUBS, 512), BF16),
    ((512, LANES), BF16),
)


def load_strip(strip, row_win, col_win, loads, re, im):
    row_win, scale = row_win[...].T, col_win[...]
    for block in range(RADIX):
        if block % (RADIX // len(loads)) == 0:
            loads[block * len(loads) // RADIX].wait()
        half = block % 2 * RADIX
        window = row_win[half : half + RADIX, block // 2 : block // 2 + 1] * scale
        rows, src = pl.ds(block * PITCH, RADIX), pl.ds(block * RADIX, RADIX)
        re[rows, :] = strip[0, src, :].astype(F32) * window
        im[rows, :] = strip[1, src, :].astype(F32) * window


def spectrum(re, im, mid_re, mid_im, wide_re, wide_im, first, second):
    def fetch(index):
        rows = strided(index, PITCH)
        return re[rows, :], im[rows, :]

    def put(index, real, imag):
        here, before = strided(WIDE + index, WIDE), strided(RADIX + index, WIDE)
        wide_re[here, :] = real
        wide_im[here, :] = imag
        wide_re[before, :] = real
        wide_im[before, :] = imag

    transform_rows(fetch, mid_re, mid_im, first, second, put)


def cut_rows(which, facet, offs, turn, wide_re, wide_im, out):
    base = offs[which]
    index = (facet * base) & (FACETS - 1)
    cosine, sine = turn[0, index], turn[1, index]
    start = WIDE + base // RADIX * WIDE + base % RADIX
    for part in range(8):
        rows = pl.ds(start + part * WIDE, RADIX)
        real, imag = wide_re[rows, :], wide_im[rows, :]
        blocks = pl.ds(part * 4, 4)
        out[which, 0, blocks] = (cosine * real + sine * imag).astype(BF16).reshape(4, 16, LANES)
        out[which, 1, blocks] = (cosine * imag - sine * real).astype(BF16).reshape(4, 16, LANES)


def backward_kernel(
    offs_hbm, turn_hbm, row_hbm, col_hbm, first_hbm, strips_hbm, second_hbm, out_hbm,
    offs, turn, row_win, col_win, first, small_sem, re, im, mid_re, mid_im, wide_re, wide_im, strips, second, out, second_sem, strip_sem, out_sem,
):
    def load(which):
        return pltpu.make_async_copy(strips_hbm.at[which], strips.at[which], strip_sem.at[which])

    pairs = zip((offs_hbm, turn_hbm, row_hbm, col_hbm, first_hbm), (offs, turn, row_win, col_win, first))
    small = [pltpu.make_async_copy(src, dst, small_sem.at[i]) for i, (src, dst) in enumerate(pairs)]
    for copy in small:
        copy.start()
    for which in range(FACETS):
        load(which).start()
    table = pltpu.make_async_copy(second_hbm, second, second_sem)
    table.start()
    facet = lax.axis_index("facet")

    def clear(step, carry):
        rows = pl.ds(pl.multiple_of(step * 128, 128), 128)
        wide_re[rows, :] = jnp.zeros((128, LANES), F32)
        wide_im[rows, :] = jnp.zeros((128, LANES), F32)
        return carry

    lax.fori_loop(0, WIDE_ROWS // 128, clear, 0, unroll=2)
    for copy in small:
        copy.wait()

    def place(which, carry):
        load(which).wait()
        base = offs[which]
        index = (facet * base) & (FACETS - 1)
        cosine, sine = turn[0, index], turn[1, index]
        start = WIDE + base // RADIX * WIDE + base % RADIX
        for part in range(8):
            rows = pl.ds(start + part * WIDE, RADIX)
            blocks = pl.ds(part * 4, 4)
            real = strips[which, 0, blocks].reshape(RADIX, LANES).astype(F32)
            imag = strips[which, 1, blocks].reshape(RADIX, LANES).astype(F32)
            wide_re[rows, :] = wide_re[rows, :] + (cosine * real - sine * imag)
            wide_im[rows, :] = wide_im[rows, :] - (sine * real + cosine * imag)
        return carry

    lax.fori_loop(0, FACETS, place, 0)
    table.wait()

    def fetch(index):
        here, before = strided(WIDE + index, WIDE), strided(RADIX + index, WIDE)
        return wide_re[here, :] + wide_re[before, :], wide_im[here, :] + wide_im[before, :]

    def put(index, real, imag):
        rows = strided(index, PITCH)
        re[rows, :] = real
        im[rows, :] = imag

    transform_rows(fetch, mid_re, mid_im, first, second, put)
    row_win, scale = row_win[...].T, col_win[...]
    quarter = LONG // 4
    copies = []
    for block in range(RADIX):
        half = block % 2 * RADIX
        window = row_win[half : half + RADIX, block // 2 : block // 2 + 1] * scale
        rows, dst = pl.ds(block * PITCH, RADIX), pl.ds(block * RADIX, RADIX)
        out[0, dst, :] = (re[rows, :] * window).astype(BF16)
        out[1, dst, :] = (im[rows, :] * -window).astype(BF16)
        if block % 16 == 15:
            done = pl.ds(block // 16 * quarter, quarter)
            copies.append(
                pltpu.make_async_copy(out.at[:, done], out_hbm.at[:, done], out_sem.at[block // 16])
            )
            copies[-1].start()
    for copy in copies:
        copy.wait()


def times(pair, cosine, sine):
    return (pair[0] * cosine - pair[1] * sine, pair[0] * sine + pair[1] * cosine)


def times_unit(pair, num, den, sign):
    num = num % den
    if num == 0:
        return pair
    if 4 * num == den:
        return (-sign * pair[1], sign * pair[0])
    if 2 * num == den:
        return (-pair[0], -pair[1])
    angle = 2 * math.pi * num / den
    return times(pair, math.cos(angle), sign * math.sin(angle))


def small_dft(items, sign):
    count = len(items)
    if count == 1:
        return items
    even = small_dft(items[0::2], sign)
    odd = small_dft(items[1::2], sign)
    odd = [times_unit(odd[i], i, count, sign) for i in range(count // 2)]
    low = [(a[0] + b[0], a[1] + b[1]) for a, b in zip(even, odd)]
    high = [(a[0] - b[0], a[1] - b[1]) for a, b in zip(even, odd)]
    return low + high


def dft_over_blocks(get, put, work, sign):
    for lo in range(8):
        items = small_dft([get(lo + 8 * hi) for hi in range(4)], sign)
        for p_lo in range(4):
            value = times_unit(items[p_lo], lo * p_lo, SUBS, sign)
            work[p_lo * 8 + lo, 0] = value[0]
            work[p_lo * 8 + lo, 1] = value[1]
    for p_lo in range(4):
        items = small_dft([(work[p_lo * 8 + lo, 0], work[p_lo * 8 + lo, 1]) for lo in range(8)], sign)
        for p_hi in range(8):
            put(p_lo + 4 * p_hi, items[p_hi])


def columns_to_tiles(blocks, phase, dense, twist, rep, sel, keep, work, folded, tiles):
    def get(s):
        pair = (blocks[0, s].astype(F32), blocks[1, s].astype(F32))
        return times(pair, phase[0, s : s + 1, :], -phase[1, s : s + 1, :])

    def put(p, pair):
        pair = times(pair, twist[0, p : p + 1, :], -twist[1, p : p + 1, :])
        rows = slice(p * 16, p * 16 + 16)
        folded[rows, 0:LANES] = pair[0].astype(BF16)
        folded[rows, LANES : 2 * LANES] = pair[1].astype(BF16)

    dft_over_blocks(get, put, work, -1.0)
    flat = mm_nt(dense[...], folded[...]).astype(BF16)
    stacked = jnp.concatenate(
        [
            jnp.concatenate([flat[0:16, 0:256], flat[16:32, 0:256]], axis=1),
            jnp.concatenate([flat[0:16, 256:512], flat[16:32, 256:512]], axis=1),
        ],
        axis=0,
    )
    spread = mm(rep[...], stacked).astype(BF16) * keep[...]
    own = as_bf(iota((512, LANES), 1) // 32 == iota((512, LANES), 0) // TS % CAP)
    tiles[...] = mm(spread, sel[...]).astype(BF16) * own


def tiles_to_columns(tiles, phase, dense, twist, rep_t, sel, keep, work, folded_f32, images):
    spread = mm_nt(tiles[...], sel[...]).astype(BF16) * keep[...]
    stacked = mm(rep_t[...], spread).astype(BF16)
    flat = jnp.concatenate(
        [
            jnp.concatenate([stacked[0:16, 0:256], stacked[16:32, 0:256]], axis=1),
            jnp.concatenate([stacked[0:16, 256:512], stacked[16:32, 256:512]], axis=1),
        ],
        axis=0,
    )
    folded_f32[...] = mm_tn(flat, dense[...])

    def get(p):
        rows = slice(p * 16, p * 16 + 16)
        pair = (folded_f32[rows, 0:LANES], folded_f32[rows, LANES : 2 * LANES])
        return times(pair, twist[0, p : p + 1, :], twist[1, p : p + 1, :])

    def put(s, pair):
        pair = times(pair, phase[0, s : s + 1, :], phase[1, s : s + 1, :])
        images[0, s] = pair[0].astype(BF16)
        images[1, s] = pair[1].astype(BF16)

    dft_over_blocks(get, put, work, 1.0)


VALUES = 8


def unit_circle(turns, total):
    half = jnp.where(turns >= total / 2.0, turns - total, turns) * (math.pi / total)
    sq = half * half
    sine = 1.0 / 6227020800.0
    for term in (-1.0 / 39916800.0, 1.0 / 362880.0, -1.0 / 5040.0, 1.0 / 120.0, -1.0 / 6.0, 1.0):
        sine = sine * sq + term
    sine = sine * half
    cosine = 1.0 / 479001600.0
    for term in (-1.0 / 3628800.0, 1.0 / 40320.0, -1.0 / 720.0, 1.0 / 24.0, -0.5, 1.0):
        cosine = cosine * sq + term
    return 1.0 - 2.0 * sine * sine, 2.0 * sine * cosine


def over_pixels(values):
    return jnp.broadcast_to(values[:, None, :], (8, TS, LANES)).reshape(8 * TS, LANES)


def pack_visibilities(measured, masked, pixels, staged, packed):
    for part in range(4):
        rows = pl.ds(part * 32, 32)
        blocks = pl.ds(part * 8, 8)
        values = []
        for z in range(2):
            value = measured[rows, z, :]
            coarse = value.astype(BF16).astype(F32)
            values += [coarse, value - coarse]
        values.append(masked[rows, :])
        values += [pixels[i, rows, :].astype(F32) for i in range(3)]
        for q in range(VALUES):
            staged[blocks, q * CAP : (q + 1) * CAP, :] = values[q].reshape(8, CAP, LANES)
        packed[blocks] = staged[blocks].astype(BF16)


def visit(tiles, vis, my_tiles):
    pixel = (iota((8 * TS, LANES), 0) % TS).astype(F32)
    square = (pixel - 8.0) * (pixel - 8.0)
    own = (iota((64, LANES), 1) // 32 == iota((64, LANES), 0) // TS).astype(F32)

    for step in range(4):
        def value(q):
            return vis[q * SUBS + step * 8 : q * SUBS + step * 8 + 8, :]

        turns = over_pixels(value(7)) * square
        turns = turns - 256.0 * jnp.floor(turns * (1.0 / 256.0))
        cosine, sine = unit_circle(turns, 256.0)
        row_off = (pixel - over_pixels(value(5))) / kernel_width
        col_off = (pixel - over_pixels(value(6))) / kernel_width
        row_fall = kernel_norm * jnp.exp(-(row_off * row_off))
        col_fall = kernel_norm * jnp.exp(-(col_off * col_off))
        row_re, row_im = (row_fall * cosine).astype(BF16), (-row_fall * sine).astype(BF16)
        upper = jnp.concatenate([row_re, row_im], axis=1)
        lower = jnp.concatenate([-row_im, row_re], axis=1)
        weights = []
        for half in range(2):
            pieces = []
            for slot in range(4):
                src = slice(half * 64 + slot * TS, half * 64 + slot * TS + TS)
                pieces += [upper[src], lower[src]]
            weights.append(jnp.concatenate(pieces, axis=0))
        col_re = (col_fall * cosine).astype(BF16).astype(F32)
        col_im = (-col_fall * sine).astype(BF16).astype(F32)
        first = step * 128
        part = jnp.concatenate(
            [mm(tiles[first + half * 64 : first + half * 64 + 64, :], weights[half]) for half in range(2)],
            axis=0,
        )
        part_re, part_im = part[:, 0:LANES], part[:, LANES : 2 * LANES]
        pred_re = jnp.sum((col_re * part_re - col_im * part_im).reshape(8, TS, LANES), axis=1)
        pred_im = jnp.sum((col_re * part_im + col_im * part_re).reshape(8, TS, LANES), axis=1)
        weight = value(4)
        res_re = over_pixels(weight * (value(0) + value(1) - pred_re))
        res_im = over_pixels(weight * (value(2) + value(3) - pred_im))
        back_re = (col_re * res_re + col_im * res_im).astype(BF16)
        back_im = (col_re * res_im - col_im * res_re).astype(BF16)
        back = jnp.concatenate([back_re, back_im], axis=1)
        for half in range(2):
            grid = mm_nt(back[half * 64 : half * 64 + 64], weights[half]) * own
            my_tiles[first + half * 64 : first + half * 64 + 64, :] = grid.astype(BF16)


def as_bf(condition):
    return condition.astype(F32).astype(BF16)


def iota(shape, dim):
    return lax.broadcasted_iota(jnp.int32, shape, dim)


def masked_weights(weight, counts, masked):
    identity = as_bf(iota((LANES, LANES), 0) == iota((LANES, LANES), 1))
    spread = jnp.broadcast_to(counts[...].astype(F32), (LANES, LANES)).astype(BF16)
    column = mm_nt(identity, spread)
    masked[...] = jnp.where(iota((LANES, LANES), 1).astype(F32) < column, weight[...], 0.0)


def column_phase(facet, offsets, phase):
    mine = jnp.where(iota((1, FACETS), 1) == facet, offsets[...], 0)
    start = jnp.sum(mine.astype(F32), axis=1, keepdims=True).astype(jnp.int32)
    column = iota((SUBS, LANES), 0) * LANES + iota((SUBS, LANES), 1)
    turns = ((column * start) & (LONG - 1)).astype(F32)
    cosine, sine = unit_circle(turns, float(LONG))
    phase[0] = cosine
    phase[1] = sine


def same_pixel(keep):
    for part in range(4):
        rows = slice(part * 128, part * 128 + 128)
        keep[rows, :] = as_bf(iota((128, 512), 0) % TS == iota((128, 512), 1) // TS % TS)


def routing(owners, choice):
    square = (SUBS, SUBS)
    up, across = iota(square, 0), iota(square, 1)
    named = as_bf(owners[...] == up)
    moved = as_bf(across == up % 2 * 16 + up // 2)
    identity = as_bf(up == across)
    earlier = mm(named, as_bf(up < across)).astype(BF16)
    named = mm(named, moved).astype(BF16)
    rank = jnp.sum(named.astype(F32) * mm(earlier, moved), axis=0, keepdims=True)
    rank = mm_nt(identity, jnp.broadcast_to(rank, (LANES, SUBS)).astype(BF16))
    by_tile = mm_nt(identity, named).astype(BF16)
    wide = (SUBS, SUBS * SUBS)
    by_tile = mm(by_tile, as_bf(iota(wide, 1) // SUBS == iota(wide, 0)))
    at_rank = (rank == (iota((SUBS, LANES), 1) % CAP).astype(F32)).astype(F32)
    both = by_tile * jnp.concatenate([at_rank] * 8, axis=1)
    which = iota(wide, 1) % SUBS // CAP
    for q in range(VALUES):
        choice[q * SUBS : (q + 1) * SUBS, :] = jnp.where(which == q, both, 0.0).astype(BF16)


def add_blocks(dst, sources, lo, count):
    def one(step, carry):
        total = sources[0][lo + step].astype(F32)
        for src in sources[1:]:
            total = total + src[lo + step].astype(F32)
        dst[lo + step] = total.astype(BF16)
        return carry

    lax.fori_loop(0, count, one, 0, unroll=4)


def facet_to_strips_kernel(
    strip_hbm, second_hbm, *rest
):
    count = len(SMALL)
    small_hbm, out_hbm, small = rest[:count], rest[count], rest[count + 1 : 2 * count + 1]
    strips_body(strip_hbm, second_hbm, small_hbm, out_hbm, small, *small, *rest[2 * count + 1 :])


def strips_body(
    strip_hbm, second_hbm, small_hbm, out_hbm, small,
    offs, turn, row_win, col_win, first, offsets, owners, measured, weight, pixels, counts,
    dense, twist, rep, rep_t, sel,
    strip, re, im, mid_re, mid_im, wide_re, wide_im, second, keep, mine,
    pair_buf, sums, carry_a, carry_b, from_dn, from_up, total, gathered,
    work, folded, folded_f32, tiles, my_tiles, images, out,
    masked, phase, staged, packed, received, choice, vis,
    load_sem, out_sem,
    pair_s, pair_r, ring_s, ring_r, send_s, rows_r, vis_r, image_r, gath_s, gath_r,
):
    me = lax.axis_index("sub")
    facet = lax.axis_index("facet")
    core, chip = lax.rem(facet, 2), facet // 2
    sib = facet + 1 - 2 * core
    up, dn = lax.rem(facet + 2, FACETS), lax.rem(facet + 6, FACETS)
    opp = lax.rem(facet + 4, FACETS)
    low, high = pl.ds(0, 16), pl.ds(16, 16)

    barrier = pltpu.get_barrier_semaphore()

    def greet(step, carry):
        pl.semaphore_signal(barrier, inc=1, device_id={"sub": lax.rem(me + step, SUBS)}, device_id_type=MESH)
        return carry

    for peer in (sib, up, dn):
        pl.semaphore_signal(barrier, inc=1, device_id={"facet": peer}, device_id_type=MESH)
    lax.fori_loop(1, SUBS, greet, 0)
    quarter = LONG // 4
    loads = [
        pltpu.make_async_copy(
            strip_hbm.at[:, pl.ds(i * quarter, quarter)], strip.at[:, pl.ds(i * quarter, quarter)], load_sem.at[i]
        )
        for i in range(4)
    ]
    second_load = pltpu.make_async_copy(second_hbm, second, load_sem.at[4])
    small_loads = [
        pltpu.make_async_copy(src, dst, load_sem.at[5 + i]) for i, (src, dst) in enumerate(zip(small_hbm, small))
    ]
    for copy in loads + small_loads + [second_load]:
        copy.start()
    for copy in small_loads:
        copy.wait()
    masked_weights(weight, counts, masked)
    pack_visibilities(measured, masked, pixels, staged, packed)
    load_strip(strip, row_win, col_win, loads, re, im)
    second_load.wait()
    spectrum(re, im, mid_re, mid_im, wide_re, wide_im, first, second)
    pl.semaphore_wait(barrier, SUBS + 2)

    def to_facet(src, dst, ssem, rsem, peer):
        return pltpu.make_async_remote_copy(
            src_ref=src, dst_ref=dst, send_sem=ssem, recv_sem=rsem,
            device_id={"facet": peer}, device_id_type=MESH,
        )

    x_at = [lax.rem(me // 8 + i, 4) * 8 for i in range(4)]
    z_at = [lax.rem(lax.rem(me, 8) + i, 8) for i in range(8)]
    steps = sorted(
        ((i, j) for i in range(4) for j in range(8) if i + j),
        key=lambda ij: -(min(ij[0], 4 - ij[0]) + min(ij[1], 8 - ij[1])),
    )
    peers = [x_at[i] + z_at[j] for i, j in steps]

    def swap(src_of, dst, kind, rsem):
        def copy_to(peer, slot):
            return pltpu.make_async_remote_copy(
                src_ref=src_of.at[peer], dst_ref=dst.at[slot],
                send_sem=send_s.at[kind, peer], recv_sem=rsem.at[slot],
                device_id={"sub": peer}, device_id_type=MESH,
            )

        def receive(step, carry):
            peer = lax.rem(me + SUBS - step, SUBS)
            copy_to(peer, peer).wait_recv()
            return carry

        def drain(step, carry):
            copy_to(lax.rem(me + step, SUBS), me).wait_send()
            return carry

        for peer in peers:
            copy_to(peer, me).start()
        dst[me] = src_of[me]
        return (
            lambda: lax.fori_loop(1, SUBS, receive, 0),
            lambda: lax.fori_loop(1, SUBS, drain, 0),
        )

    pairs = {}
    for plane in range(2):
        for hop in (2, 1, 3, 0):
            target = 2 * lax.rem(chip + hop, 4) + 1 - core
            if plane == 0:
                cut_rows(target, facet, offs, turn, wide_re, wide_im, mine)
            pairs[plane, hop] = to_facet(
                mine.at[target, plane], pair_buf.at[hop, plane],
                pair_s.at[plane, hop], pair_r.at[plane, hop], sib,
            )
            pairs[plane, hop].start()

    def merge_pair(plane, hop):
        pairs[plane, hop].wait_recv()
        target = 2 * lax.rem(chip + hop, 4) + core
        add_blocks(sums.at[hop, plane], [mine.at[target, plane], pair_buf.at[hop, plane]], 0, SUBS)

    rings = [
        [
            to_facet(src, dst, ring_s.at[plane, i], ring_r.at[plane, i], peer)
            for i, (src, dst, peer) in enumerate((
                (sums.at[2, plane, low], carry_a.at[plane], up),
                (sums.at[2, plane, high], carry_b.at[plane], dn),
                (sums.at[1, plane, high], from_dn.at[plane, high], up),
                (sums.at[3, plane, low], from_up.at[plane, low], dn),
                (sums.at[1, plane, low], from_dn.at[plane, low], up),
                (sums.at[3, plane, high], from_up.at[plane, high], dn),
            ))
        ]
        for plane in range(2)
    ]

    def merge_ring(plane):
        ring = rings[plane]
        ring[0].wait_recv()
        add_blocks(sums.at[1, plane, low], [sums.at[1, plane, low], carry_a.at[plane]], 0, 16)
        ring[4].start()
        ring[1].wait_recv()
        add_blocks(sums.at[3, plane, high], [sums.at[3, plane, high], carry_b.at[plane]], 0, 16)
        ring[5].start()

    def finish(plane):
        pairs[plane, 0].wait_recv()
        for step in (3, 4, 2, 5):
            rings[plane][step].wait_recv()
        own_target = 2 * chip + core
        add_blocks(
            total.at[plane],
            [mine.at[own_target, plane], pair_buf.at[0, plane], from_dn.at[plane], from_up.at[plane]],
            0, SUBS,
        )

    cut_rows(2 * lax.rem(chip + 2, 4) + core, facet, offs, turn, wide_re, wide_im, mine)
    merge_pair(0, 2)
    rings[0][0].start()
    rings[0][1].start()
    cut_rows(2 * lax.rem(chip + 1, 4) + core, facet, offs, turn, wide_re, wide_im, mine)
    merge_pair(0, 1)
    rings[0][2].start()
    cut_rows(2 * lax.rem(chip + 3, 4) + core, facet, offs, turn, wide_re, wide_im, mine)
    merge_pair(0, 3)
    rings[0][3].start()
    receive_vis, drain_vis = swap(packed, received, 2, vis_r)
    merge_pair(1, 2)
    rings[1][0].start()
    rings[1][1].start()
    cut_rows(2 * chip + core, facet, offs, turn, wide_re, wide_im, mine)
    merge_pair(1, 1)
    merge_pair(1, 3)
    column_phase(facet, offsets, phase)
    merge_ring(0)
    rings[1][2].start()
    rings[1][3].start()
    routing(owners, choice)
    same_pixel(keep)
    merge_ring(1)
    finish(0)
    receive_re, drain_re = swap(total.at[0], gathered.at[0], 0, rows_r.at[0])
    finish(1)
    receive_im, drain_im = swap(total.at[1], gathered.at[1], 1, rows_r.at[1])
    receive_vis()
    vis[...] = mm(choice[...], received[...].reshape(SUBS * SUBS, LANES))
    receive_re()
    receive_im()
    columns_to_tiles(gathered, phase, dense, twist, rep, sel, keep, work, folded, tiles)
    visit(tiles, vis, my_tiles)
    tiles_to_columns(my_tiles, phase, dense, twist, rep_t, sel, keep, work, folded_f32, images)

    swaps = [swap(images.at[plane], out.at[facet, plane], 3 + plane, image_r.at[plane]) for plane in range(2)]
    for copy in rings[0] + rings[1] + list(pairs.values()):
        copy.wait_send()
    for drain in (drain_vis, drain_re, drain_im):
        drain()
    stores = []
    sends = []

    def store(where):
        copy = pltpu.make_async_copy(out.at[where], out_hbm.at[where], out_sem.at[len(stores)])
        copy.start()
        stores.append(copy)

    def share(plane, index, where, peer):
        ref = out.at[where]
        return to_facet(ref, ref, gath_s.at[plane, index], gath_r.at[plane, index], peer)

    def send(plane, index, where, peer):
        sends.append(share(plane, index, where, peer))
        sends[-1].start()

    def arrives(plane, index, where):
        share(plane, index, where, sib).wait_recv()

    other = 1 - 2 * core
    for plane in range(2):
        swaps[plane][0]()
        own = (facet, plane)
        send(plane, 0, own, up)
        send(plane, 1, own, dn)
        send(plane, 2, own, sib)
        store(own)
    for plane in range(2):
        swaps[plane][1]()
    for plane in range(2):
        arrives(plane, 0, (dn, plane))
        send(plane, 3, (dn, plane, low), up)
        send(plane, 5, (dn, plane), sib)
        store((dn, plane))
        arrives(plane, 1, (up, plane))
        send(plane, 4, (up, plane, high), dn)
        send(plane, 6, (up, plane), sib)
        store((up, plane))
    for plane in range(2):
        arrives(plane, 2, (sib, plane))
        store((sib, plane))
        arrives(plane, 5, (dn + other, plane))
        store((dn + other, plane))
        arrives(plane, 6, (up + other, plane))
        store((up + other, plane))
    for plane in range(2):
        arrives(plane, 3, (opp, plane, low))
        send(plane, 7, (opp, plane, low), sib)
        store((opp, plane, low))
        arrives(plane, 4, (opp, plane, high))
        send(plane, 8, (opp, plane, high), sib)
        store((opp, plane, high))
    for plane in range(2):
        arrives(plane, 7, (opp + other, plane, low))
        store((opp + other, plane, low))
        arrives(plane, 8, (opp + other, plane, high))
        store((opp + other, plane, high))
    for copy in sends:
        copy.wait_send()
    for copy in stores:
        copy.wait()


def vmem_specs(count):
    return [pl.BlockSpec(memory_space=pltpu.VMEM)] * count


def smem_specs(count):
    return [pl.BlockSpec(memory_space=pltpu.SMEM)] * count


BIG = 60 * 1024 * 1024
STRIPS = (FACETS, 2, SUBS, 16, LANES)
WIDE_ROWS = 66 * 128


def any_specs(count):
    return [pl.BlockSpec(memory_space=pl.ANY)] * count


def row_scratch():
    narrow, wide = pltpu.VMEM((RADIX * PITCH, LANES), F32), pltpu.VMEM((WIDE_ROWS, LANES), F32)
    return [narrow] * 4 + [wide] * 2


TABLE = (RADIX, 2 * RADIX, 2 * RADIX)


def backward_call(shape):
    return pl.pallas_call(
        backward_kernel,
        out_shape=jax.ShapeDtypeStruct(shape, BF16),
        in_specs=any_specs(7),
        out_specs=pl.BlockSpec(memory_space=pl.ANY),
        scratch_shapes=[(pltpu.SMEM if i < 2 else pltpu.VMEM)(*item) for i, item in enumerate(SMALL[:5])]
        + [pltpu.SemaphoreType.DMA((5,))]
        + row_scratch()
        + [
            pltpu.VMEM(STRIPS, BF16),
            pltpu.VMEM(TABLE, BF16),
            pltpu.VMEM(shape, BF16),
            pltpu.SemaphoreType.DMA,
            pltpu.SemaphoreType.DMA((FACETS,)),
            pltpu.SemaphoreType.DMA((4,)),
        ],
        compiler_params=pltpu.CompilerParams(vmem_limit_bytes=BIG),
    )


def strips_call(shape):
    block = (2, SUBS, 16, LANES)
    half = (2, 16, 16, LANES)
    values = (SUBS, VALUES * CAP, LANES)
    vm = pltpu.VMEM
    dma = pltpu.SemaphoreType.DMA
    return pl.pallas_call(
        facet_to_strips_kernel,
        out_shape=jax.ShapeDtypeStruct(STRIPS, BF16),
        in_specs=any_specs(2 + len(SMALL)),
        out_specs=pl.BlockSpec(memory_space=pl.ANY),
        scratch_shapes=[(pltpu.SMEM if i < 2 else vm)(*item) for i, item in enumerate(SMALL)]
        + [vm(shape, BF16)]
        + row_scratch()
        + [
            vm(TABLE, BF16), vm((512, 512), BF16), vm(STRIPS, BF16),
            vm((4,) + block, BF16), vm((4,) + block, BF16), vm(half, BF16), vm(half, BF16),
            vm(block, BF16), vm(block, BF16), vm(block, BF16), vm(block, BF16),
            vm((SUBS, 2, 16, LANES), F32), vm((512, 256), BF16), vm((512, 256), F32),
            vm((512, LANES), BF16), vm((512, LANES), BF16), vm(block, BF16), vm(STRIPS, BF16),
            vm((LANES, LANES), F32), vm((2, SUBS, LANES), F32),
            vm(values, F32), vm(values, BF16), vm(values, BF16),
            vm((VALUES * SUBS, SUBS * SUBS), BF16), vm((VALUES * SUBS, LANES), F32),
            dma((5 + len(SMALL),)), dma((20,)),
            dma((2, 4)), dma((2, 4)), dma((2, 6)), dma((2, 6)), dma((5, SUBS)),
            dma((2, SUBS)), dma((SUBS,)), dma((2, SUBS)), dma((2, 9)), dma((2, 9)),
        ],
        compiler_params=pltpu.CompilerParams(
            vmem_limit_bytes=BIG, collective_id=0, has_side_effects=True
        ),
    )


def per_device(
    facet_strips, row_window, col_window, row_offsets, col_offsets,
    tile_owner, measured, vis_weight, uvw_pixels, vis_count,
):
    first, second = row_tables()
    dense, twist, rep, rep_t, sel = col_tables()
    eighth = 2 * np.pi * np.arange(FACETS) / FACETS
    turn = jnp.asarray(np.stack([np.cos(eighth), np.sin(eighth)]), F32)
    row_win = row_window.reshape(LONG // LANES, LANES)
    col_win = col_window.reshape(1, LANES)
    strips = strips_call(facet_strips.shape)(
        facet_strips, second, row_offsets, turn, row_win, col_win, first,
        col_offsets.reshape(1, FACETS), tile_owner.reshape(1, SUBS), measured[0, 0],
        vis_weight[0, 0], jnp.transpose(uvw_pixels[0, 0], (1, 0, 2)), vis_count.reshape(1, LANES),
        dense, twist, rep, rep_t, sel,
    )
    return backward_call(facet_strips.shape)(
        row_offsets, turn, row_win, col_win, first, strips, second
    )


def solution(mesh):
    in_specs = (
        P(None, "facet", "sub"),
        P(),
        P("sub"),
        P(),
        P(),
        P("sub", "facet", None, None),
        P("facet", "sub", None, None, None),
        P("facet", "sub", None, None),
        P("facet", "sub", None, None, None),
        P("facet", "sub", None),
    )
    return jax.shard_map(
        per_device, mesh=mesh, in_specs=in_specs, out_specs=P(None, "facet", "sub"), check_vma=False
    )
```

```python
import math

import jax
import jax.numpy as jnp
import numpy as np
from jax import lax
from jax.experimental import pallas as pl
from jax.experimental.pallas import tpu as pltpu
from jax.sharding import PartitionSpec as P

SG = 512
RADIX = 64
TS = 16
LONG = 4096
SUBS = 32
FACETS = 8
CAP = 4
LANES = 128
MESH = pl.DeviceIdType.MESH
F32 = jnp.float32
BF16 = jnp.bfloat16

kernel_width = 2.5
kernel_norm = 0.565


def as_real(theta):
    cosine, sine = np.cos(theta), np.sin(theta)
    return np.block([[cosine, sine], [-sine, cosine]])


def row_tables():
    idx = np.arange(RADIX)
    first = as_real(2 * np.pi * (np.outer(idx, idx) % RADIX) / RADIX)
    second = [
        as_real(2 * np.pi * (np.outer(k1 + RADIX * idx, idx) % LONG) / LONG) / RADIX
        for k1 in range(RADIX)
    ]
    return jnp.asarray(first, BF16), jnp.asarray(np.stack(second), BF16)


def col_tables():
    high = np.outer(np.arange(16), np.arange(LANES)) % LANES
    dense = as_real(2 * np.pi * high / LANES)
    low = 2 * np.pi * np.outer(np.arange(SUBS), np.arange(LANES)) / LONG
    twist = np.stack([np.cos(low), np.sin(low)]) / 64.0
    rep = np.zeros((512, 32))
    rep[np.arange(512), np.arange(512) // 16] = 1
    sel = np.zeros((2, 16, 16, 4, 2, 16))
    for z in range(2):
        for r in range(16):
            sel[z, :, r, :, z, r] = 1
    sel = sel.reshape(512, 128)
    return (
        jnp.asarray(dense, BF16),
        jnp.asarray(twist, F32),
        jnp.asarray(rep, BF16),
        jnp.asarray(rep.T, BF16),
        jnp.asarray(sel, BF16),
    )


def mm(first, other):
    return jnp.dot(first, other, preferred_element_type=F32)


def mm_nt(first, other):
    return lax.dot_general(first, other, (((1,), (1,)), ((), ())), preferred_element_type=F32)


def mm_tn(first, other):
    return lax.dot_general(first, other, (((0,), (0,)), ((), ())), preferred_element_type=F32)


STEPS = sorted(
    ((i, j) for i in range(4) for j in range(8)),
    key=lambda ij: -(min(ij[0], 4 - ij[0]) + min(ij[1], 8 - ij[1])),
)
SEEN_FROM = [STEPS.index(((4 - i) % 4, (8 - j) % 8)) for i, j in STEPS]


def devices_by_distance(me):
    x, z = lax.div(me, 8), lax.rem(me, 8)
    x_at = [lax.rem(x + i, 4) * 8 for i in range(4)]
    z_at = [lax.rem(z + i, 8) for i in range(8)]
    return [x_at[i] + z_at[j] for i, j in STEPS]


def wide_rows(peers):
    return [lax.div(peer, 4) * WIDE + lax.rem(peer, 4) * 16 for peer in peers]


PITCH = RADIX + 1
WIDE = 2 * RADIX + 1


def strided(index, pitch):
    return pl.ds(index, RADIX, stride=pitch)


def transform_rows(fetch, mid_re, mid_im, first, second, put):
    def stage_a(step, carry):
        parts = []
        for u in range(2):
            real, imag = fetch(2 * step + u)
            parts.append(jnp.concatenate([real, imag], axis=0).astype(BF16))
        res = mm(first[...], jnp.concatenate(parts, axis=1))
        for u in range(2):
            rows = strided(2 * step + u, PITCH)
            mid_re[rows, :] = res[:RADIX, u * LANES : (u + 1) * LANES]
            mid_im[rows, :] = res[RADIX:, u * LANES : (u + 1) * LANES]
        return carry

    lax.fori_loop(0, RADIX // 2, stage_a, 0, unroll=16)

    def stage_b(step, carry):
        rows = pl.ds(step * PITCH, RADIX)
        block = jnp.concatenate([mid_re[rows, :], mid_im[rows, :]], axis=0).astype(BF16)
        res = mm(second[step], block)
        put(step, res[:RADIX], res[RADIX:])
        return carry

    lax.fori_loop(0, RADIX, stage_b, 0, unroll=32)


SMALL = (
    ((FACETS,), jnp.int32), ((2, FACETS), F32), ((SUBS, LANES), F32), ((1, LANES), F32),
    ((LANES, LANES), BF16), ((1, FACETS), jnp.int32), ((1, SUBS), jnp.int32),
    ((LANES, 2, LANES), F32), ((LANES, LANES), F32), ((3, LANES, LANES), jnp.int32), ((1, LANES), jnp.int32),
    ((SUBS, 2 * LANES), BF16), ((2, SUBS, LANES), F32), ((512, SUBS), BF16), ((SUBS, 512), BF16),
    ((512, LANES), BF16),
)


def load_strip(strip, row_win, col_win, loads, re, im):
    row_win, scale = row_win[...].T, col_win[...]
    for block in range(RADIX):
        if block % (RADIX // len(loads)) == 0:
            loads[block * len(loads) // RADIX].wait()
        half = block % 2 * RADIX
        window = row_win[half : half + RADIX, block // 2 : block // 2 + 1] * scale
        rows, src = pl.ds(block * PITCH, RADIX), pl.ds(block * RADIX, RADIX)
        re[rows, :] = strip[0, src, :].astype(F32) * window
        im[rows, :] = strip[1, src, :].astype(F32) * window


def spectrum(re, im, mid_re, mid_im, wide_re, wide_im, first, second):
    def fetch(index):
        rows = strided(index, PITCH)
        return re[rows, :], im[rows, :]

    def put(index, real, imag):
        here, before = strided(WIDE + index, WIDE), strided(RADIX + index, WIDE)
        wide_re[here, :] = real
        wide_im[here, :] = imag
        wide_re[before, :] = real
        wide_im[before, :] = imag

    transform_rows(fetch, mid_re, mid_im, first, second, put)


def cut_rows(which, facet, offs, turn, places, wide_re, wide_im, out):
    base = offs[which]
    index = (facet * base) & (FACETS - 1)
    cosine, sine = turn[0, index], turn[1, index]
    start = WIDE + base // RADIX * WIDE + base % RADIX
    for i, place in enumerate(places):
        rows = pl.ds(start + place, 16)
        real, imag = wide_re[rows, :], wide_im[rows, :]
        out[which, i // 16, 0, i % 16] = (cosine * real + sine * imag).astype(BF16)
        out[which, i // 16, 1, i % 16] = (cosine * imag - sine * real).astype(BF16)


def backward_kernel(
    offs_hbm, turn_hbm, row_hbm, col_hbm, first_hbm, strips_hbm, second_hbm, out_hbm,
    offs, turn, row_win, col_win, first, small_sem, re, im, mid_re, mid_im, wide_re, wide_im, strips, second, out, second_sem, strip_sem, out_sem,
):
    def load(which):
        return pltpu.make_async_copy(strips_hbm.at[which], strips.at[which], strip_sem.at[which])

    pairs = zip((offs_hbm, turn_hbm, row_hbm, col_hbm, first_hbm), (offs, turn, row_win, col_win, first))
    small = [pltpu.make_async_copy(src, dst, small_sem.at[i]) for i, (src, dst) in enumerate(pairs)]
    for copy in small:
        copy.start()
    for which in range(FACETS):
        load(which).start()
    table = pltpu.make_async_copy(second_hbm, second, second_sem)
    table.start()
    facet = lax.axis_index("facet")

    def clear(step, carry):
        rows = pl.ds(pl.multiple_of(step * 128, 128), 128)
        wide_re[rows, :] = jnp.zeros((128, LANES), F32)
        wide_im[rows, :] = jnp.zeros((128, LANES), F32)
        return carry

    lax.fori_loop(0, WIDE_ROWS // 128, clear, 0, unroll=2)
    for copy in small:
        copy.wait()

    places = wide_rows(devices_by_distance(lax.axis_index("sub")))

    def place(which, carry):
        load(which).wait()
        base = offs[which]
        index = (facet * base) & (FACETS - 1)
        cosine, sine = turn[0, index], turn[1, index]
        start = WIDE + base // RADIX * WIDE + base % RADIX
        for i, place_at in enumerate(places):
            rows = pl.ds(start + place_at, 16)
            real = strips[which, i // 16, 0, i % 16].astype(F32)
            imag = strips[which, i // 16, 1, i % 16].astype(F32)
            wide_re[rows, :] = wide_re[rows, :] + (cosine * real - sine * imag)
            wide_im[rows, :] = wide_im[rows, :] - (sine * real + cosine * imag)
        return carry

    lax.fori_loop(0, FACETS, place, 0)
    table.wait()

    def fetch(index):
        here, before = strided(WIDE + index, WIDE), strided(RADIX + index, WIDE)
        return wide_re[here, :] + wide_re[before, :], wide_im[here, :] + wide_im[before, :]

    def put(index, real, imag):
        rows = strided(index, PITCH)
        re[rows, :] = real
        im[rows, :] = imag

    transform_rows(fetch, mid_re, mid_im, first, second, put)
    row_win, scale = row_win[...].T, col_win[...]
    quarter = LONG // 4
    copies = []
    for block in range(RADIX):
        half = block % 2 * RADIX
        window = row_win[half : half + RADIX, block // 2 : block // 2 + 1] * scale
        rows, dst = pl.ds(block * PITCH, RADIX), pl.ds(block * RADIX, RADIX)
        out[0, dst, :] = (re[rows, :] * window).astype(BF16)
        out[1, dst, :] = (im[rows, :] * -window).astype(BF16)
        if block % 16 == 15:
            done = pl.ds(block // 16 * quarter, quarter)
            copies.append(
                pltpu.make_async_copy(out.at[:, done], out_hbm.at[:, done], out_sem.at[block // 16])
            )
            copies[-1].start()
    for copy in copies:
        copy.wait()


def times(pair, cosine, sine):
    return (pair[0] * cosine - pair[1] * sine, pair[0] * sine + pair[1] * cosine)


def times_unit(pair, num, den, sign):
    num = num % den
    if num == 0:
        return pair
    if 4 * num == den:
        return (-sign * pair[1], sign * pair[0])
    if 2 * num == den:
        return (-pair[0], -pair[1])
    angle = 2 * math.pi * num / den
    return times(pair, math.cos(angle), sign * math.sin(angle))


def small_dft(items, sign):
    count = len(items)
    if count == 1:
        return items
    even = small_dft(items[0::2], sign)
    odd = small_dft(items[1::2], sign)
    odd = [times_unit(odd[i], i, count, sign) for i in range(count // 2)]
    low = [(a[0] + b[0], a[1] + b[1]) for a, b in zip(even, odd)]
    high = [(a[0] - b[0], a[1] - b[1]) for a, b in zip(even, odd)]
    return low + high


def dft_over_blocks(get, put, work, sign):
    for lo in range(8):
        items = small_dft([get(lo + 8 * hi) for hi in range(4)], sign)
        for p_lo in range(4):
            value = times_unit(items[p_lo], lo * p_lo, SUBS, sign)
            work[p_lo * 8 + lo, 0] = value[0]
            work[p_lo * 8 + lo, 1] = value[1]
    for p_lo in range(4):
        items = small_dft([(work[p_lo * 8 + lo, 0], work[p_lo * 8 + lo, 1]) for lo in range(8)], sign)
        for p_hi in range(8):
            put(p_lo + 4 * p_hi, items[p_hi])


def columns_to_tiles(blocks, phase, dense, twist, rep, sel, keep, work, folded, tiles):
    def get(s):
        pair = (blocks[0, s].astype(F32), blocks[1, s].astype(F32))
        return times(pair, phase[0, s : s + 1, :], -phase[1, s : s + 1, :])

    def put(p, pair):
        pair = times(pair, twist[0, p : p + 1, :], -twist[1, p : p + 1, :])
        rows = slice(p * 16, p * 16 + 16)
        folded[rows, 0:LANES] = pair[0].astype(BF16)
        folded[rows, LANES : 2 * LANES] = pair[1].astype(BF16)

    dft_over_blocks(get, put, work, -1.0)
    flat = mm_nt(dense[...], folded[...]).astype(BF16)
    stacked = jnp.concatenate(
        [
            jnp.concatenate([flat[0:16, 0:256], flat[16:32, 0:256]], axis=1),
            jnp.concatenate([flat[0:16, 256:512], flat[16:32, 256:512]], axis=1),
        ],
        axis=0,
    )
    spread = mm(rep[...], stacked).astype(BF16) * keep[...]
    own = as_bf(iota((512, LANES), 1) // 32 == iota((512, LANES), 0) // TS % CAP)
    tiles[...] = mm(spread, sel[...]).astype(BF16) * own


def tiles_to_columns(tiles, phase, dense, twist, rep_t, sel, keep, work, folded_f32, images):
    spread = mm_nt(tiles[...], sel[...]).astype(BF16) * keep[...]
    stacked = mm(rep_t[...], spread).astype(BF16)
    flat = jnp.concatenate(
        [
            jnp.concatenate([stacked[0:16, 0:256], stacked[16:32, 0:256]], axis=1),
            jnp.concatenate([stacked[0:16, 256:512], stacked[16:32, 256:512]], axis=1),
        ],
        axis=0,
    )
    folded_f32[...] = mm_tn(flat, dense[...])

    def get(p):
        rows = slice(p * 16, p * 16 + 16)
        pair = (folded_f32[rows, 0:LANES], folded_f32[rows, LANES : 2 * LANES])
        return times(pair, twist[0, p : p + 1, :], twist[1, p : p + 1, :])

    def put(s, pair):
        pair = times(pair, phase[0, s : s + 1, :], phase[1, s : s + 1, :])
        images[0, s] = pair[0].astype(BF16)
        images[1, s] = pair[1].astype(BF16)

    dft_over_blocks(get, put, work, 1.0)


VALUES = 8


def unit_circle(turns, total):
    half = jnp.where(turns >= total / 2.0, turns - total, turns) * (math.pi / total)
    sq = half * half
    sine = 1.0 / 6227020800.0
    for term in (-1.0 / 39916800.0, 1.0 / 362880.0, -1.0 / 5040.0, 1.0 / 120.0, -1.0 / 6.0, 1.0):
        sine = sine * sq + term
    sine = sine * half
    cosine = 1.0 / 479001600.0
    for term in (-1.0 / 3628800.0, 1.0 / 40320.0, -1.0 / 720.0, 1.0 / 24.0, -0.5, 1.0):
        cosine = cosine * sq + term
    return 1.0 - 2.0 * sine * sine, 2.0 * sine * cosine


def over_pixels(values):
    return jnp.broadcast_to(values[:, None, :], (8, TS, LANES)).reshape(8 * TS, LANES)


def pack_visibilities(measured, masked, pixels, staged, packed):
    for part in range(4):
        rows = pl.ds(part * 32, 32)
        blocks = pl.ds(part * 8, 8)
        values = []
        for z in range(2):
            value = measured[rows, z, :]
            coarse = value.astype(BF16).astype(F32)
            values += [coarse, value - coarse]
        values.append(masked[rows, :])
        values += [pixels[i, rows, :].astype(F32) for i in range(3)]
        for q in range(VALUES):
            staged[blocks, q * CAP : (q + 1) * CAP, :] = values[q].reshape(8, CAP, LANES)
        packed[blocks] = staged[blocks].astype(BF16)


def visit(tiles, vis, my_tiles):
    pixel = (iota((8 * TS, LANES), 0) % TS).astype(F32)
    square = (pixel - 8.0) * (pixel - 8.0)
    own = (iota((64, LANES), 1) // 32 == iota((64, LANES), 0) // TS).astype(F32)

    for step in range(4):
        def value(q):
            return vis[q * SUBS + step * 8 : q * SUBS + step * 8 + 8, :]

        turns = over_pixels(value(7)) * square
        turns = turns - 256.0 * jnp.floor(turns * (1.0 / 256.0))
        cosine, sine = unit_circle(turns, 256.0)
        row_off = (pixel - over_pixels(value(5))) / kernel_width
        col_off = (pixel - over_pixels(value(6))) / kernel_width
        row_fall = kernel_norm * jnp.exp(-(row_off * row_off))
        col_fall = kernel_norm * jnp.exp(-(col_off * col_off))
        row_re, row_im = (row_fall * cosine).astype(BF16), (-row_fall * sine).astype(BF16)
        upper = jnp.concatenate([row_re, row_im], axis=1)
        lower = jnp.concatenate([-row_im, row_re], axis=1)
        weights = []
        for half in range(2):
            pieces = []
            for slot in range(4):
                src = slice(half * 64 + slot * TS, half * 64 + slot * TS + TS)
                pieces += [upper[src], lower[src]]
            weights.append(jnp.concatenate(pieces, axis=0))
        col_re = (col_fall * cosine).astype(BF16).astype(F32)
        col_im = (-col_fall * sine).astype(BF16).astype(F32)
        first = step * 128
        part = jnp.concatenate(
            [mm(tiles[first + half * 64 : first + half * 64 + 64, :], weights[half]) for half in range(2)],
            axis=0,
        )
        part_re, part_im = part[:, 0:LANES], part[:, LANES : 2 * LANES]
        pred_re = jnp.sum((col_re * part_re - col_im * part_im).reshape(8, TS, LANES), axis=1)
        pred_im = jnp.sum((col_re * part_im + col_im * part_re).reshape(8, TS, LANES), axis=1)
        weight = value(4)
        res_re = over_pixels(weight * (value(0) + value(1) - pred_re))
        res_im = over_pixels(weight * (value(2) + value(3) - pred_im))
        back_re = (col_re * res_re + col_im * res_im).astype(BF16)
        back_im = (col_re * res_im - col_im * res_re).astype(BF16)
        back = jnp.concatenate([back_re, back_im], axis=1)
        for half in range(2):
            grid = mm_nt(back[half * 64 : half * 64 + 64], weights[half]) * own
            my_tiles[first + half * 64 : first + half * 64 + 64, :] = grid.astype(BF16)


def as_bf(condition):
    return condition.astype(F32).astype(BF16)


def iota(shape, dim):
    return lax.broadcasted_iota(jnp.int32, shape, dim)


def masked_weights(weight, counts, masked):
    identity = as_bf(iota((LANES, LANES), 0) == iota((LANES, LANES), 1))
    spread = jnp.broadcast_to(counts[...].astype(F32), (LANES, LANES)).astype(BF16)
    column = mm_nt(identity, spread)
    masked[...] = jnp.where(iota((LANES, LANES), 1).astype(F32) < column, weight[...], 0.0)


def column_phase(facet, offsets, phase):
    mine = jnp.where(iota((1, FACETS), 1) == facet, offsets[...], 0)
    start = jnp.sum(mine.astype(F32), axis=1, keepdims=True).astype(jnp.int32)
    column = iota((SUBS, LANES), 0) * LANES + iota((SUBS, LANES), 1)
    turns = ((column * start) & (LONG - 1)).astype(F32)
    cosine, sine = unit_circle(turns, float(LONG))
    phase[0] = cosine
    phase[1] = sine


def same_pixel(keep):
    for part in range(4):
        rows = slice(part * 128, part * 128 + 128)
        keep[rows, :] = as_bf(iota((128, 512), 0) % TS == iota((128, 512), 1) // TS % TS)


def routing(owners, choice):
    square = (SUBS, SUBS)
    up, across = iota(square, 0), iota(square, 1)
    named = as_bf(owners[...] == up)
    moved = as_bf(across == up % 2 * 16 + up // 2)
    identity = as_bf(up == across)
    earlier = mm(named, as_bf(up < across)).astype(BF16)
    named = mm(named, moved).astype(BF16)
    rank = jnp.sum(named.astype(F32) * mm(earlier, moved), axis=0, keepdims=True)
    rank = mm_nt(identity, jnp.broadcast_to(rank, (LANES, SUBS)).astype(BF16))
    by_tile = mm_nt(identity, named).astype(BF16)
    wide = (SUBS, SUBS * SUBS)
    by_tile = mm(by_tile, as_bf(iota(wide, 1) // SUBS == iota(wide, 0)))
    at_rank = (rank == (iota((SUBS, LANES), 1) % CAP).astype(F32)).astype(F32)
    both = by_tile * jnp.concatenate([at_rank] * 8, axis=1)
    which = iota(wide, 1) % SUBS // CAP
    for q in range(VALUES):
        choice[q * SUBS : (q + 1) * SUBS, :] = jnp.where(which == q, both, 0.0).astype(BF16)


def add_blocks(dst, sources, lo, count):
    def one(step, carry):
        total = sources[0][lo + step].astype(F32)
        for src in sources[1:]:
            total = total + src[lo + step].astype(F32)
        dst[lo + step] = total.astype(BF16)
        return carry

    lax.fori_loop(0, count, one, 0, unroll=4)


def facet_to_strips_kernel(
    strip_hbm, second_hbm, *rest
):
    count = len(SMALL)
    small_hbm, out_hbm, small = rest[:count], rest[count], rest[count + 1 : 2 * count + 1]
    strips_body(strip_hbm, second_hbm, small_hbm, out_hbm, small, *small, *rest[2 * count + 1 :])


def strips_body(
    strip_hbm, second_hbm, small_hbm, out_hbm, small,
    offs, turn, row_win, col_win, first, offsets, owners, measured, weight, pixels, counts,
    dense, twist, rep, rep_t, sel,
    strip, re, im, mid_re, mid_im, wide_re, wide_im, second, keep, mine,
    pair_buf, sums, carry_a, carry_b, from_dn, from_up, total, gathered,
    work, folded, folded_f32, tiles, my_tiles, images, out,
    masked, phase, staged, packed, received, choice, vis,
    load_sem, out_sem,
    pair_s, pair_r, ring_s, ring_r, send_s, rows_r, vis_r, image_r, gath_s, gath_r,
):
    me = lax.axis_index("sub")
    facet = lax.axis_index("facet")
    core, chip = lax.rem(facet, 2), facet // 2
    sib = facet + 1 - 2 * core
    up, dn = lax.rem(facet + 2, FACETS), lax.rem(facet + 6, FACETS)
    opp = lax.rem(facet + 4, FACETS)
    peers = devices_by_distance(me)
    places = wide_rows(peers)

    barrier = pltpu.get_barrier_semaphore()

    def greet(step, carry):
        pl.semaphore_signal(barrier, inc=1, device_id={"sub": lax.rem(me + step, SUBS)}, device_id_type=MESH)
        return carry

    for peer in (sib, up, dn):
        pl.semaphore_signal(barrier, inc=1, device_id={"facet": peer}, device_id_type=MESH)
    lax.fori_loop(1, SUBS, greet, 0)
    quarter = LONG // 4
    loads = [
        pltpu.make_async_copy(
            strip_hbm.at[:, pl.ds(i * quarter, quarter)], strip.at[:, pl.ds(i * quarter, quarter)], load_sem.at[i]
        )
        for i in range(4)
    ]
    second_load = pltpu.make_async_copy(second_hbm, second, load_sem.at[4])
    small_loads = [
        pltpu.make_async_copy(src, dst, load_sem.at[5 + i]) for i, (src, dst) in enumerate(zip(small_hbm, small))
    ]
    for copy in small_loads + loads + [second_load]:
        copy.start()
    for copy in small_loads:
        copy.wait()
    masked_weights(weight, counts, masked)
    pack_visibilities(measured, masked, pixels, staged, packed)
    load_strip(strip, row_win, col_win, loads, re, im)
    second_load.wait()
    spectrum(re, im, mid_re, mid_im, wide_re, wide_im, first, second)
    pl.semaphore_wait(barrier, SUBS + 2)

    def to_facet(src, dst, ssem, rsem, peer):
        return pltpu.make_async_remote_copy(
            src_ref=src, dst_ref=dst, send_sem=ssem, recv_sem=rsem,
            device_id={"facet": peer}, device_id_type=MESH,
        )

    def to_sub(src, dst, ssem, rsem, peer):
        return pltpu.make_async_remote_copy(
            src_ref=src, dst_ref=dst, send_sem=ssem, recv_sem=rsem,
            device_id={"sub": peer}, device_id_type=MESH,
        )

    def others(body):
        def one(step, carry):
            body(lax.rem(me + step, SUBS))
            return carry

        lax.fori_loop(1, SUBS, one, 0)

    def vis_copy(peer, slot, sem):
        return to_sub(packed.at[peer], received.at[slot], send_s.at[0, sem], vis_r.at[slot], peer)

    def send_vis():
        for i, peer in enumerate(peers[:-1]):
            vis_copy(peer, me, i).start()
        received[me] = packed[me]

    def rows_copy(half, block, peer, slot):
        return to_sub(
            total.at[half, :, block], gathered.at[:, slot], send_s.at[1, half * 16 + block], rows_r.at[slot], peer
        )

    def send_rows(half):
        for block in range(16 - half):
            rows_copy(half, block, peers[half * 16 + block], me).start()

    def image_copy(i, peer):
        spot = SEEN_FROM[i]
        return to_sub(
            images.at[:, peer], out.at[facet, spot // 16, :, spot % 16], send_s.at[2, i], image_r.at[spot], peer
        )

    def image_arrives(spot):
        to_sub(
            images.at[:, 0], out.at[facet, lax.div(spot, 16), :, lax.rem(spot, 16)],
            send_s.at[2, 0], image_r.at[spot], peers[0],
        ).wait_recv()

    def cut(which):
        cut_rows(which, facet, offs, turn, places, wide_re, wide_im, mine)

    pairs = {}
    for half in range(2):
        for hop in (2, 1, 3, 0):
            target = 2 * lax.rem(chip + hop, 4) + 1 - core
            if half == 0:
                cut(target)
            pairs[half, hop] = to_facet(
                mine.at[target, half], pair_buf.at[hop, half],
                pair_s.at[half, hop], pair_r.at[half, hop], sib,
            )
            pairs[half, hop].start()

    def merge_pair(half, hop):
        pairs[half, hop].wait_recv()
        target = 2 * lax.rem(chip + hop, 4) + core
        for plane in range(2):
            add_blocks(
                sums.at[hop, half, plane], [mine.at[target, half, plane], pair_buf.at[hop, half, plane]], 0, 16
            )

    rings = [
        [
            to_facet(src, dst, ring_s.at[half, i], ring_r.at[half, i], peer)
            for i, (src, dst, peer) in enumerate((
                (sums.at[2, half, 0], carry_a.at[half], up),
                (sums.at[2, half, 1], carry_b.at[half], dn),
                (sums.at[1, half, 1], from_dn.at[half, 1], up),
                (sums.at[3, half, 0], from_up.at[half, 0], dn),
                (sums.at[1, half, 0], from_dn.at[half, 0], up),
                (sums.at[3, half, 1], from_up.at[half, 1], dn),
            ))
        ]
        for half in range(2)
    ]

    def merge_ring(half):
        ring = rings[half]
        ring[0].wait_recv()
        add_blocks(sums.at[1, half, 0], [sums.at[1, half, 0], carry_a.at[half]], 0, 16)
        ring[4].start()
        ring[1].wait_recv()
        add_blocks(sums.at[3, half, 1], [sums.at[3, half, 1], carry_b.at[half]], 0, 16)
        ring[5].start()

    def finish(half):
        pairs[half, 0].wait_recv()
        own_target = 2 * chip + core
        for plane, steps in ((0, (3, 4)), (1, (2, 5))):
            for step in steps:
                rings[half][step].wait_recv()
            add_blocks(
                total.at[half, plane],
                [
                    ref.at[half, plane]
                    for ref in (mine.at[own_target], pair_buf.at[0], from_dn, from_up)
                ],
                0, 16,
            )

    cut(2 * lax.rem(chip + 2, 4) + core)
    merge_pair(0, 2)
    rings[0][0].start()
    rings[0][1].start()
    cut(2 * lax.rem(chip + 1, 4) + core)
    merge_pair(0, 1)
    rings[0][2].start()
    cut(2 * lax.rem(chip + 3, 4) + core)
    merge_pair(0, 3)
    rings[0][3].start()
    send_vis()
    merge_pair(1, 2)
    rings[1][0].start()
    rings[1][1].start()
    cut(2 * chip + core)
    merge_pair(1, 1)
    merge_pair(1, 3)
    column_phase(facet, offsets, phase)
    merge_ring(0)
    rings[1][2].start()
    rings[1][3].start()
    routing(owners, choice)
    same_pixel(keep)
    merge_ring(1)
    finish(0)
    send_rows(0)
    finish(1)
    send_rows(1)
    for plane in range(2):
        gathered[plane, me] = total[1, plane, 15]
    others(lambda peer: vis_copy(peer, peer, 0).wait_recv())
    vis[...] = mm(choice[...], received[...].reshape(SUBS * SUBS, LANES))
    others(lambda peer: rows_copy(0, 0, peer, peer).wait_recv())
    columns_to_tiles(gathered, phase, dense, twist, rep, sel, keep, work, folded, tiles)
    visit(tiles, vis, my_tiles)
    tiles_to_columns(my_tiles, phase, dense, twist, rep_t, sel, keep, work, folded_f32, images)

    for i, peer in enumerate(peers[:-1]):
        image_copy(i, peer).start()
    for plane in range(2):
        out[facet, 1, plane, 15] = images[plane, me]
    for copy in rings[0] + rings[1] + list(pairs.values()):
        copy.wait_send()

    def drain(kind, src):
        def one(step, carry):
            to_sub(src, src, send_s.at[kind, step], vis_r.at[0], sib).wait_send()
            return carry

        lax.fori_loop(0, SUBS - 1, one, 0)

    drain(0, packed.at[0])
    drain(1, total.at[0, :, 0])
    stores = []
    sends = []

    def store(where):
        copy = pltpu.make_async_copy(out.at[where], out_hbm.at[where], out_sem.at[len(stores)])
        copy.start()
        stores.append(copy)

    def share(half, index, where, peer):
        ref = out.at[where]
        return to_facet(ref, ref, gath_s.at[half, index], gath_r.at[half, index], peer)

    def send(half, index, where, peer):
        sends.append(share(half, index, where, peer))
        sends[-1].start()

    def arrives(half, index, where):
        share(half, index, where, sib).wait_recv()

    def one_image(spot, carry):
        image_arrives(spot)
        return carry

    def own_half(half):
        lax.fori_loop(16 * half, 16 + 15 * half, one_image, 0)
        own = (facet, half)
        send(half, 0, own, up)
        send(half, 1, own, dn)
        send(half, 2, own, sib)
        store(own)

    def onward(half):
        arrives(half, 0, (dn, half))
        send(half, 3, (dn, half, 0), up)
        send(half, 5, (dn, half), sib)
        store((dn, half))
        arrives(half, 1, (up, half))
        send(half, 4, (up, half, 1), dn)
        send(half, 6, (up, half), sib)
        store((up, half))

    def opposite(half):
        arrives(half, 3, (opp, half, 0))
        send(half, 7, (opp, half, 0), sib)
        store((opp, half, 0))
        arrives(half, 4, (opp, half, 1))
        send(half, 8, (opp, half, 1), sib)
        store((opp, half, 1))

    other = 1 - 2 * core
    own_half(1)
    own_half(0)
    drain(2, images.at[:, 0])
    onward(1)
    onward(0)
    opposite(1)
    for half in (1, 0):
        arrives(half, 2, (sib, half))
        store((sib, half))
        arrives(half, 5, (dn + other, half))
        store((dn + other, half))
        arrives(half, 6, (up + other, half))
        store((up + other, half))
    opposite(0)
    for half in (1, 0):
        arrives(half, 7, (opp + other, half, 0))
        store((opp + other, half, 0))
        arrives(half, 8, (opp + other, half, 1))
        store((opp + other, half, 1))
    for copy in sends:
        copy.wait_send()
    for copy in stores:
        copy.wait()


def vmem_specs(count):
    return [pl.BlockSpec(memory_space=pltpu.VMEM)] * count


def smem_specs(count):
    return [pl.BlockSpec(memory_space=pltpu.SMEM)] * count


BIG = 60 * 1024 * 1024
STRIPS = (FACETS, 2, 2, 16, 16, LANES)
WIDE_ROWS = 66 * 128


def any_specs(count):
    return [pl.BlockSpec(memory_space=pl.ANY)] * count


def row_scratch():
    narrow, wide = pltpu.VMEM((RADIX * PITCH, LANES), F32), pltpu.VMEM((WIDE_ROWS, LANES), F32)
    return [narrow] * 4 + [wide] * 2


TABLE = (RADIX, 2 * RADIX, 2 * RADIX)


def backward_call(shape):
    return pl.pallas_call(
        backward_kernel,
        out_shape=jax.ShapeDtypeStruct(shape, BF16),
        in_specs=any_specs(7),
        out_specs=pl.BlockSpec(memory_space=pl.ANY),
        scratch_shapes=[(pltpu.SMEM if i < 2 else pltpu.VMEM)(*item) for i, item in enumerate(SMALL[:5])]
        + [pltpu.SemaphoreType.DMA((5,))]
        + row_scratch()
        + [
            pltpu.VMEM(STRIPS, BF16),
            pltpu.VMEM(TABLE, BF16),
            pltpu.VMEM(shape, BF16),
            pltpu.SemaphoreType.DMA,
            pltpu.SemaphoreType.DMA((FACETS,)),
            pltpu.SemaphoreType.DMA((4,)),
        ],
        compiler_params=pltpu.CompilerParams(vmem_limit_bytes=BIG),
    )


def strips_call(shape):
    block = (2, SUBS, 16, LANES)
    halves = (2, 2, 16, 16, LANES)
    half = (2, 16, 16, LANES)
    values = (SUBS, VALUES * CAP, LANES)
    vm = pltpu.VMEM
    dma = pltpu.SemaphoreType.DMA
    return pl.pallas_call(
        facet_to_strips_kernel,
        out_shape=jax.ShapeDtypeStruct(STRIPS, BF16),
        in_specs=any_specs(2 + len(SMALL)),
        out_specs=pl.BlockSpec(memory_space=pl.ANY),
        scratch_shapes=[(pltpu.SMEM if i < 2 else vm)(*item) for i, item in enumerate(SMALL)]
        + [vm(shape, BF16)]
        + row_scratch()
        + [
            vm(TABLE, BF16), vm((512, 512), BF16), vm(STRIPS, BF16),
            vm((4,) + halves, BF16), vm((4,) + halves, BF16), vm(half, BF16), vm(half, BF16),
            vm(halves, BF16), vm(halves, BF16), vm(halves, BF16), vm(block, BF16),
            vm((SUBS, 2, 16, LANES), F32), vm((512, 256), BF16), vm((512, 256), F32),
            vm((512, LANES), BF16), vm((512, LANES), BF16), vm(block, BF16), vm(STRIPS, BF16),
            vm((LANES, LANES), F32), vm((2, SUBS, LANES), F32),
            vm(values, F32), vm(values, BF16), vm(values, BF16),
            vm((VALUES * SUBS, SUBS * SUBS), BF16), vm((VALUES * SUBS, LANES), F32),
            dma((5 + len(SMALL),)), dma((20,)),
            dma((2, 4)), dma((2, 4)), dma((2, 6)), dma((2, 6)), dma((3, SUBS)),
            dma((SUBS,)), dma((SUBS,)), dma((SUBS,)), dma((2, 9)), dma((2, 9)),
        ],
        compiler_params=pltpu.CompilerParams(
            vmem_limit_bytes=BIG, collective_id=0, has_side_effects=True
        ),
    )


def per_device(
    facet_strips, row_window, col_window, row_offsets, col_offsets,
    tile_owner, measured, vis_weight, uvw_pixels, vis_count,
):
    first, second = row_tables()
    dense, twist, rep, rep_t, sel = col_tables()
    eighth = 2 * np.pi * np.arange(FACETS) / FACETS
    turn = jnp.asarray(np.stack([np.cos(eighth), np.sin(eighth)]), F32)
    row_win = row_window.reshape(LONG // LANES, LANES)
    col_win = col_window.reshape(1, LANES)
    strips = strips_call(facet_strips.shape)(
        facet_strips, second, row_offsets, turn, row_win, col_win, first,
        col_offsets.reshape(1, FACETS), tile_owner.reshape(1, SUBS), measured[0, 0],
        vis_weight[0, 0], jnp.transpose(uvw_pixels[0, 0], (1, 0, 2)), vis_count.reshape(1, LANES),
        dense, twist, rep, rep_t, sel,
    )
    return backward_call(facet_strips.shape)(
        row_offsets, turn, row_win, col_win, first, strips, second
    )


def solution(mesh):
    in_specs = (
        P(None, "facet", "sub"),
        P(),
        P("sub"),
        P(),
        P(),
        P("sub", "facet", None, None),
        P("facet", "sub", None, None, None),
        P("facet", "sub", None, None),
        P("facet", "sub", None, None, None),
        P("facet", "sub", None),
    )
    return jax.shard_map(
        per_device, mesh=mesh, in_specs=in_specs, out_specs=P(None, "facet", "sub"), check_vma=False
    )
```

```python
import math

import jax
import jax.numpy as jnp
import numpy as np
from jax import lax
from jax.experimental import pallas as pl
from jax.experimental.pallas import tpu as pltpu
from jax.sharding import PartitionSpec as P

SG = 512
RADIX = 64
TS = 16
LONG = 4096
SUBS = 32
FACETS = 8
CAP = 4
LANES = 128
MESH = pl.DeviceIdType.MESH
F32 = jnp.float32
BF16 = jnp.bfloat16

kernel_width = 2.5
kernel_norm = 0.565


def as_real(theta):
    cosine, sine = np.cos(theta), np.sin(theta)
    return np.block([[cosine, sine], [-sine, cosine]])


def row_tables():
    idx = np.arange(RADIX)
    first = as_real(2 * np.pi * (np.outer(idx, idx) % RADIX) / RADIX)
    second = [
        as_real(2 * np.pi * (np.outer(k1 + RADIX * idx, idx) % LONG) / LONG) / RADIX
        for k1 in range(RADIX)
    ]
    return jnp.asarray(first, BF16), jnp.asarray(np.stack(second), BF16)


def col_tables():
    high = np.outer(np.arange(16), np.arange(LANES)) % LANES
    dense = as_real(2 * np.pi * high / LANES)
    low = 2 * np.pi * np.outer(np.arange(SUBS), np.arange(LANES)) / LONG
    twist = np.stack([np.cos(low), np.sin(low)]) / 64.0
    rep = np.zeros((512, 32))
    rep[np.arange(512), np.arange(512) // 16] = 1
    sel = np.zeros((2, 16, 16, 4, 2, 16))
    for z in range(2):
        for r in range(16):
            sel[z, :, r, :, z, r] = 1
    sel = sel.reshape(512, 128)
    return (
        jnp.asarray(dense, BF16),
        jnp.asarray(twist, F32),
        jnp.asarray(rep, BF16),
        jnp.asarray(rep.T, BF16),
        jnp.asarray(sel, BF16),
    )


def mm(first, other):
    return jnp.dot(first, other, preferred_element_type=F32)


def mm_nt(first, other):
    return lax.dot_general(first, other, (((1,), (1,)), ((), ())), preferred_element_type=F32)


def mm_tn(first, other):
    return lax.dot_general(first, other, (((0,), (0,)), ((), ())), preferred_element_type=F32)


STEPS = sorted(
    ((i, j) for i in range(4) for j in range(8)),
    key=lambda ij: -(min(ij[0], 4 - ij[0]) + min(ij[1], 8 - ij[1])),
)
SEEN_FROM = [STEPS.index(((4 - i) % 4, (8 - j) % 8)) for i, j in STEPS]


def devices_by_distance(me):
    x, z = lax.div(me, 8), lax.rem(me, 8)
    x_at = [lax.rem(x + i, 4) * 8 for i in range(4)]
    z_at = [lax.rem(z + i, 8) for i in range(8)]
    return [x_at[i] + z_at[j] for i, j in STEPS]


def wide_rows(peers):
    return [lax.div(peer, 4) * WIDE + lax.rem(peer, 4) * 16 for peer in peers]


PITCH = RADIX + 1
WIDE = 2 * RADIX + 1


def strided(index, pitch):
    return pl.ds(index, RADIX, stride=pitch)


def transform_rows(fetch, mid_re, mid_im, first, second, put):
    def stage_a(step, carry):
        parts = []
        for u in range(2):
            real, imag = fetch(2 * step + u)
            parts.append(jnp.concatenate([real, imag], axis=0).astype(BF16))
        res = mm(first[...], jnp.concatenate(parts, axis=1))
        for u in range(2):
            rows = strided(2 * step + u, PITCH)
            mid_re[rows, :] = res[:RADIX, u * LANES : (u + 1) * LANES]
            mid_im[rows, :] = res[RADIX:, u * LANES : (u + 1) * LANES]
        return carry

    lax.fori_loop(0, RADIX // 2, stage_a, 0, unroll=16)

    def stage_b(step, carry):
        rows = pl.ds(step * PITCH, RADIX)
        block = jnp.concatenate([mid_re[rows, :], mid_im[rows, :]], axis=0).astype(BF16)
        res = mm(second[step], block)
        put(step, res[:RADIX], res[RADIX:])
        return carry

    lax.fori_loop(0, RADIX, stage_b, 0, unroll=32)


SMALL = (
    ((FACETS,), jnp.int32), ((2, FACETS), F32), ((SUBS, LANES), F32), ((1, LANES), F32),
    ((LANES, LANES), BF16), ((1, FACETS), jnp.int32), ((1, SUBS), jnp.int32),
    ((LANES, 2, LANES), F32), ((LANES, LANES), F32), ((3, LANES, LANES), jnp.int32), ((1, LANES), jnp.int32),
    ((SUBS, 2 * LANES), BF16), ((2, SUBS, LANES), F32), ((512, SUBS), BF16), ((SUBS, 512), BF16),
    ((512, LANES), BF16),
)


def load_strip(strip, row_win, col_win, loads, re, im):
    row_win, scale = row_win[...].T, col_win[...]
    for block in range(RADIX):
        if block % (RADIX // len(loads)) == 0:
            loads[block * len(loads) // RADIX].wait()
        half = block % 2 * RADIX
        window = row_win[half : half + RADIX, block // 2 : block // 2 + 1] * scale
        rows, src = pl.ds(block * PITCH, RADIX), pl.ds(block * RADIX, RADIX)
        re[rows, :] = strip[0, src, :].astype(F32) * window
        im[rows, :] = strip[1, src, :].astype(F32) * window


def spectrum(re, im, mid_re, mid_im, wide_re, wide_im, first, second):
    def fetch(index):
        rows = strided(index, PITCH)
        return re[rows, :], im[rows, :]

    def put(index, real, imag):
        here, before = strided(WIDE + index, WIDE), strided(RADIX + index, WIDE)
        wide_re[here, :] = real
        wide_im[here, :] = imag
        wide_re[before, :] = real
        wide_im[before, :] = imag

    transform_rows(fetch, mid_re, mid_im, first, second, put)


def cut_rows(which, facet, offs, turn, places, wide_re, wide_im, out):
    base = offs[which]
    index = (facet * base) & (FACETS - 1)
    cosine, sine = turn[0, index], turn[1, index]
    start = WIDE + base // RADIX * WIDE + base % RADIX
    for i, place in enumerate(places):
        rows = pl.ds(start + place, 16)
        real, imag = wide_re[rows, :], wide_im[rows, :]
        out[which, i // 16, 0, i % 16] = (cosine * real + sine * imag).astype(BF16)
        out[which, i // 16, 1, i % 16] = (cosine * imag - sine * real).astype(BF16)


def backward_kernel(
    offs_hbm, turn_hbm, row_hbm, col_hbm, first_hbm, strips_hbm, second_hbm, out_hbm,
    offs, turn, row_win, col_win, first, small_sem, re, im, mid_re, mid_im, wide_re, wide_im, strips, second, out, second_sem, strip_sem, out_sem,
):
    def load(which):
        return pltpu.make_async_copy(strips_hbm.at[which], strips.at[which], strip_sem.at[which])

    pairs = zip((offs_hbm, turn_hbm, row_hbm, col_hbm, first_hbm), (offs, turn, row_win, col_win, first))
    small = [pltpu.make_async_copy(src, dst, small_sem.at[i]) for i, (src, dst) in enumerate(pairs)]
    for copy in small:
        copy.start()
    for which in range(FACETS):
        load(which).start()
    table = pltpu.make_async_copy(second_hbm, second, second_sem)
    table.start()
    facet = lax.axis_index("facet")

    def clear(step, carry):
        rows = pl.ds(pl.multiple_of(step * 128, 128), 128)
        wide_re[rows, :] = jnp.zeros((128, LANES), F32)
        wide_im[rows, :] = jnp.zeros((128, LANES), F32)
        return carry

    lax.fori_loop(0, WIDE_ROWS // 128, clear, 0, unroll=2)
    for copy in small:
        copy.wait()

    places = wide_rows(devices_by_distance(lax.axis_index("sub")))

    def place(which, carry):
        load(which).wait()
        base = offs[which]
        index = (facet * base) & (FACETS - 1)
        cosine, sine = turn[0, index], turn[1, index]
        start = WIDE + base // RADIX * WIDE + base % RADIX
        for i, place_at in enumerate(places):
            rows = pl.ds(start + place_at, 16)
            real = strips[which, i // 16, 0, i % 16].astype(F32)
            imag = strips[which, i // 16, 1, i % 16].astype(F32)
            wide_re[rows, :] = wide_re[rows, :] + (cosine * real - sine * imag)
            wide_im[rows, :] = wide_im[rows, :] - (sine * real + cosine * imag)
        return carry

    lax.fori_loop(0, FACETS, place, 0)
    table.wait()

    def fetch(index):
        here, before = strided(WIDE + index, WIDE), strided(RADIX + index, WIDE)
        return wide_re[here, :] + wide_re[before, :], wide_im[here, :] + wide_im[before, :]

    def put(index, real, imag):
        rows = strided(index, PITCH)
        re[rows, :] = real
        im[rows, :] = imag

    transform_rows(fetch, mid_re, mid_im, first, second, put)
    row_win, scale = row_win[...].T, col_win[...]
    quarter = LONG // 4
    copies = []
    for block in range(RADIX):
        half = block % 2 * RADIX
        window = row_win[half : half + RADIX, block // 2 : block // 2 + 1] * scale
        rows, dst = pl.ds(block * PITCH, RADIX), pl.ds(block * RADIX, RADIX)
        out[0, dst, :] = (re[rows, :] * window).astype(BF16)
        out[1, dst, :] = (im[rows, :] * -window).astype(BF16)
        if block % 16 == 15:
            done = pl.ds(block // 16 * quarter, quarter)
            copies.append(
                pltpu.make_async_copy(out.at[:, done], out_hbm.at[:, done], out_sem.at[block // 16])
            )
            copies[-1].start()
    for copy in copies:
        copy.wait()


def times(pair, cosine, sine):
    return (pair[0] * cosine - pair[1] * sine, pair[0] * sine + pair[1] * cosine)


def times_unit(pair, num, den, sign):
    num = num % den
    if num == 0:
        return pair
    if 4 * num == den:
        return (-sign * pair[1], sign * pair[0])
    if 2 * num == den:
        return (-pair[0], -pair[1])
    angle = 2 * math.pi * num / den
    return times(pair, math.cos(angle), sign * math.sin(angle))


def small_dft(items, sign):
    count = len(items)
    if count == 1:
        return items
    even = small_dft(items[0::2], sign)
    odd = small_dft(items[1::2], sign)
    odd = [times_unit(odd[i], i, count, sign) for i in range(count // 2)]
    low = [(a[0] + b[0], a[1] + b[1]) for a, b in zip(even, odd)]
    high = [(a[0] - b[0], a[1] - b[1]) for a, b in zip(even, odd)]
    return low + high


def dft_over_blocks(get, put, work, sign):
    for lo in range(8):
        items = small_dft([get(lo + 8 * hi) for hi in range(4)], sign)
        for p_lo in range(4):
            value = times_unit(items[p_lo], lo * p_lo, SUBS, sign)
            work[p_lo * 8 + lo, 0] = value[0]
            work[p_lo * 8 + lo, 1] = value[1]
    for p_lo in range(4):
        items = small_dft([(work[p_lo * 8 + lo, 0], work[p_lo * 8 + lo, 1]) for lo in range(8)], sign)
        for p_hi in range(8):
            put(p_lo + 4 * p_hi, items[p_hi])


def columns_to_tiles(blocks, phase, dense, twist, rep, sel, keep, work, folded, tiles):
    def get(s):
        pair = (blocks[0, s].astype(F32), blocks[1, s].astype(F32))
        return times(pair, phase[0, s : s + 1, :], -phase[1, s : s + 1, :])

    def put(p, pair):
        pair = times(pair, twist[0, p : p + 1, :], -twist[1, p : p + 1, :])
        rows = slice(p * 16, p * 16 + 16)
        folded[rows, 0:LANES] = pair[0].astype(BF16)
        folded[rows, LANES : 2 * LANES] = pair[1].astype(BF16)

    dft_over_blocks(get, put, work, -1.0)
    flat = mm_nt(dense[...], folded[...]).astype(BF16)
    stacked = jnp.concatenate(
        [
            jnp.concatenate([flat[0:16, 0:256], flat[16:32, 0:256]], axis=1),
            jnp.concatenate([flat[0:16, 256:512], flat[16:32, 256:512]], axis=1),
        ],
        axis=0,
    )
    spread = mm(rep[...], stacked).astype(BF16) * keep[...]
    own = as_bf(iota((512, LANES), 1) // 32 == iota((512, LANES), 0) // TS % CAP)
    tiles[...] = mm(spread, sel[...]).astype(BF16) * own


def tiles_to_columns(tiles, phase, dense, twist, rep_t, sel, keep, work, folded_f32, images):
    spread = mm_nt(tiles[...], sel[...]).astype(BF16) * keep[...]
    stacked = mm(rep_t[...], spread).astype(BF16)
    flat = jnp.concatenate(
        [
            jnp.concatenate([stacked[0:16, 0:256], stacked[16:32, 0:256]], axis=1),
            jnp.concatenate([stacked[0:16, 256:512], stacked[16:32, 256:512]], axis=1),
        ],
        axis=0,
    )
    folded_f32[...] = mm_tn(flat, dense[...])

    def get(p):
        rows = slice(p * 16, p * 16 + 16)
        pair = (folded_f32[rows, 0:LANES], folded_f32[rows, LANES : 2 * LANES])
        return times(pair, twist[0, p : p + 1, :], twist[1, p : p + 1, :])

    def put(s, pair):
        pair = times(pair, phase[0, s : s + 1, :], phase[1, s : s + 1, :])
        images[0, s] = pair[0].astype(BF16)
        images[1, s] = pair[1].astype(BF16)

    dft_over_blocks(get, put, work, 1.0)


VALUES = 8


def unit_circle(turns, total):
    half = jnp.where(turns >= total / 2.0, turns - total, turns) * (math.pi / total)
    sq = half * half
    sine = 1.0 / 6227020800.0
    for term in (-1.0 / 39916800.0, 1.0 / 362880.0, -1.0 / 5040.0, 1.0 / 120.0, -1.0 / 6.0, 1.0):
        sine = sine * sq + term
    sine = sine * half
    cosine = 1.0 / 479001600.0
    for term in (-1.0 / 3628800.0, 1.0 / 40320.0, -1.0 / 720.0, 1.0 / 24.0, -0.5, 1.0):
        cosine = cosine * sq + term
    return 1.0 - 2.0 * sine * sine, 2.0 * sine * cosine


def over_pixels(values):
    return jnp.broadcast_to(values[:, None, :], (8, TS, LANES)).reshape(8 * TS, LANES)


def pack_visibilities(measured, masked, pixels, staged, packed):
    for part in range(4):
        rows = pl.ds(part * 32, 32)
        blocks = pl.ds(part * 8, 8)
        values = []
        for z in range(2):
            value = measured[rows, z, :]
            coarse = value.astype(BF16).astype(F32)
            values += [coarse, value - coarse]
        values.append(masked[rows, :])
        values += [pixels[i, rows, :].astype(F32) for i in range(3)]
        for q in range(VALUES):
            staged[blocks, q * CAP : (q + 1) * CAP, :] = values[q].reshape(8, CAP, LANES)
        packed[blocks] = staged[blocks].astype(BF16)


def visit(tiles, vis, my_tiles):
    pixel = (iota((8 * TS, LANES), 0) % TS).astype(F32)
    square = (pixel - 8.0) * (pixel - 8.0)
    own = (iota((64, LANES), 1) // 32 == iota((64, LANES), 0) // TS).astype(F32)

    for step in range(4):
        def value(q):
            return vis[q * SUBS + step * 8 : q * SUBS + step * 8 + 8, :]

        turns = over_pixels(value(7)) * square
        turns = turns - 256.0 * jnp.floor(turns * (1.0 / 256.0))
        cosine, sine = unit_circle(turns, 256.0)
        row_off = (pixel - over_pixels(value(5))) / kernel_width
        col_off = (pixel - over_pixels(value(6))) / kernel_width
        row_fall = kernel_norm * jnp.exp(-(row_off * row_off))
        col_fall = kernel_norm * jnp.exp(-(col_off * col_off))
        row_re, row_im = (row_fall * cosine).astype(BF16), (-row_fall * sine).astype(BF16)
        upper = jnp.concatenate([row_re, row_im], axis=1)
        lower = jnp.concatenate([-row_im, row_re], axis=1)
        weights = []
        for half in range(2):
            pieces = []
            for slot in range(4):
                src = slice(half * 64 + slot * TS, half * 64 + slot * TS + TS)
                pieces += [upper[src], lower[src]]
            weights.append(jnp.concatenate(pieces, axis=0))
        col_re = (col_fall * cosine).astype(BF16).astype(F32)
        col_im = (-col_fall * sine).astype(BF16).astype(F32)
        first = step * 128
        part = jnp.concatenate(
            [mm(tiles[first + half * 64 : first + half * 64 + 64, :], weights[half]) for half in range(2)],
            axis=0,
        )
        part_re, part_im = part[:, 0:LANES], part[:, LANES : 2 * LANES]
        pred_re = jnp.sum((col_re * part_re - col_im * part_im).reshape(8, TS, LANES), axis=1)
        pred_im = jnp.sum((col_re * part_im + col_im * part_re).reshape(8, TS, LANES), axis=1)
        weight = value(4)
        res_re = over_pixels(weight * (value(0) + value(1) - pred_re))
        res_im = over_pixels(weight * (value(2) + value(3) - pred_im))
        back_re = (col_re * res_re + col_im * res_im).astype(BF16)
        back_im = (col_re * res_im - col_im * res_re).astype(BF16)
        back = jnp.concatenate([back_re, back_im], axis=1)
        for half in range(2):
            grid = mm_nt(back[half * 64 : half * 64 + 64], weights[half]) * own
            my_tiles[first + half * 64 : first + half * 64 + 64, :] = grid.astype(BF16)


def as_bf(condition):
    return condition.astype(F32).astype(BF16)


def iota(shape, dim):
    return lax.broadcasted_iota(jnp.int32, shape, dim)


def masked_weights(weight, counts, masked):
    identity = as_bf(iota((LANES, LANES), 0) == iota((LANES, LANES), 1))
    spread = jnp.broadcast_to(counts[...].astype(F32), (LANES, LANES)).astype(BF16)
    column = mm_nt(identity, spread)
    masked[...] = jnp.where(iota((LANES, LANES), 1).astype(F32) < column, weight[...], 0.0)


def column_phase(facet, offsets, phase):
    mine = jnp.where(iota((1, FACETS), 1) == facet, offsets[...], 0)
    start = jnp.sum(mine.astype(F32), axis=1, keepdims=True).astype(jnp.int32)
    column = iota((SUBS, LANES), 0) * LANES + iota((SUBS, LANES), 1)
    turns = ((column * start) & (LONG - 1)).astype(F32)
    cosine, sine = unit_circle(turns, float(LONG))
    phase[0] = cosine
    phase[1] = sine


def same_pixel(keep):
    for part in range(4):
        rows = slice(part * 128, part * 128 + 128)
        keep[rows, :] = as_bf(iota((128, 512), 0) % TS == iota((128, 512), 1) // TS % TS)


def routing(owners, choice):
    square = (SUBS, SUBS)
    up, across = iota(square, 0), iota(square, 1)
    named = as_bf(owners[...] == up)
    moved = as_bf(across == up % 2 * 16 + up // 2)
    identity = as_bf(up == across)
    earlier = mm(named, as_bf(up < across)).astype(BF16)
    named = mm(named, moved).astype(BF16)
    rank = jnp.sum(named.astype(F32) * mm(earlier, moved), axis=0, keepdims=True)
    rank = mm_nt(identity, jnp.broadcast_to(rank, (LANES, SUBS)).astype(BF16))
    by_tile = mm_nt(identity, named).astype(BF16)
    wide = (SUBS, SUBS * SUBS)
    by_tile = mm(by_tile, as_bf(iota(wide, 1) // SUBS == iota(wide, 0)))
    at_rank = (rank == (iota((SUBS, LANES), 1) % CAP).astype(F32)).astype(F32)
    both = by_tile * jnp.concatenate([at_rank] * 8, axis=1)
    which = iota(wide, 1) % SUBS // CAP
    for q in range(VALUES):
        choice[q * SUBS : (q + 1) * SUBS, :] = jnp.where(which == q, both, 0.0).astype(BF16)


def add_blocks(dst, sources, lo, count):
    def one(step, carry):
        total = sources[0][lo + step].astype(F32)
        for src in sources[1:]:
            total = total + src[lo + step].astype(F32)
        dst[lo + step] = total.astype(BF16)
        return carry

    lax.fori_loop(0, count, one, 0, unroll=4)


def facet_to_strips_kernel(
    strip_hbm, second_hbm, *rest
):
    count = len(SMALL)
    small_hbm, out_hbm, small = rest[:count], rest[count], rest[count + 1 : 2 * count + 1]
    strips_body(strip_hbm, second_hbm, small_hbm, out_hbm, small, *small, *rest[2 * count + 1 :])


def strips_body(
    strip_hbm, second_hbm, small_hbm, out_hbm, small,
    offs, turn, row_win, col_win, first, offsets, owners, measured, weight, pixels, counts,
    dense, twist, rep, rep_t, sel,
    strip, re, im, mid_re, mid_im, wide_re, wide_im, second, keep, mine,
    pair_buf, sums, carry_a, carry_b, from_dn, from_up, total, gathered,
    work, folded, folded_f32, tiles, my_tiles, images, out,
    masked, phase, staged, packed, received, choice, vis,
    load_sem, out_sem,
    pair_s, pair_r, ring_s, ring_r, send_s, rows_r, vis_r, image_r, gath_s, gath_r,
):
    me = lax.axis_index("sub")
    facet = lax.axis_index("facet")
    core, chip = lax.rem(facet, 2), facet // 2
    sib = facet + 1 - 2 * core
    up, dn = lax.rem(facet + 2, FACETS), lax.rem(facet + 6, FACETS)
    opp = lax.rem(facet + 4, FACETS)
    peers = devices_by_distance(me)
    places = wide_rows(peers)

    barrier = pltpu.get_barrier_semaphore()

    def greet(step, carry):
        pl.semaphore_signal(barrier, inc=1, device_id={"sub": lax.rem(me + step, SUBS)}, device_id_type=MESH)
        return carry

    for peer in (sib, up, dn):
        pl.semaphore_signal(barrier, inc=1, device_id={"facet": peer}, device_id_type=MESH)
    lax.fori_loop(1, SUBS, greet, 0)
    quarter = LONG // 4
    loads = [
        pltpu.make_async_copy(
            strip_hbm.at[:, pl.ds(i * quarter, quarter)], strip.at[:, pl.ds(i * quarter, quarter)], load_sem.at[i]
        )
        for i in range(4)
    ]
    second_load = pltpu.make_async_copy(second_hbm, second, load_sem.at[4])
    small_loads = [
        pltpu.make_async_copy(src, dst, load_sem.at[5 + i]) for i, (src, dst) in enumerate(zip(small_hbm, small))
    ]
    for copy in small_loads + loads + [second_load]:
        copy.start()
    for copy in small_loads:
        copy.wait()
    masked_weights(weight, counts, masked)
    pack_visibilities(measured, masked, pixels, staged, packed)
    load_strip(strip, row_win, col_win, loads, re, im)
    second_load.wait()
    spectrum(re, im, mid_re, mid_im, wide_re, wide_im, first, second)
    pl.semaphore_wait(barrier, SUBS + 2)

    def to_facet(src, dst, ssem, rsem, peer):
        return pltpu.make_async_remote_copy(
            src_ref=src, dst_ref=dst, send_sem=ssem, recv_sem=rsem,
            device_id={"facet": peer}, device_id_type=MESH,
        )

    def to_sub(src, dst, ssem, rsem, peer):
        return pltpu.make_async_remote_copy(
            src_ref=src, dst_ref=dst, send_sem=ssem, recv_sem=rsem,
            device_id={"sub": peer}, device_id_type=MESH,
        )

    def others(body):
        def one(step, carry):
            body(lax.rem(me + step, SUBS))
            return carry

        lax.fori_loop(1, SUBS, one, 0)

    def vis_copy(peer, slot, sem):
        return to_sub(packed.at[peer], received.at[slot], send_s.at[0, sem], vis_r.at[slot], peer)

    def send_vis():
        for i, peer in enumerate(peers[:-1]):
            vis_copy(peer, me, i).start()
        received[me] = packed[me]

    def rows_copy(half, block, peer, slot):
        return to_sub(
            total.at[half, :, block], gathered.at[:, slot], send_s.at[1, half * 16 + block], rows_r.at[slot], peer
        )

    def send_rows(half):
        for block in range(16 - half):
            rows_copy(half, block, peers[half * 16 + block], me).start()

    def image_copy(i, peer):
        spot = SEEN_FROM[i]
        return to_sub(
            images.at[:, peer], out.at[facet, spot // 16, :, spot % 16], send_s.at[2, i], image_r.at[spot], peer
        )

    def image_arrives(spot):
        to_sub(
            images.at[:, 0], out.at[facet, lax.div(spot, 16), :, lax.rem(spot, 16)],
            send_s.at[2, 0], image_r.at[spot], peers[0],
        ).wait_recv()

    def cut(which):
        cut_rows(which, facet, offs, turn, places, wide_re, wide_im, mine)

    pairs = {}
    for half in range(2):
        for hop in (2, 1, 3, 0):
            target = 2 * lax.rem(chip + hop, 4) + 1 - core
            if half == 0:
                cut(target)
            pairs[half, hop] = to_facet(
                mine.at[target, half], pair_buf.at[hop, half],
                pair_s.at[half, hop], pair_r.at[half, hop], sib,
            )
            pairs[half, hop].start()

    def merge_pair(half, hop):
        pairs[half, hop].wait_recv()
        target = 2 * lax.rem(chip + hop, 4) + core
        for plane in range(2):
            add_blocks(
                sums.at[hop, half, plane], [mine.at[target, half, plane], pair_buf.at[hop, half, plane]], 0, 16
            )

    rings = [
        [
            to_facet(src, dst, ring_s.at[half, i], ring_r.at[half, i], peer)
            for i, (src, dst, peer) in enumerate((
                (sums.at[2, half, 0], carry_a.at[half], up),
                (sums.at[2, half, 1], carry_b.at[half], dn),
                (sums.at[1, half, 1], from_dn.at[half, 1], up),
                (sums.at[3, half, 0], from_up.at[half, 0], dn),
                (sums.at[1, half, 0], from_dn.at[half, 0], up),
                (sums.at[3, half, 1], from_up.at[half, 1], dn),
            ))
        ]
        for half in range(2)
    ]

    def merge_ring(half):
        ring = rings[half]
        ring[0].wait_recv()
        add_blocks(sums.at[1, half, 0], [sums.at[1, half, 0], carry_a.at[half]], 0, 16)
        ring[4].start()
        ring[1].wait_recv()
        add_blocks(sums.at[3, half, 1], [sums.at[3, half, 1], carry_b.at[half]], 0, 16)
        ring[5].start()

    def finish(half):
        pairs[half, 0].wait_recv()
        own_target = 2 * chip + core
        for plane, steps in ((0, (3, 4)), (1, (2, 5))):
            for step in steps:
                rings[half][step].wait_recv()
            add_blocks(
                total.at[half, plane],
                [
                    ref.at[half, plane]
                    for ref in (mine.at[own_target], pair_buf.at[0], from_dn, from_up)
                ],
                0, 16,
            )

    cut(2 * lax.rem(chip + 2, 4) + core)
    merge_pair(0, 2)
    rings[0][0].start()
    rings[0][1].start()
    cut(2 * lax.rem(chip + 1, 4) + core)
    merge_pair(0, 1)
    rings[0][2].start()
    cut(2 * lax.rem(chip + 3, 4) + core)
    merge_pair(0, 3)
    rings[0][3].start()
    send_vis()
    merge_pair(1, 2)
    rings[1][0].start()
    rings[1][1].start()
    cut(2 * chip + core)
    merge_pair(1, 1)
    merge_pair(1, 3)
    column_phase(facet, offsets, phase)
    merge_ring(0)
    rings[1][2].start()
    rings[1][3].start()
    routing(owners, choice)
    same_pixel(keep)
    merge_ring(1)
    finish(0)
    send_rows(0)
    finish(1)
    send_rows(1)
    for plane in range(2):
        gathered[plane, me] = total[1, plane, 15]
    others(lambda peer: vis_copy(peer, peer, 0).wait_recv())
    vis[...] = mm(choice[...], received[...].reshape(SUBS * SUBS, LANES))
    others(lambda peer: rows_copy(0, 0, peer, peer).wait_recv())
    columns_to_tiles(gathered, phase, dense, twist, rep, sel, keep, work, folded, tiles)
    visit(tiles, vis, my_tiles)
    tiles_to_columns(my_tiles, phase, dense, twist, rep_t, sel, keep, work, folded_f32, images)

    for i in reversed(range(SUBS - 1)):
        image_copy(i, peers[i]).start()
    for plane in range(2):
        out[facet, 1, plane, 15] = images[plane, me]
    for copy in rings[0] + rings[1] + list(pairs.values()):
        copy.wait_send()

    def drain(kind, src):
        def one(step, carry):
            to_sub(src, src, send_s.at[kind, step], vis_r.at[0], sib).wait_send()
            return carry

        lax.fori_loop(0, SUBS - 1, one, 0)

    drain(0, packed.at[0])
    drain(1, total.at[0, :, 0])
    stores = []
    sends = []

    def store(where):
        copy = pltpu.make_async_copy(out.at[where], out_hbm.at[where], out_sem.at[len(stores)])
        copy.start()
        stores.append(copy)

    def share(half, index, where, peer):
        ref = out.at[where]
        return to_facet(ref, ref, gath_s.at[half, index], gath_r.at[half, index], peer)

    def send(half, index, where, peer):
        sends.append(share(half, index, where, peer))
        sends[-1].start()

    def arrives(half, index, where):
        share(half, index, where, sib).wait_recv()

    def one_image(spot, carry):
        image_arrives(spot)
        return carry

    def own_half(half):
        lax.fori_loop(16 * half, 16 + 15 * half, one_image, 0)
        own = (facet, half)
        send(half, 0, own, up)
        send(half, 1, own, dn)
        send(half, 2, own, sib)
        store(own)

    def onward(half):
        arrives(half, 0, (dn, half))
        send(half, 3, (dn, half, 0), up)
        send(half, 5, (dn, half), sib)
        store((dn, half))
        arrives(half, 1, (up, half))
        send(half, 4, (up, half, 1), dn)
        send(half, 6, (up, half), sib)
        store((up, half))

    def opposite(half):
        arrives(half, 3, (opp, half, 0))
        send(half, 7, (opp, half, 0), sib)
        store((opp, half, 0))
        arrives(half, 4, (opp, half, 1))
        send(half, 8, (opp, half, 1), sib)
        store((opp, half, 1))

    other = 1 - 2 * core
    own_half(1)
    own_half(0)
    drain(2, images.at[:, 0])
    onward(1)
    onward(0)
    opposite(1)
    for half in (1, 0):
        arrives(half, 2, (sib, half))
        store((sib, half))
        arrives(half, 5, (dn + other, half))
        store((dn + other, half))
        arrives(half, 6, (up + other, half))
        store((up + other, half))
    opposite(0)
    for half in (1, 0):
        arrives(half, 7, (opp + other, half, 0))
        store((opp + other, half, 0))
        arrives(half, 8, (opp + other, half, 1))
        store((opp + other, half, 1))
    for copy in sends:
        copy.wait_send()
    for copy in stores:
        copy.wait()


def vmem_specs(count):
    return [pl.BlockSpec(memory_space=pltpu.VMEM)] * count


def smem_specs(count):
    return [pl.BlockSpec(memory_space=pltpu.SMEM)] * count


BIG = 60 * 1024 * 1024
STRIPS = (FACETS, 2, 2, 16, 16, LANES)
WIDE_ROWS = 66 * 128


def any_specs(count):
    return [pl.BlockSpec(memory_space=pl.ANY)] * count


def row_scratch():
    narrow, wide = pltpu.VMEM((RADIX * PITCH, LANES), F32), pltpu.VMEM((WIDE_ROWS, LANES), F32)
    return [narrow] * 4 + [wide] * 2


TABLE = (RADIX, 2 * RADIX, 2 * RADIX)


def backward_call(shape):
    return pl.pallas_call(
        backward_kernel,
        out_shape=jax.ShapeDtypeStruct(shape, BF16),
        in_specs=any_specs(7),
        out_specs=pl.BlockSpec(memory_space=pl.ANY),
        scratch_shapes=[(pltpu.SMEM if i < 2 else pltpu.VMEM)(*item) for i, item in enumerate(SMALL[:5])]
        + [pltpu.SemaphoreType.DMA((5,))]
        + row_scratch()
        + [
            pltpu.VMEM(STRIPS, BF16),
            pltpu.VMEM(TABLE, BF16),
            pltpu.VMEM(shape, BF16),
            pltpu.SemaphoreType.DMA,
            pltpu.SemaphoreType.DMA((FACETS,)),
            pltpu.SemaphoreType.DMA((4,)),
        ],
        compiler_params=pltpu.CompilerParams(vmem_limit_bytes=BIG),
    )


def strips_call(shape):
    block = (2, SUBS, 16, LANES)
    halves = (2, 2, 16, 16, LANES)
    half = (2, 16, 16, LANES)
    values = (SUBS, VALUES * CAP, LANES)
    vm = pltpu.VMEM
    dma = pltpu.SemaphoreType.DMA
    return pl.pallas_call(
        facet_to_strips_kernel,
        out_shape=jax.ShapeDtypeStruct(STRIPS, BF16),
        in_specs=any_specs(2 + len(SMALL)),
        out_specs=pl.BlockSpec(memory_space=pl.ANY),
        scratch_shapes=[(pltpu.SMEM if i < 2 else vm)(*item) for i, item in enumerate(SMALL)]
        + [vm(shape, BF16)]
        + row_scratch()
        + [
            vm(TABLE, BF16), vm((512, 512), BF16), vm(STRIPS, BF16),
            vm((4,) + halves, BF16), vm((4,) + halves, BF16), vm(half, BF16), vm(half, BF16),
            vm(halves, BF16), vm(halves, BF16), vm(halves, BF16), vm(block, BF16),
            vm((SUBS, 2, 16, LANES), F32), vm((512, 256), BF16), vm((512, 256), F32),
            vm((512, LANES), BF16), vm((512, LANES), BF16), vm(block, BF16), vm(STRIPS, BF16),
            vm((LANES, LANES), F32), vm((2, SUBS, LANES), F32),
            vm(values, F32), vm(values, BF16), vm(values, BF16),
            vm((VALUES * SUBS, SUBS * SUBS), BF16), vm((VALUES * SUBS, LANES), F32),
            dma((5 + len(SMALL),)), dma((20,)),
            dma((2, 4)), dma((2, 4)), dma((2, 6)), dma((2, 6)), dma((3, SUBS)),
            dma((SUBS,)), dma((SUBS,)), dma((SUBS,)), dma((2, 9)), dma((2, 9)),
        ],
        compiler_params=pltpu.CompilerParams(
            vmem_limit_bytes=BIG, collective_id=0, has_side_effects=True
        ),
    )


def per_device(
    facet_strips, row_window, col_window, row_offsets, col_offsets,
    tile_owner, measured, vis_weight, uvw_pixels, vis_count,
):
    first, second = row_tables()
    dense, twist, rep, rep_t, sel = col_tables()
    eighth = 2 * np.pi * np.arange(FACETS) / FACETS
    turn = jnp.asarray(np.stack([np.cos(eighth), np.sin(eighth)]), F32)
    row_win = row_window.reshape(LONG // LANES, LANES)
    col_win = col_window.reshape(1, LANES)
    strips = strips_call(facet_strips.shape)(
        facet_strips, second, row_offsets, turn, row_win, col_win, first,
        col_offsets.reshape(1, FACETS), tile_owner.reshape(1, SUBS), measured[0, 0],
        vis_weight[0, 0], jnp.transpose(uvw_pixels[0, 0], (1, 0, 2)), vis_count.reshape(1, LANES),
        dense, twist, rep, rep_t, sel,
    )
    return backward_call(facet_strips.shape)(
        row_offsets, turn, row_win, col_win, first, strips, second
    )


def solution(mesh):
    in_specs = (
        P(None, "facet", "sub"),
        P(),
        P("sub"),
        P(),
        P(),
        P("sub", "facet", None, None),
        P("facet", "sub", None, None, None),
        P("facet", "sub", None, None),
        P("facet", "sub", None, None, None),
        P("facet", "sub", None),
    )
    return jax.shard_map(
        per_device, mesh=mesh, in_specs=in_specs, out_specs=P(None, "facet", "sub"), check_vma=False
    )
```
